256 devices in a mesh: gx: 8 (over z), gy: 16 (over y, x), gz: 2 (over core).
Axes of the slice: x: 4, y: 4, z: 8, core: 2. Of those that a mesh axis runs over, the one named last changes fastest.
Arguments:
- tensor: float32 [1024, 1024, 256], P('gx', 'gy', 'gz'), may hold values from -60 to 60
- factor_a: float32 [1024, 64], P(('gx', 'gy', 'gz')), may hold values from -6 to 6
- factor_b: float32 [1024, 64], P(('gy', 'gx', 'gz')), may hold values from -6 to 6
- factor_c: float32 [256, 64], P(('gz', 'gx', 'gy')), may hold values from -6 to 6
Outputs:
- slope_a: float32 [1024, 64], P(('gx', 'gy', 'gz'))
- slope_b: float32 [1024, 64], P(('gy', 'gx', 'gz'))
- slope_c: float32 [256, 64], P(('gz', 'gx', 'gy'))
The draws below stay inside these ranges and needn't reach their ends.
All inputs are finite; a program needn't handle non-finite values.
Results may differ from the reference program's by a relative error of at most 0.0003.
Values sent between devices are 32-bit elements; how exact they have to be, the bound alone decides.
No kernel may reach another device: no remote copies, remote signals or barrier semaphores. Data moves between devices by JAX's collectives and lax.ppermute only.
A program may use at most 64 MiB of HBM per device.

```python
import math
import jax
import jax.numpy as jnp
from jax import lax

R = 64
STEPS = 2
I = 1024
J = 1024
K = 256


def factor_pair(key, row_count, salt):
    folded = jax.random.fold_in(key, salt)
    key_one, key_two, key_three, key_four = jax.random.split(folded, 4)
    row_scale = jnp.exp(jax.random.uniform(key_one, (row_count, 1), jnp.float32, math.log(0.4), math.log(4.0)))
    entries = jax.random.normal(key_two, (row_count, R), jnp.float32)
    common = 0.6 * jax.random.normal(key_three, (row_count, 1), jnp.float32)
    jitter = jax.random.normal(key_four, (row_count, R), jnp.float32)
    target = jnp.clip(0.5 * row_scale * (entries + common), -6.0, 6.0)
    initial = jnp.clip(target + 0.15 * row_scale * jitter, -6.0, 6.0)
    return (target, initial)


def draw_tensor(key, part):
    model_a = factor_pair(key, I, 1)[0]
    model_b = factor_pair(key, J, 2)[0]
    model_c = factor_pair(key, K, 3)[0]
    paired = (model_a[:, None, :] * model_b[None, :, :]).reshape(I * J, R)
    model = jnp.dot(paired, model_c.T, precision=lax.Precision.HIGHEST).reshape(I, J, K)
    extra_key = jax.random.fold_in(key, 4)
    extra = jax.random.normal(extra_key, (I, J, K), jnp.float32)
    return jnp.clip(model + 0.05 * extra, -60.0, 60.0)


def draw_factor_a(key, part):
    return factor_pair(key, I, 1)[1]


def draw_factor_b(key, part):
    return factor_pair(key, J, 2)[1]


def draw_factor_c(key, part):
    return factor_pair(key, K, 3)[1]


def setup_inputs(seed: int = 0) -> dict:
    splits = jax.random.split(jax.random.key(seed), 5)
    return {
        "tensor": draw_tensor(jax.random.fold_in(splits[4], 71), 0),
        "factor_a": draw_factor_a(jax.random.fold_in(splits[4], 71), 0),
        "factor_b": draw_factor_b(jax.random.fold_in(splits[4], 71), 0),
        "factor_c": draw_factor_c(jax.random.fold_in(splits[4], 71), 0),
    }


def reference(tensor, factor_a, factor_b, factor_c):
    highest = lax.Precision.HIGHEST
    step_size = 0.1
    first, second, third = factor_a, factor_b, factor_c
    for round_index in range(STEPS):
        gram_a = jnp.dot(first.T, first, precision=highest, preferred_element_type=jnp.float32)
        gram_b = jnp.dot(second.T, second, precision=highest, preferred_element_type=jnp.float32)
        gram_c = jnp.dot(third.T, third, precision=highest, preferred_element_type=jnp.float32)
        along_k = jnp.einsum("ijk,kr->ijr", tensor, third, precision=highest)
        moment_a = jnp.einsum("ijr,jr->ir", along_k, second, precision=highest)
        moment_b = jnp.einsum("ijr,ir->jr", along_k, first, precision=highest)
        along_i = jnp.einsum("ijk,ir->jkr", tensor, first, precision=highest)
        moment_c = jnp.einsum("jkr,jr->kr", along_i, second, precision=highest)
        slope_a = (jnp.dot(first, gram_b * gram_c, precision=highest) - moment_a) / (J * K)
        slope_b = (jnp.dot(second, gram_a * gram_c, precision=highest) - moment_b) / (I * K)
        slope_c = (jnp.dot(third, gram_a * gram_b, precision=highest) - moment_c) / (I * J)
        if round_index + 1 < STEPS:
            first = first - step_size * slope_a
            second = second - step_size * slope_b
            third = third - step_size * slope_c
    return slope_a, slope_b, slope_c
```

```python
import functools

import jax
import jax.numpy as jnp
from jax import lax
from jax.experimental import pallas as pl
from jax.experimental.pallas import tpu as pltpu
from jax.sharding import PartitionSpec as P

STEPS = 2
STEP_SIZE = 0.1
F32 = jnp.float32
BF16 = jnp.bfloat16
HIGHEST = lax.Precision.HIGHEST
VMEM = pl.BlockSpec(memory_space=pltpu.VMEM)
CHUNK = 512


def split(x):
    high = x.astype(BF16)
    return high, (x - high.astype(F32)).astype(BF16)


def prep_kernel(count_i, count_j, count_k, t_ref, rows_ref, turned_ref):
    def natural(c, _):
        at = pl.multiple_of(c * CHUNK, CHUNK)
        high, low = split(t_ref[pl.ds(at, CHUNK), :])
        rows_ref[pl.ds(at, CHUNK), :count_k] = high
        rows_ref[pl.ds(at, CHUNK), count_k:] = low
        return 0

    lax.fori_loop(0, count_i * count_j // CHUNK, natural, 0)

    def turned(j, _):
        high, low = split(t_ref[pl.ds(j, count_i, stride=count_j), :].T)
        at = pl.multiple_of(j * count_k, count_k)
        turned_ref[pl.ds(at, count_k), :count_i] = high
        turned_ref[pl.ds(at, count_k), count_i:] = low
        return 0

    lax.fori_loop(0, count_j, turned, 0, unroll=2)


def prep(tensor):
    count_i, count_j, count_k = tensor.shape
    return pl.pallas_call(
        functools.partial(prep_kernel, count_i, count_j, count_k),
        out_shape=(
            jax.ShapeDtypeStruct((count_i * count_j, 2 * count_k), BF16),
            jax.ShapeDtypeStruct((count_j * count_k, 2 * count_i), BF16),
        ),
        in_specs=[VMEM],
        out_specs=(VMEM, VMEM),
        compiler_params=pltpu.CompilerParams(vmem_limit_bytes=24 << 20),
        cost_estimate=pl.CostEstimate(flops=1 << 24, bytes_accessed=12 << 20, transcendentals=0),
        name="prep",
    )(tensor.reshape(count_i * count_j, count_k))


def wide(x, upper):
    lower = lax.broadcasted_iota(jnp.int32, x.shape, 1) < x.shape[1] // 2
    turned = pltpu.roll(x, x.shape[1] // 2, 1)
    return jnp.where(lower, turned, x) if upper else jnp.where(lower, x, turned)


def weights(x):
    high = x.astype(BF16).astype(F32)
    lower = lax.broadcasted_iota(jnp.int32, x.shape, 1) < x.shape[1] // 2
    both = jnp.where(lower, high, x - high).astype(BF16)
    return jnp.concatenate([both, both], axis=0)


def gram(x):
    return lax.dot_general(
        x, x, (((0,), (0,)), ((), ())), precision=HIGHEST, preferred_element_type=F32
    )


def round_kernel(keep, scale, mixed, ac_ref, b_ref, rows_ref, turned_ref, oa_ref, ob_ref, oc_ref, a2_ref, b2_ref, ma_ref, c_ref):
    count_i, count_j, count_k = a2_ref.shape[0], b2_ref.shape[0], c_ref.shape[0]
    if mixed:
        groups, each = ac_ref.shape[0], ac_ref.shape[1]
        ac = ac_ref[...].reshape(count_i, ac_ref.shape[2])
        for g in range(each):
            c_ref[g * groups : (g + 1) * groups, :] = ac_ref[:, g, :]
        c2 = wide(c_ref[...], True)
    else:
        ac = ac_ref[...]
        c2 = wide(ac, True)
    a2 = wide(ac, False)
    b2 = wide(b_ref[...], False)
    a2_ref[...] = a2
    b2_ref[...] = b2
    weights_a, weights_c = weights(a2), weights(c2)
    per_i, per_j = CHUNK // count_j, CHUNK // count_k

    def step(c, carry):
        moment_b, moment_c = carry
        at = pl.multiple_of(c * CHUNK, CHUNK)
        y = jnp.dot(rows_ref[pl.ds(at, CHUNK), :], weights_c, preferred_element_type=F32)
        y = y.reshape(per_i, count_j, y.shape[1])
        at_i = pl.multiple_of(c * per_i, per_i)
        ma_ref[pl.ds(at_i, per_i), :] = jnp.sum(y * b2_ref[...][None], axis=1)
        for n in range(per_i):
            moment_b = moment_b + y[n] * a2_ref[pl.ds(c * per_i + n, 1), :]
        z = jnp.dot(turned_ref[pl.ds(at, CHUNK), :], weights_a, preferred_element_type=F32)
        z = z.reshape(per_j, count_k, z.shape[1])
        for n in range(per_j):
            moment_c = moment_c + z[n] * b2_ref[pl.ds(c * per_j + n, 1), :]
        return moment_b, moment_c

    moment_b, moment_c = lax.fori_loop(
        0,
        count_i * count_j // CHUNK,
        step,
        (jnp.zeros(b2.shape, F32), jnp.zeros(c2.shape, F32)),
    )
    gram_a, gram_b, gram_c = gram(a2), gram(b2), gram(c2)

    def result(factor, gram_one, gram_two, moment, weight, factor_scale):
        model = jnp.dot(factor, gram_one * gram_two, precision=HIGHEST, preferred_element_type=F32)
        partial = 0.5 * model - (moment + pltpu.roll(moment, moment.shape[1] // 2, 1))
        out = partial * factor_scale
        return out + factor * weight if weight else out

    oa_ref[...] = result(a2, gram_b, gram_c, ma_ref[...], keep[0], scale[0])
    ob_ref[...] = result(b2, gram_a, gram_c, moment_b, keep[1], scale[1])
    oc_ref[...] = result(c2, gram_a, gram_b, moment_c, keep[2], scale[2])


def partials(keep, scale, ac, b, rows, turned, sizes):
    count_i, count_j, count_k = sizes
    width = b.shape[1]
    return pl.pallas_call(
        functools.partial(round_kernel, keep, scale, ac.ndim == 3),
        out_shape=tuple(jax.ShapeDtypeStruct((n, width), F32) for n in sizes),
        in_specs=[VMEM] * 4,
        out_specs=(VMEM,) * 3,
        scratch_shapes=[
            pltpu.VMEM((count_i, width), F32),
            pltpu.VMEM((count_j, width), F32),
            pltpu.VMEM((count_i, width), F32),
            pltpu.VMEM((count_k, width), F32),
        ],
        compiler_params=pltpu.CompilerParams(vmem_limit_bytes=24 << 20),
        cost_estimate=pl.CostEstimate(flops=1 << 30, bytes_accessed=8 << 20, transcendentals=0),
        name="partials",
    )(ac, b, rows, turned)


def send_all(x, axis):
    count = lax.axis_size(axis)
    return lax.all_to_all(jnp.broadcast_to(x[None], (count, *x.shape)), axis, 0, 0, tiled=True)


def shift(x, axis, stride, count, by):
    total = lax.axis_size(axis)
    pairs = []
    for n in range(total):
        place = n // stride % count
        pairs.append((n, n + ((place + by) % count - place) * stride))
    return lax.ppermute(x, axis, pairs)


def ring8(x):
    below, above = shift(x, "gx", 1, 8, 1), shift(x, "gx", 1, 8, -1)
    two = x + above
    three = two + below
    return three + (shift(three, "gx", 1, 8, -3) + shift(two, "gx", 1, 8, 3))


def ring4(x, stride):
    ones = shift(x, "gy", stride, 4, 1) + shift(x, "gy", stride, 4, -1)
    return (x + ones) + shift(x, "gy", stride, 4, 2)


def swap(x):
    return lax.ppermute(x, "gz", [(0, 1), (1, 0)])


def shards(tensor, factor_a, factor_b, factor_c):
    count_x, count_y, count_z = (lax.axis_size(n) for n in ("gx", "gy", "gz"))
    sizes = count_i, count_j, count_k = tensor.shape
    whole = (
        float(count_j * count_y * count_k * count_z),
        float(count_i * count_x * count_k * count_z),
        float(count_i * count_x * count_j * count_y),
    )
    copies = (count_y * count_z, count_x * count_z, count_x * count_y)
    rank = factor_a.shape[1]
    rows, turned = prep(tensor)

    own = lax.all_gather(jnp.concatenate([factor_a, factor_b], axis=1), "gz", axis=0, tiled=True)
    each = own.shape[0]
    padded_c = jnp.pad(factor_c, ((0, each - 1), (0, 0)))
    along_x = send_all(jnp.concatenate([own[:, rank:], padded_c], axis=1), "gx")
    block_b = along_x.reshape(count_j, 2 * rank)
    block_ac = send_all(jnp.concatenate([own[:, :rank], along_x[:, 0, rank:]], axis=1), "gy")

    keep = tuple(1.0 / n for n in copies)
    scale = tuple(-STEP_SIZE / n for n in whole)
    part_a, part_b, part_c = partials(keep, scale, block_ac, block_b, rows, turned, sizes)
    lower = lax.broadcasted_iota(jnp.int32, (count_k, 2 * rank), 1) < rank
    tall_b = jnp.pad(part_b, ((0, count_k - count_j), (0, 0)))
    bc = ring8(jnp.where(lower, tall_b, part_c))
    ac = ring4(ring4(jnp.where(lower, part_a, bc), 1), 4)
    ab = jnp.concatenate([ac[:, :rank], bc[:, :rank]], axis=1)
    ab = ab + swap(ab)
    ac = jnp.concatenate([ab[:, :rank], ac[:, rank:]], axis=1)
    block_b = ab[:count_j, rank:]
    block_b = jnp.concatenate([block_b, block_b], axis=1)

    scale = tuple(1.0 / n for n in whole)
    part_a, part_b, part_c = partials((0.0,) * 3, scale, ac, block_b, rows, turned, sizes)
    slots_b = jnp.pad(
        part_b.reshape(count_x, each, 2 * rank), ((0, 0), (0, count_y - each), (0, 0))
    )
    slots_c = part_c.reshape(count_x, count_y, 2 * rank)
    lower = lax.broadcasted_iota(jnp.int32, slots_c.shape, 2) < rank
    bc = jnp.sum(
        lax.all_to_all(jnp.where(lower, slots_b, slots_c), "gx", 0, 0, tiled=True), axis=0
    )
    slots_c = jnp.pad(bc[:, None, rank:], ((0, 0), (0, each - 1), (0, 0)))
    slots_a = part_a.reshape(count_y, each, 2 * rank)[:, :, :rank]
    ac = jnp.sum(
        lax.all_to_all(jnp.concatenate([slots_a, slots_c], axis=2), "gy", 0, 0, tiled=True), axis=0
    )
    ab = jnp.concatenate([ac[:, :rank], bc[:each, :rank]], axis=1)
    ab = ab + swap(ab)
    mine = lax.dynamic_slice_in_dim(ab, lax.axis_index("gz") * (each // 2), each // 2, axis=0)
    return mine[:, :rank], mine[:, rank:], ac[:1, rank:]


def solution(mesh):
    factors = (
        P(("gx", "gy", "gz"), None),
        P(("gy", "gx", "gz"), None),
        P(("gz", "gx", "gy"), None),
    )
    return jax.shard_map(
        shards,
        mesh=mesh,
        in_specs=(P("gx", "gy", "gz"), *factors),
        out_specs=factors,
        check_vma=False,
    )
```

```python
import functools

import jax
import jax.numpy as jnp
from jax import lax
from jax.experimental import pallas as pl
from jax.experimental.pallas import tpu as pltpu
from jax.sharding import PartitionSpec as P

STEPS = 2
STEP_SIZE = 0.1
F32 = jnp.float32
BF16 = jnp.bfloat16
HIGHEST = lax.Precision.HIGHEST
VMEM_BYTES = 60 << 20
GRID = 8
CHUNK = 512


def split(x):
    high = x.astype(BF16)
    return high, (x - high.astype(F32)).astype(BF16)


def rows_kernel(t_ref, out_ref):
    width = t_ref.shape[1]

    def step(c, _):
        at = pl.multiple_of(c * 128, 128)
        high, low = split(t_ref[pl.ds(at, 128), :])
        out_ref[pl.ds(at, 128), :width] = high
        out_ref[pl.ds(at, 128), width:] = low
        return 0

    lax.fori_loop(0, t_ref.shape[0] // 128, step, 0, unroll=2)


def split_rows(tensor):
    count_i, count_j, count_k = tensor.shape
    block = count_i * count_j // GRID
    return pl.pallas_call(
        rows_kernel,
        grid=(GRID,),
        out_shape=jax.ShapeDtypeStruct((count_i * count_j, 2 * count_k), BF16),
        in_specs=[pl.BlockSpec((block, count_k), lambda n: (n, 0))],
        out_specs=pl.BlockSpec((block, 2 * count_k), lambda n: (n, 0)),
        compiler_params=pltpu.CompilerParams(vmem_limit_bytes=VMEM_BYTES),
        cost_estimate=pl.CostEstimate(flops=1 << 24, bytes_accessed=8 << 20, transcendentals=0),
        name="split_rows",
    )(tensor.reshape(count_i * count_j, count_k))


def turned_kernel(t_ref, out_ref):
    count_i, per, count_k = t_ref.shape
    for j in range(per):
        high, low = split(t_ref[:, j, :].T)
        out_ref[j * count_k : (j + 1) * count_k, :count_i] = high
        out_ref[j * count_k : (j + 1) * count_k, count_i:] = low


def split_turned(tensor):
    count_i, count_j, count_k = tensor.shape
    per = count_j // GRID
    return pl.pallas_call(
        turned_kernel,
        grid=(GRID,),
        out_shape=jax.ShapeDtypeStruct((count_j * count_k, 2 * count_i), BF16),
        in_specs=[pl.BlockSpec((count_i, per, count_k), lambda n: (0, n, 0))],
        out_specs=pl.BlockSpec((per * count_k, 2 * count_i), lambda n: (n, 0)),
        compiler_params=pltpu.CompilerParams(vmem_limit_bytes=VMEM_BYTES),
        cost_estimate=pl.CostEstimate(flops=1 << 24, bytes_accessed=8 << 20, transcendentals=0),
        name="split_turned",
    )(tensor)


def lower_half(shape):
    return lax.broadcasted_iota(jnp.int32, shape, len(shape) - 1) < shape[-1] // 2


def turn(x):
    return pltpu.roll(x, x.shape[1] // 2, 1)


def weights(x):
    high = x.astype(BF16).astype(F32)
    both = jnp.where(lower_half(x.shape), high, x - high).astype(BF16)
    return jnp.concatenate([both, both], axis=0)


def gram(x):
    return lax.dot_general(
        x, x, (((0,), (0,)), ((), ())), precision=HIGHEST, preferred_element_type=F32
    )


def unpack_first(ac_ref, b_ref, a2_ref, b2_ref, c2_ref):
    slots, each = ac_ref.shape[0], ac_ref.shape[1]
    own = a2_ref.shape[0] // slots
    core = lax.axis_index("gz")
    flat = ac_ref.reshape(slots * each, ac_ref.shape[2])
    for n in range(slots):
        a2_ref[n * own : (n + 1) * own, :] = ac_ref[n, :own, :]
    count = c2_ref.shape[0] // each
    for g in range(each):
        c2_ref[g * count : (g + 1) * count, :] = flat[pl.ds(core * each + g, count, stride=2 * each), :]
    a, b, c = a2_ref[...], b_ref[...], c2_ref[...]
    a2_ref[...] = jnp.where(lower_half(a.shape), a, turn(a))
    b2_ref[...] = jnp.where(lower_half(b.shape), b, turn(b))
    c2_ref[...] = jnp.where(lower_half(c.shape), turn(c), c)


def unpack_second(all_ref, a2_ref, b2_ref, c2_ref):
    half, count_c = a2_ref.shape[0] // 2, c2_ref.shape[0]
    a = all_ref[:half, :]
    c = all_ref[half : half + count_c, :]
    b2_ref[...] = all_ref[half + count_c :, :]
    lower = lower_half(a.shape)
    a2_ref[:half, :] = jnp.where(lower, a, turn(a))
    a2_ref[half:, :] = jnp.where(lower, turn(a), a)
    core = lax.axis_index("gz")
    keep = lower_half(c.shape).astype(jnp.int32) != core
    c2_ref[...] = jnp.where(keep, c, turn(c))


def pack_first(a, b, c, out_ref):
    half, count_c = a.shape[0] // 2, c.shape[0]
    out_ref[:half, :] = jnp.where(lower_half((half, a.shape[1])), a[:half], a[half:])
    out_ref[half : half + count_c, :] = c
    out_ref[half + count_c :, :] = b


def pack_second(a, b, c, bc_ref, ac_ref):
    core = lax.axis_index("gz")
    slots, tall, width = bc_ref.shape
    own = b.shape[0] // slots
    lower = lower_half((own, width))
    for n in range(slots):
        g, z = n // 2, n % 2
        block = jnp.where(core == z, c[g * tall : (g + 1) * tall], 0.0)
        bc_ref[n, :, :] = block
        bc_ref[n, :own, :] = jnp.where(lower, b[n * own : (n + 1) * own], block[:own])
    slots, each, width = ac_ref.shape
    own = a.shape[0] // slots
    for n in range(slots):
        ac_ref[n, :, :] = jnp.zeros((each, width), F32)
        ac_ref[n, :own, :] = a[n * own : (n + 1) * own]


def round_kernel(first, keep, scale, *refs):
    n_in, n_out = (2, 1) if first else (1, 2)
    small, (rows_ref, turned_ref) = refs[:n_in], refs[n_in : n_in + 2]
    outs = refs[n_in + 2 : n_in + 2 + n_out]
    a2_ref, b2_ref, c2_ref, wa_ref, wc_ref, ma_ref, mb_ref, mc_ref = refs[n_in + 2 + n_out :]
    count_i, count_j, count_k = a2_ref.shape[0], b2_ref.shape[0], c2_ref.shape[0]
    at_step = pl.program_id(0)

    @pl.when(at_step == 0)
    def _():
        (unpack_first if first else unpack_second)(*small, a2_ref, b2_ref, c2_ref)
        wa_ref[...] = weights(a2_ref[...])
        wc_ref[...] = weights(c2_ref[...])
        mb_ref[...] = jnp.zeros(mb_ref.shape, F32)
        mc_ref[...] = jnp.zeros(mc_ref.shape, F32)

    per_i, per_j = CHUNK // count_j, CHUNK // count_k
    chunks = rows_ref.shape[0] // CHUNK
    moment_b, moment_c = mb_ref[...], mc_ref[...]
    for n in range(chunks):
        c = at_step * chunks + n
        y = jnp.dot(rows_ref[n * CHUNK : (n + 1) * CHUNK, :], wc_ref[...], preferred_element_type=F32)
        y = y.reshape(per_i, count_j, y.shape[1])
        at_i = pl.multiple_of(c * per_i, per_i)
        ma_ref[pl.ds(at_i, per_i), :] = jnp.sum(y * b2_ref[...][None], axis=1)
        for m in range(per_i):
            moment_b = moment_b + y[m] * a2_ref[pl.ds(at_i + m, 1), :]
        z = jnp.dot(turned_ref[n * CHUNK : (n + 1) * CHUNK, :], wa_ref[...], preferred_element_type=F32)
        z = z.reshape(per_j, count_k, z.shape[1])
        for m in range(per_j):
            moment_c = moment_c + z[m] * b2_ref[pl.ds(c * per_j + m, 1), :]
    mb_ref[...] = moment_b
    mc_ref[...] = moment_c

    @pl.when(at_step == pl.num_programs(0) - 1)
    def _():
        a2, b2, c2 = a2_ref[...], b2_ref[...], c2_ref[...]
        gram_a, gram_b, gram_c = gram(a2), gram(b2), gram(c2)

        def result(factor, gram_one, gram_two, moment, weight, factor_scale):
            model = jnp.dot(
                factor, gram_one * gram_two, precision=HIGHEST, preferred_element_type=F32
            )
            out = (0.5 * model - (moment + turn(moment))) * factor_scale
            return out + factor * weight if weight else out

        a = result(a2, gram_b, gram_c, ma_ref[...], keep[0], scale[0])
        b = result(b2, gram_a, gram_c, mb_ref[...], keep[1], scale[1])
        c = result(c2, gram_a, gram_b, mc_ref[...], keep[2], scale[2])
        (pack_first if first else pack_second)(a, b, c, *outs)


def partials(first, keep, scale, small, rows, turned, sizes, out_shapes):
    count_i, count_j, count_k = sizes
    width = small[0].shape[-1]
    tall = rows.shape[0] // GRID

    def whole(shape):
        return pl.BlockSpec(shape, lambda n: (0,) * len(shape))

    return pl.pallas_call(
        functools.partial(round_kernel, first, keep, scale),
        grid=(GRID,),
        out_shape=tuple(jax.ShapeDtypeStruct(s, F32) for s in out_shapes),
        in_specs=[whole(x.shape) for x in small]
        + [pl.BlockSpec((tall, x.shape[1]), lambda n: (n, 0)) for x in (rows, turned)],
        out_specs=tuple(whole(s) for s in out_shapes),
        scratch_shapes=[
            pltpu.VMEM((count_i, width), F32),
            pltpu.VMEM((count_j, width), F32),
            pltpu.VMEM((count_k, width), F32),
            pltpu.VMEM((2 * count_i, width), BF16),
            pltpu.VMEM((2 * count_k, width), BF16),
            pltpu.VMEM((count_i, width), F32),
            pltpu.VMEM((count_j, width), F32),
            pltpu.VMEM((count_k, width), F32),
        ],
        compiler_params=pltpu.CompilerParams(vmem_limit_bytes=VMEM_BYTES),
        cost_estimate=pl.CostEstimate(flops=1 << 30, bytes_accessed=8 << 20, transcendentals=0),
        name="partials",
    )(*small, rows, turned)


def send_all(x, axes):
    count = 1
    for name in axes:
        count *= lax.axis_size(name)
    return lax.all_to_all(jnp.broadcast_to(x[None], (count, *x.shape)), axes, 0, 0, tiled=True)


def shift(x, axis, stride, count, by):
    pairs = []
    for n in range(lax.axis_size(axis)):
        place = n // stride % count
        to = n + ((place + by) % count - place) * stride
        pairs.append((2 * n + 1, 2 * to + 1))
    return lax.ppermute(x, (axis, "gz"), pairs)


def ring8(x):
    below, above = shift(x, "gx", 1, 8, 1), shift(x, "gx", 1, 8, -1)
    two = x + above
    three = two + below
    return three + (shift(three, "gx", 1, 8, -3) + shift(two, "gx", 1, 8, 3))


def ring4(x, stride):
    ones = shift(x, "gy", stride, 4, 1) + shift(x, "gy", stride, 4, -1)
    return (x + ones) + shift(x, "gy", stride, 4, 2)


def shards(tensor, factor_a, factor_b, factor_c):
    count_x, count_y, count_z = (lax.axis_size(n) for n in ("gx", "gy", "gz"))
    core = lax.axis_index("gz")
    sizes = count_i, count_j, count_k = tensor.shape
    whole = (
        float(count_j * count_y * count_k * count_z),
        float(count_i * count_x * count_k * count_z),
        float(count_i * count_x * count_j * count_y),
    )
    copies = (count_y * count_z, count_x * count_z, count_x * count_y)
    own, rank = factor_a.shape
    wide = 2 * rank

    rows = split_rows(tensor)
    padded_c = jnp.pad(factor_c, ((0, own - 1), (0, 0)))
    along_x = send_all(jnp.concatenate([factor_b, padded_c], axis=1), ("gx", "gz"))
    tensor, along_x = lax.optimization_barrier((tensor, along_x))
    turned = split_turned(tensor)
    rows_c = along_x.reshape(count_x, count_z, own, wide)[:, :, 0, rank:]
    rows_c = jnp.where(core == 0, rows_c[:, 0], rows_c[:, 1])
    rows, factor_a = lax.optimization_barrier((rows, factor_a))
    padded_a = jnp.pad(factor_a, ((0, count_x - own), (0, 0)))
    along_y = send_all(jnp.concatenate([padded_a, rows_c], axis=1), ("gy", "gz"))

    keep = tuple(1.0 / n for n in copies)
    scale = tuple(-STEP_SIZE / n for n in whole)
    half = count_i // 2
    packed_shape = (half + count_k + count_j, wide)
    (packed,) = partials(
        True, keep, scale, (along_y, along_x.reshape(count_j, wide)), rows, turned, sizes, (packed_shape,)
    )
    other = lax.ppermute(packed, "gz", [(0, 1)])
    middle = slice(half, half + count_k)
    sums = packed + other
    both_c = jnp.where(lower_half((count_k, wide)), other[middle], packed[middle])
    cb = ring8(jnp.concatenate([both_c, sums[half + count_k :]], axis=0))
    ac = ring4(ring4(jnp.concatenate([sums[:half], cb[:count_k]], axis=0), 1), 4)
    packed = jnp.concatenate([ac, cb[count_k:]], axis=0)
    packed = jnp.where(core == 1, packed, lax.ppermute(packed, "gz", [(1, 0)]))

    scale = tuple(1.0 / n for n in whole)
    slots_bc, slots_a = partials(
        False,
        (0.0,) * 3,
        scale,
        (packed,),
        rows,
        turned,
        sizes,
        ((count_x * count_z, count_y, wide), (count_y * count_z, 2 * own, wide)),
    )
    bc = jnp.sum(lax.all_to_all(slots_bc, ("gx", "gz"), 0, 0, tiled=True), axis=0)
    mine = jnp.arange(count_z)[None, :, None, None] == core
    slots_c = jnp.where(mine, bc[:, None, None, rank:], 0.0).reshape(count_y * count_z, 1, rank)
    slots_c = jnp.pad(slots_c, ((0, 0), (0, 2 * own - 1), (0, 0)))
    slots_ac = jnp.concatenate([slots_a[:, :, :rank], slots_c], axis=2)
    ac = jnp.sum(lax.all_to_all(slots_ac, ("gy", "gz"), 0, 0, tiled=True), axis=0)
    return ac[:own, :rank], bc[:own, :rank], ac[:1, rank:]


def solution(mesh):
    factors = (
        P(("gx", "gy", "gz"), None),
        P(("gy", "gx", "gz"), None),
        P(("gz", "gx", "gy"), None),
    )
    return jax.shard_map(
        shards,
        mesh=mesh,
        in_specs=(P("gx", "gy", "gz"), *factors),
        out_specs=factors,
        check_vma=False,
    )
```

```python
import functools

import jax
import jax.numpy as jnp
from jax import lax
from jax.experimental import pallas as pl
from jax.experimental.pallas import tpu as pltpu
from jax.sharding import PartitionSpec as P

STEPS = 2
STEP_SIZE = 0.1
F32 = jnp.float32
BF16 = jnp.bfloat16
HIGHEST = lax.Precision.HIGHEST
VMEM = pl.BlockSpec(memory_space=pltpu.VMEM)
HBM = pl.BlockSpec(memory_space=pltpu.HBM)
CHUNK = 512
UNROLL = 2


def split(x):
    high = x.astype(BF16)
    return high, (x - high.astype(F32)).astype(BF16)


def lower_half(shape):
    return lax.broadcasted_iota(jnp.int32, shape, len(shape) - 1) < shape[-1] // 2


def turn(x):
    return pltpu.roll(x, x.shape[1] // 2, 1)


def from_lower(x):
    return jnp.where(lower_half(x.shape), x, turn(x))


def from_upper(x):
    return jnp.where(lower_half(x.shape), turn(x), x)


def gram(x):
    return lax.dot_general(
        x, x, (((0,), (0,)), ((), ())), precision=HIGHEST, preferred_element_type=F32
    )


def unpack_first(ac_ref, b_ref, a2_ref, b2_ref, c2_ref):
    slots, each = ac_ref.shape[0], ac_ref.shape[1]
    own = a2_ref.shape[0] // slots
    core = lax.axis_index("gz")
    flat = ac_ref.reshape(slots * each, ac_ref.shape[2])
    for n in range(slots):
        a2_ref[n * own : (n + 1) * own, :] = ac_ref[n, :own, :]
    count = c2_ref.shape[0] // each
    for g in range(each):
        c2_ref[g * count : (g + 1) * count, :] = flat[pl.ds(core * each + g, count, stride=2 * each), :]
    a2_ref[...] = from_lower(a2_ref[...])
    b2_ref[...] = from_lower(b_ref[...])
    c2_ref[...] = from_upper(c2_ref[...])


def unpack_second(ac_ref, cb_ref, a2_ref, b2_ref, c2_ref):
    a2_ref[...] = from_lower(ac_ref[...])
    b2_ref[...] = from_upper(cb_ref[: b2_ref.shape[0], :])
    c2_ref[...] = from_upper(ac_ref[...])


def pack_first(a, b, c_ref, ab_ref, out_c_ref):
    count_b = b.shape[0]
    lower = lower_half(b.shape)
    ab_ref[:count_b, :] = jnp.where(lower, a[:count_b], b)
    ab_ref[count_b:, :] = jnp.where(lower_half(a[count_b:].shape), a[count_b:], 0.0)
    out_c_ref[...] = c_ref[...]


def pack_second(a, b, c_ref, ac_ref, b_ref):
    core = lax.axis_index("gz")
    slots, each, width = ac_ref.shape
    own, apart = a.shape[0] // slots, c_ref.shape[0] // each
    lower = lower_half((own, width))
    for n in range(slots):
        block = c_ref[pl.ds(n // 2, each, stride=apart), :]
        block = jnp.where(core == n % 2, block, 0.0)
        ac_ref[n, :, :] = block
        ac_ref[n, :own, :] = jnp.where(lower, a[n * own : (n + 1) * own], block[:own])
    b_ref[...] = b


def round_kernel(first, keep, scale, *refs):
    small, t_ref, outs = refs[:2], refs[2], refs[3:5]
    a2_ref, b2_ref, c2_ref, wc_ref, at_ref, ma_ref = refs[5:11]
    if first:
        t_hbm, (t_ref, sems) = t_ref, refs[11:]
    count_i, count_j, count_k = a2_ref.shape[0], b2_ref.shape[0], c2_ref.shape[0]
    width = a2_ref.shape[1]
    rank = width // 2
    chunks = t_ref.shape[0] // CHUNK
    per = CHUNK // count_j

    def fetch(c):
        at = pl.ds(pl.multiple_of(c * CHUNK, CHUNK), CHUNK)
        return pltpu.make_async_copy(t_hbm.at[at, :], t_ref.at[at, :], sems.at[c])

    for c in range(chunks if first else 0):
        fetch(c).start()

    (unpack_first if first else unpack_second)(*small, a2_ref, b2_ref, c2_ref)
    a2, b2, c2 = a2_ref[...], b2_ref[...], c2_ref[...]
    high = c2.astype(BF16).astype(F32)
    both = jnp.where(lower_half(c2.shape), high, c2 - high).astype(BF16)
    wc_ref[:count_k, :] = both
    wc_ref[count_k:, :] = both
    at_ref[...] = a2.T[:rank]
    turned_b = b2.T[:rank]
    turned_b = jnp.concatenate([turned_b] * (128 // count_j), axis=1)
    gram_a, gram_b, gram_c = gram(a2), gram(b2), gram(c2)

    def model(factor, one, two):
        return 0.5 * jnp.dot(factor, one * two, precision=HIGHEST, preferred_element_type=F32)

    model_a = model(a2, gram_b, gram_c)
    model_b = model(b2, gram_a, gram_c)
    model_c = model(c2, gram_a, gram_b)
    group = 128 // count_j
    lane = lax.broadcasted_iota(jnp.int32, (rank, 128), 1) // count_j

    def step(c, carry):
        moment_b, moment_c = carry
        if first:
            fetch(c).wait()
        high, low = split(t_ref[pl.ds(pl.multiple_of(c * CHUNK, CHUNK), CHUNK), :])
        terms = jnp.concatenate([high, low], axis=1)
        y = jnp.dot(terms, wc_ref[...], preferred_element_type=F32)
        y = y.reshape(per, count_j, width)
        at_i = pl.multiple_of(c * per, per)
        ma_ref[pl.ds(at_i, per), :] = jnp.sum(y * b2_ref[...][None], axis=1)
        for m in range(per):
            moment_b = moment_b + y[m] * a2_ref[pl.ds(at_i + m, 1), :]
        near = pltpu.roll(at_ref[...], count_i - at_i, 1)
        pieces = []
        for m in range(0, per, group):
            columns = jnp.broadcast_to(near[:, m : m + 1], (rank, 128))
            for g in range(1, group):
                other = jnp.broadcast_to(near[:, m + g : m + g + 1], (rank, 128))
                columns = jnp.where(lane == g, other, columns)
            pieces.append(columns * turned_b)
        rows_high, rows_low = split(jnp.concatenate(pieces, axis=1))
        rows = jnp.concatenate([rows_high, rows_low], axis=0)
        moment_c = moment_c + jnp.dot(rows, terms, preferred_element_type=F32)
        return moment_b, moment_c

    moment_b, moment_c = lax.fori_loop(
        0,
        chunks,
        step,
        (jnp.zeros((count_j, width), F32), jnp.zeros((width, 2 * count_k), F32)),
        unroll=UNROLL,
    )
    moment_c = moment_c[:, :count_k] + moment_c[:, count_k:]
    moment_c = moment_c[:rank] + moment_c[rank:]
    moment_c = jnp.concatenate([moment_c, moment_c], axis=0).T
    moment_a = ma_ref[...]

    def result(factor, whole, moment, weight, factor_scale):
        out = (whole - moment) * factor_scale
        return out + factor * weight if weight else out

    a = result(a2_ref[...], model_a, moment_a + turn(moment_a), keep[0], scale[0])
    b = result(b2_ref[...], model_b, moment_b + turn(moment_b), keep[1], scale[1])
    c2_ref[...] = result(c2_ref[...], model_c, moment_c, keep[2], scale[2])
    (pack_first if first else pack_second)(a, b, c2_ref, *outs)


def partials(first, keep, scale, small, tensor, out_shapes):
    count_i, count_j, count_k = tensor.shape
    width = small[0].shape[-1]
    tall = count_i * count_j
    fetched = [pltpu.VMEM((tall, count_k), F32), pltpu.SemaphoreType.DMA((tall // CHUNK,))]
    fetched = fetched if first else []
    return pl.pallas_call(
        functools.partial(round_kernel, first, keep, scale),
        out_shape=tuple(jax.ShapeDtypeStruct(s, F32) for s in out_shapes),
        in_specs=[VMEM, VMEM, HBM if first else VMEM],
        out_specs=(VMEM, VMEM),
        scratch_shapes=[
            pltpu.VMEM((count_i, width), F32),
            pltpu.VMEM((count_j, width), F32),
            pltpu.VMEM((count_k, width), F32),
            pltpu.VMEM((2 * count_k, width), BF16),
            pltpu.VMEM((width // 2, count_i), F32),
            pltpu.VMEM((count_i, width), F32),
            *fetched,
        ],
        compiler_params=pltpu.CompilerParams(vmem_limit_bytes=(60 if first else 24) << 20),
        cost_estimate=pl.CostEstimate(flops=1 << 30, bytes_accessed=4 << 20, transcendentals=0),
        name="partials",
    )(*small, tensor.reshape(tall, count_k))


def send_all(x, axes):
    count = 1
    for name in axes:
        count *= lax.axis_size(name)
    return lax.all_to_all(jnp.broadcast_to(x[None], (count, *x.shape)), axes, 0, 0, tiled=True)


def shift(x, axis, stride, count, by):
    pairs = []
    for n in range(lax.axis_size(axis)):
        place = n // stride % count
        pairs.append((n, n + ((place + by) % count - place) * stride))
    return lax.ppermute(x, axis, pairs)


def ring8(x):
    below, above = shift(x, "gx", 1, 8, 1), shift(x, "gx", 1, 8, -1)
    two = x + above
    three = two + below
    return three + (shift(three, "gx", 1, 8, -3) + shift(two, "gx", 1, 8, 3))


def ring4(x, stride):
    ones = shift(x, "gy", stride, 4, 1) + shift(x, "gy", stride, 4, -1)
    return (x + ones) + shift(x, "gy", stride, 4, 2)


def swap(x):
    return lax.ppermute(x, "gz", [(0, 1), (1, 0)])


def shards(tensor, factor_a, factor_b, factor_c):
    count_x, count_y, count_z = (lax.axis_size(n) for n in ("gx", "gy", "gz"))
    core = lax.axis_index("gz")
    count_i, count_j, count_k = tensor.shape
    whole = (
        float(count_j * count_y * count_k * count_z),
        float(count_i * count_x * count_k * count_z),
        float(count_i * count_x * count_j * count_y),
    )
    copies = (count_y * count_z, count_x * count_z, count_x * count_y)
    own, rank = factor_a.shape
    wide = 2 * rank

    padded_c = jnp.pad(factor_c, ((0, own - 1), (0, 0)))
    along_x = send_all(jnp.concatenate([factor_b, padded_c], axis=1), ("gx", "gz"))
    rows_c = along_x.reshape(count_x, count_z, own, wide)[:, :, 0, rank:]
    rows_c = jnp.where(core == 0, rows_c[:, 0], rows_c[:, 1])
    padded_a = jnp.pad(factor_a, ((0, count_x - own), (0, 0)))
    along_y = send_all(jnp.concatenate([padded_a, rows_c], axis=1), ("gy", "gz"))

    keep = tuple(1.0 / n for n in copies)
    scale = tuple(-STEP_SIZE / n for n in whole)
    small = (along_y, along_x.reshape(count_j, wide))
    ab, c = partials(True, keep, scale, small, tensor, ((count_i, wide), (count_k, wide)))
    ab = ab + swap(ab)
    cb = ring8(jnp.where(lower_half(c.shape), c, ab))
    ac = ring4(ring4(jnp.concatenate([ab[:, :rank], cb[:, :rank]], axis=1), 1), 4)

    scale = tuple(1.0 / n for n in whole)
    shapes = ((count_y * count_z, 2 * own, wide), (count_j, wide))
    slots_ac, b = partials(False, (0.0,) * 3, scale, (ac, cb), tensor, shapes)
    ac = jnp.sum(lax.all_to_all(slots_ac, ("gy", "gz"), 0, 0, tiled=True), axis=0)
    mine = (jnp.arange(count_z) == core)[None, :, None, None]
    slots_c = jnp.where(mine, ac[:, None, None, rank:], 0.0)
    slots_c = jnp.pad(slots_c, ((0, 0), (0, 0), (0, own - 1), (0, 0)))
    slots_b = b.reshape(count_x, count_z, own, wide)[..., :rank]
    slots_bc = jnp.concatenate([slots_b, slots_c], axis=3).reshape(-1, own, wide)
    bc = jnp.sum(lax.all_to_all(slots_bc, ("gx", "gz"), 0, 0, tiled=True), axis=0)
    return ac[:own, :rank], bc[:, :rank], bc[:1, rank:]


def solution(mesh):
    factors = (
        P(("gx", "gy", "gz"), None),
        P(("gy", "gx", "gz"), None),
        P(("gz", "gx", "gy"), None),
    )
    return jax.shard_map(
        shards,
        mesh=mesh,
        in_specs=(P("gx", "gy", "gz"), *factors),
        out_specs=factors,
        check_vma=False,
    )
```

```python
import functools

import jax
import jax.numpy as jnp
from jax import lax
from jax.experimental import pallas as pl
from jax.experimental.pallas import tpu as pltpu
from jax.sharding import PartitionSpec as P

STEPS = 2
STEP_SIZE = 0.1
F32 = jnp.float32
BF16 = jnp.bfloat16
HIGHEST = lax.Precision.HIGHEST
VMEM = pl.BlockSpec(memory_space=pltpu.VMEM)
HBM = pl.BlockSpec(memory_space=pltpu.HBM)
CHUNK = 512


def split(x):
    high = x.astype(BF16)
    return high, (x - high.astype(F32)).astype(BF16)


def lower_half(shape):
    return lax.broadcasted_iota(jnp.int32, shape, len(shape) - 1) < shape[-1] // 2


def turn(x):
    return pltpu.roll(x, x.shape[1] // 2, 1)


def from_lower(x):
    return jnp.where(lower_half(x.shape), x, turn(x))


def from_upper(x):
    return jnp.where(lower_half(x.shape), turn(x), x)


def gram(x):
    return lax.dot_general(
        x, x, (((0,), (0,)), ((), ())), precision=HIGHEST, preferred_element_type=F32
    )


def unpack_first(ac_ref, b_ref, a2_ref, b2_ref, c2_ref):
    slots, each = ac_ref.shape[0], ac_ref.shape[1]
    own = a2_ref.shape[0] // slots
    core = lax.axis_index("gz")
    flat = ac_ref.reshape(slots * each, ac_ref.shape[2])
    for n in range(slots):
        a2_ref[n * own : (n + 1) * own, :] = ac_ref[n, :own, :]
    count = c2_ref.shape[0] // each
    for g in range(each):
        c2_ref[g * count : (g + 1) * count, :] = flat[pl.ds(core * each + g, count, stride=2 * each), :]
    a2_ref[...] = from_lower(a2_ref[...])
    b2_ref[...] = from_lower(b_ref[...])
    c2_ref[...] = from_upper(c2_ref[...])


def unpack_second(ac_ref, cb_ref, a2_ref, b2_ref, c2_ref):
    a2_ref[...] = from_lower(ac_ref[...])
    b2_ref[...] = from_upper(cb_ref[: b2_ref.shape[0], :])
    c2_ref[...] = from_upper(ac_ref[...])


def pack_first(a, b, c_ref, ab_ref, out_c_ref):
    count_b = b.shape[0]
    lower = lower_half(b.shape)
    ab_ref[:count_b, :] = jnp.where(lower, a[:count_b], b)
    ab_ref[count_b:, :] = jnp.where(lower_half(a[count_b:].shape), a[count_b:], 0.0)
    out_c_ref[...] = c_ref[...]


def pack_second(a, b, c_ref, ac_ref, b_ref):
    core = lax.axis_index("gz")
    slots, each, width = ac_ref.shape
    own, apart = a.shape[0] // slots, c_ref.shape[0] // each
    lower = lower_half((own, width))
    for n in range(slots):
        block = c_ref[pl.ds(n // 2, each, stride=apart), :]
        block = jnp.where(core == n % 2, block, 0.0)
        ac_ref[n, :, :] = block
        ac_ref[n, :own, :] = jnp.where(lower, a[n * own : (n + 1) * own], block[:own])
    b_ref[...] = b


def round_kernel(first, keep, scale, *refs):
    small, t_ref, outs = refs[:2], refs[2], refs[3:5]
    a2_ref, b2_ref, c2_ref, wc_ref, at_ref, ma_ref = refs[5:11]
    if first:
        t_hbm, (t_ref, sems) = t_ref, refs[11:]
    count_i, count_j, count_k = a2_ref.shape[0], b2_ref.shape[0], c2_ref.shape[0]
    width = a2_ref.shape[1]
    rank = width // 2
    chunks = t_ref.shape[0] // CHUNK
    per = CHUNK // count_j

    def fetch(c):
        at = pl.ds(pl.multiple_of(c * CHUNK, CHUNK), CHUNK)
        return pltpu.make_async_copy(t_hbm.at[at, :], t_ref.at[at, :], sems.at[c])

    for c in range(chunks if first else 0):
        fetch(c).start()

    (unpack_first if first else unpack_second)(*small, a2_ref, b2_ref, c2_ref)
    a2, b2, c2 = a2_ref[...], b2_ref[...], c2_ref[...]
    high = c2.astype(BF16).astype(F32)
    both = jnp.where(lower_half(c2.shape), high, c2 - high).astype(BF16)
    wc_ref[:count_k, :] = both
    wc_ref[count_k:, :] = both
    at_ref[...] = a2.T[:rank]
    turned_b = b2.T[:rank]
    turned_b = jnp.concatenate([turned_b] * (128 // count_j), axis=1)
    gram_a, gram_b, gram_c = gram(a2), gram(b2), gram(c2)

    def model(factor, one, two):
        return 0.5 * jnp.dot(factor, one * two, precision=HIGHEST, preferred_element_type=F32)

    model_a = model(a2, gram_b, gram_c)
    model_b = model(b2, gram_a, gram_c)
    model_c = model(c2, gram_a, gram_b)
    group = 128 // count_j
    lane = lax.broadcasted_iota(jnp.int32, (rank, 128), 1) // count_j

    def step(c, carry):
        moment_b, moment_c = carry
        if first:
            fetch(c).wait()
        high, low = split(t_ref[pl.ds(pl.multiple_of(c * CHUNK, CHUNK), CHUNK), :])
        terms = jnp.concatenate([high, low], axis=1)
        y = jnp.dot(terms, wc_ref[...], preferred_element_type=F32)
        y = y.reshape(per, count_j, width)
        at_i = pl.multiple_of(c * per, per)
        ma_ref[pl.ds(at_i, per), :] = jnp.sum(y * b2_ref[...][None], axis=1)
        for m in range(per):
            moment_b = moment_b + y[m] * a2_ref[pl.ds(at_i + m, 1), :]
        near = pltpu.roll(at_ref[...], count_i - at_i, 1)
        pieces = []
        for m in range(0, per, group):
            columns = jnp.broadcast_to(near[:, m : m + 1], (rank, 128))
            for g in range(1, group):
                other = jnp.broadcast_to(near[:, m + g : m + g + 1], (rank, 128))
                columns = jnp.where(lane == g, other, columns)
            pieces.append(columns * turned_b)
        rows_high, rows_low = split(jnp.concatenate(pieces, axis=1))
        rows = jnp.concatenate([rows_high, rows_low], axis=0)
        moment_c = moment_c + jnp.dot(rows, terms, preferred_element_type=F32)
        return moment_b, moment_c

    moment_b, moment_c = lax.fori_loop(
        0,
        chunks,
        step,
        (jnp.zeros((count_j, width), F32), jnp.zeros((width, 2 * count_k), F32)),
        unroll=True,
    )
    moment_c = moment_c[:, :count_k] + moment_c[:, count_k:]
    moment_c = moment_c[:rank] + moment_c[rank:]
    moment_c = jnp.concatenate([moment_c, moment_c], axis=0).T
    moment_a = ma_ref[...]

    def result(factor, whole, moment, weight, factor_scale):
        out = (whole - moment) * factor_scale
        return out + factor * weight if weight else out

    a = result(a2_ref[...], model_a, moment_a + turn(moment_a), keep[0], scale[0])
    b = result(b2_ref[...], model_b, moment_b + turn(moment_b), keep[1], scale[1])
    c2_ref[...] = result(c2_ref[...], model_c, moment_c, keep[2], scale[2])
    (pack_first if first else pack_second)(a, b, c2_ref, *outs)


def partials(first, keep, scale, small, tensor, out_shapes):
    count_i, count_j, count_k = tensor.shape
    width = small[0].shape[-1]
    tall = count_i * count_j
    fetched = [pltpu.VMEM((tall, count_k), F32), pltpu.SemaphoreType.DMA((tall // CHUNK,))]
    fetched = fetched if first else []
    tensor = tensor.reshape(tall, count_k)
    if first:
        tensor = pltpu.with_memory_space_constraint(tensor, pltpu.HBM)
    return pl.pallas_call(
        functools.partial(round_kernel, first, keep, scale),
        out_shape=tuple(jax.ShapeDtypeStruct(s, F32) for s in out_shapes),
        in_specs=[VMEM, VMEM, HBM if first else VMEM],
        out_specs=(VMEM, VMEM),
        scratch_shapes=[
            pltpu.VMEM((count_i, width), F32),
            pltpu.VMEM((count_j, width), F32),
            pltpu.VMEM((count_k, width), F32),
            pltpu.VMEM((2 * count_k, width), BF16),
            pltpu.VMEM((width // 2, count_i), F32),
            pltpu.VMEM((count_i, width), F32),
            *fetched,
        ],
        compiler_params=pltpu.CompilerParams(vmem_limit_bytes=24 << 20),
        cost_estimate=pl.CostEstimate(flops=1 << 30, bytes_accessed=4 << 20, transcendentals=0),
        name="partials",
    )(*small, tensor)


def send_all(left, right, axes):
    count = 1
    for name in axes:
        count *= lax.axis_size(name)
    both = jnp.concatenate([left, right], axis=1)
    return lax.all_to_all(jnp.broadcast_to(both[None], (count, *both.shape)), axes, 0, 0, tiled=True)


def shift(x, axis, stride, count, by):
    pairs = []
    for n in range(lax.axis_size(axis)):
        place = n // stride % count
        pairs.append((n, n + ((place + by) % count - place) * stride))
    return lax.ppermute(x, axis, pairs)


def ring8(x):
    below, above = shift(x, "gx", 1, 8, 1), shift(x, "gx", 1, 8, -1)
    two = x + above
    three = two + below
    return three + (shift(three, "gx", 1, 8, -3) + shift(two, "gx", 1, 8, 3))


def ring4(x, stride):
    ones = shift(x, "gy", stride, 4, 1) + shift(x, "gy", stride, 4, -1)
    return (x + ones) + shift(x, "gy", stride, 4, 2)


def swap(x):
    return lax.ppermute(x, "gz", [(0, 1), (1, 0)])


def shards(tensor, factor_a, factor_b, factor_c):
    count_x, count_y, count_z = (lax.axis_size(n) for n in ("gx", "gy", "gz"))
    core = lax.axis_index("gz")
    count_i, count_j, count_k = tensor.shape
    whole = (
        float(count_j * count_y * count_k * count_z),
        float(count_i * count_x * count_k * count_z),
        float(count_i * count_x * count_j * count_y),
    )
    copies = (count_y * count_z, count_x * count_z, count_x * count_y)
    own, rank = factor_a.shape
    wide = 2 * rank

    padded_c = jnp.pad(factor_c, ((0, own - 1), (0, 0)))
    along_x = send_all(factor_b, padded_c, ("gx", "gz"))
    rows_c = along_x.reshape(count_x, count_z, own, wide)[:, :, 0, rank:]
    rows_c = jnp.where(core == 0, rows_c[:, 0], rows_c[:, 1])
    padded_a = lax.optimization_barrier(jnp.pad(factor_a, ((0, count_x - own), (0, 0))))
    along_y = send_all(padded_a, rows_c, ("gy", "gz"))

    keep = tuple(1.0 / n for n in copies)
    scale = tuple(-STEP_SIZE / n for n in whole)
    small = (along_y, along_x.reshape(count_j, wide))
    ab, c = partials(True, keep, scale, small, tensor, ((count_i, wide), (count_k, wide)))
    ab = ab + swap(ab)
    cb = ring8(jnp.where(lower_half(c.shape), c, ab))
    ac = ring4(ring4(jnp.concatenate([ab[:, :rank], cb[:, :rank]], axis=1), 1), 4)

    scale = tuple(1.0 / n for n in whole)
    shapes = ((count_y * count_z, 2 * own, wide), (count_j, wide))
    slots_ac, b = partials(False, (0.0,) * 3, scale, (ac, cb), tensor, shapes)
    ac = jnp.sum(lax.all_to_all(slots_ac, ("gy", "gz"), 0, 0, tiled=True), axis=0)
    mine = (jnp.arange(count_z) == core)[None, :, None, None]
    slots_c = jnp.where(mine, ac[:, None, None, rank:], 0.0)
    slots_c = jnp.pad(slots_c, ((0, 0), (0, 0), (0, own - 1), (0, 0)))
    slots_b = b.reshape(count_x, count_z, own, wide)[..., :rank]
    slots_bc = jnp.concatenate([slots_b, slots_c], axis=3).reshape(-1, own, wide)
    bc = lax.all_to_all(slots_bc, ("gx", "gz"), 0, 0, tiled=True)
    return ac[:own, :rank], jnp.sum(bc[:, :, :rank], axis=0), jnp.sum(bc[:, :1, rank:], axis=0)


def solution(mesh):
    factors = (
        P(("gx", "gy", "gz"), None),
        P(("gy", "gx", "gz"), None),
        P(("gz", "gx", "gy"), None),
    )
    return jax.shard_map(
        shards,
        mesh=mesh,
        in_specs=(P("gx", "gy", "gz"), *factors),
        out_specs=factors,
        check_vma=False,
    )
```

```python
import functools

import jax
import jax.numpy as jnp
from jax import lax
from jax.experimental import pallas as pl
from jax.experimental.pallas import tpu as pltpu
from jax.sharding import PartitionSpec as P

STEPS = 2
STEP_SIZE = 0.1
F32 = jnp.float32
BF16 = jnp.bfloat16
HIGHEST = lax.Precision.HIGHEST
VMEM = pl.BlockSpec(memory_space=pltpu.VMEM)
HBM = pl.BlockSpec(memory_space=pltpu.HBM)
CHUNK = 512


def split(x):
    high = x.astype(BF16)
    return high, (x - high.astype(F32)).astype(BF16)


def lower_half(shape):
    return lax.broadcasted_iota(jnp.int32, shape, len(shape) - 1) < shape[-1] // 2


def turn(x):
    return pltpu.roll(x, x.shape[1] // 2, 1)


def from_lower(x):
    return jnp.where(lower_half(x.shape), x, turn(x))


def from_upper(x):
    return jnp.where(lower_half(x.shape), turn(x), x)


def gram(x):
    return lax.dot_general(
        x, x, (((0,), (0,)), ((), ())), precision=HIGHEST, preferred_element_type=F32
    )


def unpack_first(ac_ref, b_ref, a2_ref, b2_ref, c2_ref):
    slots, each = ac_ref.shape[0], ac_ref.shape[1]
    own = a2_ref.shape[0] // slots
    core = lax.axis_index("gz")
    flat = ac_ref.reshape(slots * each, ac_ref.shape[2])
    for n in range(slots):
        a2_ref[n * own : (n + 1) * own, :] = ac_ref[n, :own, :]
    count = c2_ref.shape[0] // each
    for g in range(each):
        c2_ref[g * count : (g + 1) * count, :] = flat[pl.ds(core * each + g, count, stride=2 * each), :]
    a2_ref[...] = from_lower(a2_ref[...])
    b2_ref[...] = from_lower(b_ref[...])
    c2_ref[...] = from_upper(c2_ref[...])


def unpack_second(ac_ref, cb_ref, a2_ref, b2_ref, c2_ref):
    a2_ref[...] = from_lower(ac_ref[...])
    b2_ref[...] = from_upper(cb_ref[: b2_ref.shape[0], :])
    c2_ref[...] = from_upper(ac_ref[...])


def pack_first(a, b, c_ref, ab_ref, out_c_ref):
    count_b = b.shape[0]
    lower = lower_half(b.shape)
    ab_ref[:count_b, :] = jnp.where(lower, a[:count_b], b)
    ab_ref[count_b:, :] = jnp.where(lower_half(a[count_b:].shape), a[count_b:], 0.0)
    out_c_ref[...] = c_ref[...]


def pack_second(a, b, c_ref, ac_ref, b_ref):
    core = lax.axis_index("gz")
    slots, each, width = ac_ref.shape
    own, apart = a.shape[0] // slots, c_ref.shape[0] // each
    lower = lower_half((own, width))
    for n in range(slots):
        block = c_ref[pl.ds(n // 2, each, stride=apart), :]
        block = jnp.where(core == n % 2, block, 0.0)
        ac_ref[n, :, :] = block
        ac_ref[n, :own, :] = jnp.where(lower, a[n * own : (n + 1) * own], block[:own])
    b_ref[...] = b


def round_kernel(first, keep, scale, *refs):
    small, t_ref, outs = refs[:2], refs[2], refs[3:5]
    if first:
        t_hbm, t_ref, sems = t_ref, refs[5], refs[-1]
    a2_ref, b2_ref, c2_ref, wc_ref, at_ref, ma_ref = refs[6:12] if first else refs[5:]
    count_i, count_j, count_k = a2_ref.shape[0], b2_ref.shape[0], c2_ref.shape[0]
    width = a2_ref.shape[1]
    rank = width // 2
    chunks = t_ref.shape[0] // CHUNK
    per = CHUNK // count_j

    def fetch(c):
        at = pl.ds(pl.multiple_of(c * CHUNK, CHUNK), CHUNK)
        return pltpu.make_async_copy(t_hbm.at[at, :], t_ref.at[at, :], sems.at[c])

    for c in range(chunks if first else 0):
        fetch(c).start()

    (unpack_first if first else unpack_second)(*small, a2_ref, b2_ref, c2_ref)
    a2, b2, c2 = a2_ref[...], b2_ref[...], c2_ref[...]
    high = c2.astype(BF16).astype(F32)
    both = jnp.where(lower_half(c2.shape), high, c2 - high).astype(BF16)
    wc_ref[:count_k, :] = both
    wc_ref[count_k:, :] = both
    at_ref[...] = a2.T[:rank]
    turned_b = b2.T[:rank]
    turned_b = jnp.concatenate([turned_b] * (128 // count_j), axis=1)
    gram_a, gram_b, gram_c = gram(a2), gram(b2), gram(c2)

    def model(factor, one, two):
        return 0.5 * jnp.dot(factor, one * two, precision=HIGHEST, preferred_element_type=F32)

    model_a = model(a2, gram_b, gram_c)
    model_b = model(b2, gram_a, gram_c)
    model_c = model(c2, gram_a, gram_b)
    group = 128 // count_j
    lane = lax.broadcasted_iota(jnp.int32, (rank, 128), 1) // count_j

    def step(c, carry):
        moment_b, moment_c = carry
        if first:
            fetch(c).wait()
        high, low = split(t_ref[pl.ds(pl.multiple_of(c * CHUNK, CHUNK), CHUNK), :])
        terms = jnp.concatenate([high, low], axis=1)
        y = jnp.dot(terms, wc_ref[...], preferred_element_type=F32)
        y = y.reshape(per, count_j, width)
        at_i = pl.multiple_of(c * per, per)
        ma_ref[pl.ds(at_i, per), :] = jnp.sum(y * b2_ref[...][None], axis=1)
        for m in range(per):
            moment_b = moment_b + y[m] * a2_ref[pl.ds(at_i + m, 1), :]
        near = pltpu.roll(at_ref[...], count_i - at_i, 1)
        pieces = []
        for m in range(0, per, group):
            columns = jnp.broadcast_to(near[:, m : m + 1], (rank, 128))
            for g in range(1, group):
                other = jnp.broadcast_to(near[:, m + g : m + g + 1], (rank, 128))
                columns = jnp.where(lane == g, other, columns)
            pieces.append(columns * turned_b)
        rows_high, rows_low = split(jnp.concatenate(pieces, axis=1))
        rows = jnp.concatenate([rows_high, rows_low], axis=0)
        moment_c = moment_c + jnp.dot(rows, terms, preferred_element_type=F32)
        return moment_b, moment_c

    moment_b, moment_c = lax.fori_loop(
        0,
        chunks,
        step,
        (jnp.zeros((count_j, width), F32), jnp.zeros((width, 2 * count_k), F32)),
        unroll=True,
    )
    moment_c = moment_c[:, :count_k] + moment_c[:, count_k:]
    moment_c = moment_c[:rank] + moment_c[rank:]
    moment_c = jnp.concatenate([moment_c, moment_c], axis=0).T
    moment_a = ma_ref[...]

    def result(factor, whole, moment, weight, factor_scale):
        out = (whole - moment) * factor_scale
        return out + factor * weight if weight else out

    a = result(a2_ref[...], model_a, moment_a + turn(moment_a), keep[0], scale[0])
    b = result(b2_ref[...], model_b, moment_b + turn(moment_b), keep[1], scale[1])
    c2_ref[...] = result(c2_ref[...], model_c, moment_c, keep[2], scale[2])
    (pack_first if first else pack_second)(a, b, c2_ref, *outs)


def partials(first, keep, scale, small, tensor, sizes, out_shapes):
    count_i, count_j, count_k = sizes
    width = small[0].shape[-1]
    tall = count_i * count_j
    if first:
        tensor = pltpu.with_memory_space_constraint(tensor, pltpu.HBM)
        out_shapes += ((tall, count_k),)
    return pl.pallas_call(
        functools.partial(round_kernel, first, keep, scale),
        out_shape=tuple(jax.ShapeDtypeStruct(s, F32) for s in out_shapes),
        in_specs=[VMEM, VMEM, HBM if first else VMEM],
        out_specs=(VMEM,) * len(out_shapes),
        scratch_shapes=[
            pltpu.VMEM((count_i, width), F32),
            pltpu.VMEM((count_j, width), F32),
            pltpu.VMEM((count_k, width), F32),
            pltpu.VMEM((2 * count_k, width), BF16),
            pltpu.VMEM((width // 2, count_i), F32),
            pltpu.VMEM((count_i, width), F32),
        ]
        + [pltpu.SemaphoreType.DMA((tall // CHUNK,))] * first,
        compiler_params=pltpu.CompilerParams(vmem_limit_bytes=24 << 20),
        cost_estimate=pl.CostEstimate(flops=1 << 30, bytes_accessed=4 << 20, transcendentals=0),
        name="partials",
    )(*small, tensor)


def first_kernel(a_hbm, b_hbm, c_hbm, slots_ref, a_out_ref, a_ref, b_ref, c_ref, sems):
    own, rank = a_ref.shape
    pairs = ((a_hbm, a_ref), (b_hbm, b_ref), (c_hbm, c_ref))
    copies = [pltpu.make_async_copy(x, y, sems.at[n]) for n, (x, y) in enumerate(pairs)]
    for copy in copies:
        copy.start()
    a_out_ref[...] = jnp.zeros(a_out_ref.shape, F32)
    for copy in copies:
        copy.wait()
    a_out_ref[:own, :rank] = a_ref[...]
    slot = jnp.concatenate([b_ref[...], jnp.broadcast_to(c_ref[...], (own, rank))], axis=1)
    for n in range(slots_ref.shape[0]):
        slots_ref[n, :, :] = slot


def first_slots(a, b, c, count, tall):
    own, rank = a.shape
    factors = [pltpu.with_memory_space_constraint(x, pltpu.HBM) for x in (a, b, c)]
    return pl.pallas_call(
        first_kernel,
        out_shape=(
            jax.ShapeDtypeStruct((count, own, 2 * rank), F32),
            jax.ShapeDtypeStruct((tall, 2 * rank), F32),
        ),
        in_specs=[HBM] * 3,
        out_specs=(VMEM, VMEM),
        scratch_shapes=[pltpu.VMEM(x.shape, F32) for x in (a, b, c)]
        + [pltpu.SemaphoreType.DMA((3,))],
        compiler_params=pltpu.CompilerParams(vmem_limit_bytes=4 << 20),
        name="first_slots",
    )(*factors)


def last_kernel(ac_ref, bc_ref, a_ref, b_ref, c_ref):
    own, rank = a_ref.shape
    bc = jnp.sum(bc_ref[...], axis=0)
    a_ref[...] = ac_ref[:own, :rank]
    b_ref[...] = bc[:, :rank]
    c_ref[...] = bc[:1, rank:]


def last_sums(ac, bc, own, rank):
    return pl.pallas_call(
        last_kernel,
        out_shape=tuple(jax.ShapeDtypeStruct((n, rank), F32) for n in (own, own, 1)),
        compiler_params=pltpu.CompilerParams(vmem_limit_bytes=4 << 20),
        name="last_sums",
    )(ac, bc)


def shift(x, axis, stride, count, by):
    pairs = []
    for n in range(lax.axis_size(axis)):
        place = n // stride % count
        pairs.append((n, n + ((place + by) % count - place) * stride))
    return lax.ppermute(x, axis, pairs)


def ring8(x):
    below, above = shift(x, "gx", 1, 8, 1), shift(x, "gx", 1, 8, -1)
    two = x + above
    three = two + below
    return three + (shift(three, "gx", 1, 8, -3) + shift(two, "gx", 1, 8, 3))


def ring4(x, stride):
    ones = shift(x, "gy", stride, 4, 1) + shift(x, "gy", stride, 4, -1)
    return (x + ones) + shift(x, "gy", stride, 4, 2)


def swap(x):
    return lax.ppermute(x, "gz", [(0, 1), (1, 0)])


def shards(tensor, factor_a, factor_b, factor_c):
    count_x, count_y, count_z = (lax.axis_size(n) for n in ("gx", "gy", "gz"))
    core = lax.axis_index("gz")
    count_i, count_j, count_k = tensor.shape
    whole = (
        float(count_j * count_y * count_k * count_z),
        float(count_i * count_x * count_k * count_z),
        float(count_i * count_x * count_j * count_y),
    )
    copies = (count_y * count_z, count_x * count_z, count_x * count_y)
    own, rank = factor_a.shape
    wide = 2 * rank

    slots, rows_a = first_slots(factor_a, factor_b, factor_c, count_x * count_z, count_x)
    along_x = lax.all_to_all(slots, ("gx", "gz"), 0, 0, tiled=True)
    rows_c = along_x.reshape(count_x, count_z, own, wide)[:, :, 0]
    rows_c = jnp.where(core == 0, rows_c[:, 0], rows_c[:, 1])
    slot = jnp.where(lower_half(rows_c.shape), rows_a, rows_c)
    slots = jnp.broadcast_to(slot[None], (count_y * count_z, count_x, wide))
    along_y = lax.all_to_all(slots, ("gy", "gz"), 0, 0, tiled=True)

    keep = tuple(1.0 / n for n in copies)
    scale = tuple(-STEP_SIZE / n for n in whole)
    small = (along_y, along_x.reshape(count_j, wide))
    sizes = tensor.shape
    tensor = tensor.reshape(count_i * count_j, count_k)
    shapes = ((count_i, wide), (count_k, wide))
    ab, c, tensor = partials(True, keep, scale, small, tensor, sizes, shapes)
    ab = ab + swap(ab)
    cb = ring8(jnp.where(lower_half(c.shape), c, ab))
    ac = ring4(ring4(jnp.concatenate([ab[:, :rank], cb[:, :rank]], axis=1), 1), 4)

    scale = tuple(1.0 / n for n in whole)
    shapes = ((count_y * count_z, 2 * own, wide), (count_j, wide))
    slots_ac, b = partials(False, (0.0,) * 3, scale, (ac, cb), tensor, sizes, shapes)
    ac = jnp.sum(lax.all_to_all(slots_ac, ("gy", "gz"), 0, 0, tiled=True), axis=0)
    mine = (jnp.arange(count_z) == core)[None, :, None, None]
    slots_c = jnp.where(mine, ac[:, None, None, rank:], 0.0)
    slots_c = jnp.pad(slots_c, ((0, 0), (0, 0), (0, own - 1), (0, 0)))
    slots_b = b.reshape(count_x, count_z, own, wide)[..., :rank]
    slots_bc = jnp.concatenate([slots_b, slots_c], axis=3).reshape(-1, own, wide)
    bc = lax.all_to_all(slots_bc, ("gx", "gz"), 0, 0, tiled=True)
    return last_sums(ac, bc, own, rank)


def solution(mesh):
    factors = (
        P(("gx", "gy", "gz"), None),
        P(("gy", "gx", "gz"), None),
        P(("gz", "gx", "gy"), None),
    )
    return jax.shard_map(
        shards,
        mesh=mesh,
        in_specs=(P("gx", "gy", "gz"), *factors),
        out_specs=factors,
        check_vma=False,
    )
```

```python
import functools

import jax
import jax.numpy as jnp
from jax import lax
from jax.experimental import pallas as pl
from jax.experimental.pallas import tpu as pltpu
from jax.sharding import PartitionSpec as P

STEPS = 2
STEP_SIZE = 0.1
F32 = jnp.float32
BF16 = jnp.bfloat16
HIGHEST = lax.Precision.HIGHEST
VMEM = pl.BlockSpec(memory_space=pltpu.VMEM)
HBM = pl.BlockSpec(memory_space=pltpu.HBM)
CHUNK = 512


def split(x):
    high = x.astype(BF16)
    return high, (x - high.astype(F32)).astype(BF16)


def lower_half(shape):
    return lax.broadcasted_iota(jnp.int32, shape, len(shape) - 1) < shape[-1] // 2


def turn(x):
    return pltpu.roll(x, x.shape[1] // 2, 1)


def from_lower(x):
    return jnp.where(lower_half(x.shape), x, turn(x))


def from_upper(x):
    return jnp.where(lower_half(x.shape), turn(x), x)


def gram(x):
    return lax.dot_general(
        x, x, (((0,), (0,)), ((), ())), precision=HIGHEST, preferred_element_type=F32
    )


def unpack_first(ac_ref, own_ref, other_ref, a2_ref, b2_ref, c2_ref):
    slots, each, width = ac_ref.shape
    core = lax.axis_index("gz")
    a2_ref[...] = from_lower(ac_ref[...].reshape(slots * each, width))
    for g in range(each):
        c2_ref[g * slots : (g + 1) * slots, :] = ac_ref[:, g, :]
    c2_ref[...] = from_upper(c2_ref[...])
    slots, each, width = own_ref.shape
    for n in range(slots):
        own, other = own_ref[n], other_ref[n]
        at = 2 * each * n
        b2_ref[at : at + each, :] = jnp.where(core == 0, own, other)
        b2_ref[at + each : at + 2 * each, :] = jnp.where(core == 0, other, own)
    b2_ref[...] = from_lower(b2_ref[...])


def unpack_second(ca_ref, b_ref, a2_ref, b2_ref, c2_ref):
    a2_ref[...] = from_upper(ca_ref[...])
    b2_ref[...] = from_upper(b_ref[...])
    c2_ref[...] = from_lower(ca_ref[...])


def pack_first(a, b, c_ref, a_ref, cb_ref):
    count_b = b.shape[0]
    c = c_ref[...]
    a_ref[...] = a
    cb_ref[:count_b, :] = jnp.where(lower_half(b.shape), c[:count_b], b)
    cb_ref[count_b:, :] = jnp.where(lower_half(c[count_b:].shape), c[count_b:], 0.0)


def pack_second(a, b, c_ref, ac_ref, b_ref):
    slots, each, width = ac_ref.shape
    lower = lower_half((each, width))
    for n in range(slots):
        block = c_ref[pl.ds(n, each, stride=slots), :]
        ac_ref[n, :, :] = jnp.where(lower, a[n * each : (n + 1) * each], block)
    b_ref[...] = b


def round_kernel(first, keep, scale, *refs):
    n_small = 3 if first else 2
    small, t_ref, outs, refs = refs[:n_small], refs[n_small], refs[n_small + 1 :][:2], refs[n_small + 3 :]
    if first:
        t_hbm, t_ref, sems, refs = t_ref, refs[0], refs[-1], refs[1:-1]
    a2_ref, b2_ref, c2_ref, wc_ref, ma_ref = refs
    count_i, count_j, count_k = a2_ref.shape[0], b2_ref.shape[0], c2_ref.shape[0]
    width = a2_ref.shape[1]
    rank = width // 2
    chunks = t_ref.shape[0] // CHUNK
    per = CHUNK // count_j

    def fetch(c):
        at = pl.ds(c * CHUNK, CHUNK)
        return pltpu.make_async_copy(t_hbm.at[at, :], t_ref.at[at, :], sems.at[c])

    for c in range(chunks if first else 0):
        fetch(c).start()

    (unpack_first if first else unpack_second)(*small, a2_ref, b2_ref, c2_ref)
    a2, b2, c2 = a2_ref[...], b2_ref[...], c2_ref[...]
    high = c2.astype(BF16).astype(F32)
    both = jnp.where(lower_half(c2.shape), high, c2 - high).astype(BF16)
    wc_ref[:count_k, :] = both
    wc_ref[count_k:, :] = both
    turned_a = a2.T[:rank]
    turned_b = b2.T[:rank]
    turned_b = jnp.concatenate([turned_b] * (128 // count_j), axis=1)
    gram_a, gram_b, gram_c = gram(a2), gram(b2), gram(c2)

    def model(factor, one, two):
        return 0.5 * jnp.dot(factor, one * two, precision=HIGHEST, preferred_element_type=F32)

    model_a = model(a2, gram_b, gram_c)
    model_b = model(b2, gram_a, gram_c)
    model_c = model(c2, gram_a, gram_b)
    group = 128 // count_j
    lane = lax.broadcasted_iota(jnp.int32, (rank, 128), 1) // count_j

    moment_b = jnp.zeros((count_j, width), F32)
    moment_c = jnp.zeros((width, 2 * count_k), F32)
    for c in range(chunks):
        if first and c % (chunks // 2) == 0:
            for n in range(c, c + chunks // 2):
                fetch(n).wait()
        high, low = split(t_ref[c * CHUNK : (c + 1) * CHUNK, :])
        terms = jnp.concatenate([high, low], axis=1)
        y = jnp.dot(terms, wc_ref[...], preferred_element_type=F32)
        y = y.reshape(per, count_j, width)
        at_i = c * per
        ma_ref[at_i : at_i + per, :] = jnp.sum(y * b2_ref[...][None], axis=1)
        for m in range(per):
            moment_b = moment_b + y[m] * a2_ref[at_i + m : at_i + m + 1, :]
        pieces = []
        for m in range(at_i, at_i + per, group):
            columns = jnp.broadcast_to(turned_a[:, m : m + 1], (rank, 128))
            for g in range(1, group):
                other = jnp.broadcast_to(turned_a[:, m + g : m + g + 1], (rank, 128))
                columns = jnp.where(lane == g, other, columns)
            pieces.append(columns * turned_b)
        rows_high, rows_low = split(jnp.concatenate(pieces, axis=1))
        rows = jnp.concatenate([rows_high, rows_low], axis=0)
        moment_c = moment_c + jnp.dot(rows, terms, preferred_element_type=F32)
    moment_c = moment_c[:, :count_k] + moment_c[:, count_k:]
    moment_c = moment_c[:rank] + moment_c[rank:]
    moment_c = jnp.concatenate([moment_c, moment_c], axis=0).T
    moment_a = ma_ref[...]

    def result(factor, whole, moment, weight, factor_scale):
        out = (whole - moment) * factor_scale
        return out + factor * weight if weight else out

    a = result(a2_ref[...], model_a, moment_a + turn(moment_a), keep[0], scale[0])
    b = result(b2_ref[...], model_b, moment_b + turn(moment_b), keep[1], scale[1])
    c2_ref[...] = result(c2_ref[...], model_c, moment_c, keep[2], scale[2])
    (pack_first if first else pack_second)(a, b, c2_ref, *outs)


def partials(first, keep, scale, small, tensor, sizes, out_shapes):
    count_i, count_j, count_k = sizes
    width = small[0].shape[-1]
    tall = count_i * count_j
    if first:
        tensor = pltpu.with_memory_space_constraint(tensor, pltpu.HBM)
        out_shapes += ((tall, count_k),)
    return pl.pallas_call(
        functools.partial(round_kernel, first, keep, scale),
        out_shape=tuple(jax.ShapeDtypeStruct(s, F32) for s in out_shapes),
        in_specs=[VMEM] * len(small) + [HBM if first else VMEM],
        out_specs=(VMEM,) * len(out_shapes),
        scratch_shapes=[
            pltpu.VMEM((count_i, width), F32),
            pltpu.VMEM((count_j, width), F32),
            pltpu.VMEM((count_k, width), F32),
            pltpu.VMEM((2 * count_k, width), BF16),
            pltpu.VMEM((count_i, width), F32),
        ]
        + [pltpu.SemaphoreType.DMA((tall // CHUNK,))] * first,
        compiler_params=pltpu.CompilerParams(vmem_limit_bytes=24 << 20),
        cost_estimate=pl.CostEstimate(flops=1 << 30, bytes_accessed=4 << 20, transcendentals=0),
        name="partials",
    )(*small, tensor)


def first_kernel(a_hbm, b_hbm, c_hbm, slots_ref, a_out_ref, a_ref, b_ref, c_ref, sems):
    own, rank = a_ref.shape
    pairs = ((a_hbm, a_ref), (b_hbm, b_ref), (c_hbm, c_ref))
    copies = [pltpu.make_async_copy(x, y, sems.at[n]) for n, (x, y) in enumerate(pairs)]
    for copy in copies:
        copy.start()
    for copy in copies:
        copy.wait()
    a = a_ref[...]
    a_out_ref[...] = jnp.concatenate([a, a], axis=1)
    slot = jnp.concatenate([b_ref[...], jnp.broadcast_to(c_ref[...], (own, rank))], axis=1)
    for n in range(slots_ref.shape[0]):
        slots_ref[n, :, :] = slot


def first_slots(a, b, c, count):
    own, rank = a.shape
    factors = [pltpu.with_memory_space_constraint(x, pltpu.HBM) for x in (a, b, c)]
    return pl.pallas_call(
        first_kernel,
        out_shape=(
            jax.ShapeDtypeStruct((count, own, 2 * rank), F32),
            jax.ShapeDtypeStruct((own, 2 * rank), F32),
        ),
        in_specs=[HBM] * 3,
        out_specs=(VMEM, VMEM),
        scratch_shapes=[pltpu.VMEM(x.shape, F32) for x in (a, b, c)]
        + [pltpu.SemaphoreType.DMA((3,))],
        compiler_params=pltpu.CompilerParams(vmem_limit_bytes=4 << 20),
        name="first_slots",
    )(*factors)


def last_kernel(ac_ref, other_ref, bc_ref, a_ref, b_ref, c_ref, sum_a_ref, sum_b_ref):
    own, rank = a_ref.shape
    sum_a_ref[...] = ac_ref[...] + other_ref[...]
    sum_b_ref[...] = jnp.sum(bc_ref[...], axis=0)
    mine = pl.ds(lax.axis_index("gz") * own, own)
    a_ref[...] = sum_a_ref[mine, :][:, :rank]
    b_ref[...] = sum_b_ref[mine, :][:, :rank]
    c_ref[...] = sum_b_ref[:1, :][:, rank:]


def last_sums(ac, other, bc, own, rank):
    return pl.pallas_call(
        last_kernel,
        out_shape=tuple(jax.ShapeDtypeStruct((n, rank), F32) for n in (own, own, 1)),
        scratch_shapes=[pltpu.VMEM(ac.shape, F32)] * 2,
        compiler_params=pltpu.CompilerParams(vmem_limit_bytes=4 << 20),
        name="last_sums",
    )(ac, other, bc)


def shift(x, axis, stride, count, by):
    pairs = []
    for n in range(lax.axis_size(axis)):
        place = n // stride % count
        pairs.append((n, n + ((place + by) % count - place) * stride))
    return lax.ppermute(x, axis, pairs)


def ring8(x):
    below, above = shift(x, "gx", 1, 8, 1), shift(x, "gx", 1, 8, -1)
    two = x + above
    three = two + below
    return three + (shift(three, "gx", 1, 8, -3) + shift(two, "gx", 1, 8, 3))


def ring4(x, stride):
    ones = shift(x, "gy", stride, 4, 1) + shift(x, "gy", stride, 4, -1)
    return (x + ones) + shift(x, "gy", stride, 4, 2)


def swap(x):
    return lax.ppermute(x, "gz", [(0, 1), (1, 0)])


def shards(tensor, factor_a, factor_b, factor_c):
    count_x, count_y, count_z = (lax.axis_size(n) for n in ("gx", "gy", "gz"))
    core = lax.axis_index("gz")
    count_i, count_j, count_k = tensor.shape
    whole = (
        float(count_j * count_y * count_k * count_z),
        float(count_i * count_x * count_k * count_z),
        float(count_i * count_x * count_j * count_y),
    )
    copies = (count_y * count_z, count_x * count_z, count_x * count_y)
    own, rank = factor_a.shape
    wide = 2 * rank

    slots, mine = first_slots(factor_a, factor_b, factor_c, count_x)
    other = swap(mine)
    along_x = lax.all_to_all(slots, "gx", 0, 0, tiled=True)
    rows_a = jnp.concatenate(
        [jnp.where(core == 0, mine, other), jnp.where(core == 0, other, mine)], axis=0
    )
    slot = jnp.where(lower_half(rows_a.shape), rows_a, along_x[:, 0])
    other_x = swap(along_x)
    along_y = lax.all_to_all(jnp.broadcast_to(slot[None], (count_y, *slot.shape)), "gy", 0, 0, tiled=True)

    keep = tuple(1.0 / n for n in copies)
    scale = tuple(-STEP_SIZE / n for n in whole)
    sizes = tensor.shape
    tensor = tensor.reshape(count_i * count_j, count_k)
    shapes = ((count_i, wide), (count_k, wide))
    a, cb, tensor = partials(True, keep, scale, (along_y, along_x, other_x), tensor, sizes, shapes)
    a = a + swap(a)
    cb = ring8(cb)
    ca = ring4(ring4(jnp.where(lower_half(cb.shape), cb, a), 1), 4)
    b = cb[:count_j]
    b = b + swap(b)

    scale = tuple(1.0 / n for n in whole)
    shapes = ((count_y, 2 * own, wide), (count_j, wide))
    slots_ac, b = partials(False, (0.0,) * 3, scale, (ca, b), tensor, sizes, shapes)
    b = b + swap(b)
    ac = jnp.sum(lax.all_to_all(slots_ac, "gy", 0, 0, tiled=True), axis=0)
    other = swap(ac)
    slots_b = b.reshape(count_x, 2 * own, wide)
    slots_bc = jnp.where(lower_half(slots_b.shape), slots_b, ac[:, None])
    bc = lax.all_to_all(slots_bc, "gx", 0, 0, tiled=True)
    return last_sums(ac, other, bc, own, rank)


def solution(mesh):
    factors = (
        P(("gx", "gy", "gz"), None),
        P(("gy", "gx", "gz"), None),
        P(("gz", "gx", "gy"), None),
    )
    return jax.shard_map(
        shards,
        mesh=mesh,
        in_specs=(P("gx", "gy", "gz"), *factors),
        out_specs=factors,
        check_vma=False,
    )
```

```python
import functools

import jax
import jax.numpy as jnp
from jax import lax
from jax.experimental import pallas as pl
from jax.experimental.pallas import tpu as pltpu
from jax.sharding import PartitionSpec as P

STEPS = 2
STEP_SIZE = 0.1
F32 = jnp.float32
BF16 = jnp.bfloat16
HIGHEST = lax.Precision.HIGHEST
VMEM = pl.BlockSpec(memory_space=pltpu.VMEM)
HBM = pl.BlockSpec(memory_space=pltpu.HBM)
CHUNK = 512


def split(x):
    high = x.astype(BF16)
    return high, (x - high.astype(F32)).astype(BF16)


def lower_half(shape):
    return lax.broadcasted_iota(jnp.int32, shape, len(shape) - 1) < shape[-1] // 2


def turn(x):
    return pltpu.roll(x, x.shape[1] // 2, 1)


def from_lower(x):
    return jnp.where(lower_half(x.shape), x, turn(x))


def from_upper(x):
    return jnp.where(lower_half(x.shape), turn(x), x)


def gram(x):
    return lax.dot_general(
        x, x, (((0,), (0,)), ((), ())), precision=HIGHEST, preferred_element_type=F32
    )


def unpack_first(ac_ref, own_ref, other_ref, a2_ref, b2_ref, c2_ref):
    slots, each, width = ac_ref.shape
    core = lax.axis_index("gz")
    a2_ref[...] = from_lower(ac_ref[...].reshape(slots * each, width))
    for g in range(each):
        c2_ref[g * slots : (g + 1) * slots, :] = ac_ref[:, g, :]
    c2_ref[...] = from_upper(c2_ref[...])
    slots, each, width = own_ref.shape
    for n in range(slots):
        own, other = own_ref[n], other_ref[n]
        at = 2 * each * n
        b2_ref[at : at + each, :] = jnp.where(core == 0, own, other)
        b2_ref[at + each : at + 2 * each, :] = jnp.where(core == 0, other, own)
    b2_ref[...] = from_lower(b2_ref[...])


def unpack_second(ca_ref, b_ref, a2_ref, b2_ref, c2_ref):
    a2_ref[...] = from_upper(ca_ref[...])
    b2_ref[...] = from_upper(b_ref[...])
    c2_ref[...] = from_lower(ca_ref[...])


def pack_first(a, b, c_ref, a_ref, cb_ref):
    count_b = b.shape[0]
    c = c_ref[...]
    a_ref[...] = a
    cb_ref[:count_b, :] = jnp.where(lower_half(b.shape), c[:count_b], b)
    cb_ref[count_b:, :] = jnp.where(lower_half(c[count_b:].shape), c[count_b:], 0.0)


def pack_second(a, b, c_ref, ac_ref, b_ref):
    slots, each, width = ac_ref.shape
    lower = lower_half((each, width))
    for n in range(slots):
        block = c_ref[pl.ds(n, each, stride=slots), :]
        ac_ref[n, :, :] = jnp.where(lower, a[n * each : (n + 1) * each], block)
    b_ref[...] = b


def round_kernel(first, keep, scale, *refs):
    n_small = 3 if first else 2
    small, t_ref, outs, refs = refs[:n_small], refs[n_small], refs[n_small + 1 :][:2], refs[n_small + 3 :]
    if first:
        t_hbm, t_ref, sems, refs = t_ref, refs[0], refs[-1], refs[1:-1]
    a2_ref, b2_ref, c2_ref, wc_ref, ma_ref = refs
    count_i, count_j, count_k = a2_ref.shape[0], b2_ref.shape[0], c2_ref.shape[0]
    width = a2_ref.shape[1]
    rank = width // 2
    chunks = t_ref.shape[0] // CHUNK
    per = CHUNK // count_j

    def fetch(c):
        at = pl.ds(c * CHUNK, CHUNK)
        return pltpu.make_async_copy(t_hbm.at[at, :], t_ref.at[at, :], sems.at[c])

    for c in range(chunks if first else 0):
        fetch(c).start()

    (unpack_first if first else unpack_second)(*small, a2_ref, b2_ref, c2_ref)
    a2, b2, c2 = a2_ref[...], b2_ref[...], c2_ref[...]
    high = c2.astype(BF16).astype(F32)
    both = jnp.where(lower_half(c2.shape), high, c2 - high).astype(BF16)
    wc_ref[:count_k, :] = both
    wc_ref[count_k:, :] = both
    turned_a = a2.T[:rank]
    turned_b = b2.T[:rank]
    turned_b = jnp.concatenate([turned_b] * (128 // count_j), axis=1)
    gram_a, gram_b, gram_c = gram(a2), gram(b2), gram(c2)

    def model(factor, one, two):
        return 0.5 * jnp.dot(factor, one * two, precision=HIGHEST, preferred_element_type=F32)

    model_a = model(a2, gram_b, gram_c)
    model_b = model(b2, gram_a, gram_c)
    model_c = model(c2, gram_a, gram_b)
    group = 128 // count_j
    lane = lax.broadcasted_iota(jnp.int32, (rank, 128), 1) // count_j

    moment_b = jnp.zeros((count_j, width), F32)
    moment_c = jnp.zeros((width, 2 * count_k), F32)
    for c in range(chunks):
        if first and c % (chunks // 2) == 0:
            for n in range(c, c + chunks // 2):
                fetch(n).wait()
        high, low = split(t_ref[c * CHUNK : (c + 1) * CHUNK, :])
        terms = jnp.concatenate([high, low], axis=1)
        y = jnp.dot(terms, wc_ref[...], preferred_element_type=F32)
        y = y.reshape(per, count_j, width)
        at_i = c * per
        ma_ref[at_i : at_i + per, :] = jnp.sum(y * b2_ref[...][None], axis=1)
        for m in range(per):
            moment_b = moment_b + y[m] * a2_ref[at_i + m : at_i + m + 1, :]
        pieces = []
        for m in range(at_i, at_i + per, group):
            columns = jnp.broadcast_to(turned_a[:, m : m + 1], (rank, 128))
            for g in range(1, group):
                other = jnp.broadcast_to(turned_a[:, m + g : m + g + 1], (rank, 128))
                columns = jnp.where(lane == g, other, columns)
            pieces.append(columns * turned_b)
        rows_high, rows_low = split(jnp.concatenate(pieces, axis=1))
        rows = jnp.concatenate([rows_high, rows_low], axis=0)
        moment_c = moment_c + jnp.dot(rows, terms, preferred_element_type=F32)
    moment_c = moment_c[:, :count_k] + moment_c[:, count_k:]
    moment_c = moment_c[:rank] + moment_c[rank:]
    moment_c = jnp.concatenate([moment_c, moment_c], axis=0).T
    moment_a = ma_ref[...]

    def result(factor, whole, moment, weight, factor_scale):
        out = (whole - moment) * factor_scale
        return out + factor * weight if weight else out

    a = result(a2_ref[...], model_a, moment_a + turn(moment_a), keep[0], scale[0])
    b = result(b2_ref[...], model_b, moment_b + turn(moment_b), keep[1], scale[1])
    c2_ref[...] = result(c2_ref[...], model_c, moment_c, keep[2], scale[2])
    (pack_first if first else pack_second)(a, b, c2_ref, *outs)


def partials(first, keep, scale, small, tensor, sizes, out_shapes):
    count_i, count_j, count_k = sizes
    width = small[0].shape[-1]
    tall = count_i * count_j
    if first:
        tensor = pltpu.with_memory_space_constraint(tensor, pltpu.HBM)
        out_shapes += ((tall, count_k),)
    return pl.pallas_call(
        functools.partial(round_kernel, first, keep, scale),
        out_shape=tuple(jax.ShapeDtypeStruct(s, F32) for s in out_shapes),
        in_specs=[VMEM] * len(small) + [HBM if first else VMEM],
        out_specs=(VMEM,) * len(out_shapes),
        scratch_shapes=[
            pltpu.VMEM((count_i, width), F32),
            pltpu.VMEM((count_j, width), F32),
            pltpu.VMEM((count_k, width), F32),
            pltpu.VMEM((2 * count_k, width), BF16),
            pltpu.VMEM((count_i, width), F32),
        ]
        + [pltpu.SemaphoreType.DMA((tall // CHUNK,))] * first,
        compiler_params=pltpu.CompilerParams(vmem_limit_bytes=24 << 20),
        cost_estimate=pl.CostEstimate(flops=1 << 30, bytes_accessed=4 << 20, transcendentals=0),
        name="partials",
    )(*small, tensor)


def first_kernel(a_hbm, b_hbm, c_hbm, slots_ref, a_out_ref, a_ref, b_ref, c_ref, sems):
    own, rank = a_ref.shape
    pairs = ((a_hbm, a_ref), (b_hbm, b_ref), (c_hbm, c_ref))
    copies = [pltpu.make_async_copy(x, y, sems.at[n]) for n, (x, y) in enumerate(pairs)]
    for copy in copies:
        copy.start()
    for copy in copies:
        copy.wait()
    a = a_ref[...]
    a_out_ref[...] = jnp.concatenate([a, a], axis=1)
    slot = jnp.concatenate([b_ref[...], jnp.broadcast_to(c_ref[...], (own, rank))], axis=1)
    for n in range(slots_ref.shape[0]):
        slots_ref[n, :, :] = slot


def first_slots(a, b, c, count):
    own, rank = a.shape
    factors = [pltpu.with_memory_space_constraint(x, pltpu.HBM) for x in (a, b, c)]
    return pl.pallas_call(
        first_kernel,
        out_shape=(
            jax.ShapeDtypeStruct((count, own, 2 * rank), F32),
            jax.ShapeDtypeStruct((own, 2 * rank), F32),
        ),
        in_specs=[HBM] * 3,
        out_specs=(VMEM, VMEM),
        scratch_shapes=[pltpu.VMEM(x.shape, F32) for x in (a, b, c)]
        + [pltpu.SemaphoreType.DMA((3,))],
        compiler_params=pltpu.CompilerParams(vmem_limit_bytes=4 << 20),
        name="first_slots",
    )(*factors)


def last_kernel(ac_ref, other_ref, bc_ref, a_ref, b_ref, c_ref, sum_a_ref, sum_b_ref):
    own, rank = a_ref.shape
    sum_a_ref[...] = ac_ref[...] + other_ref[other_ref.shape[0] - ac_ref.shape[0] :, :]
    sum_b_ref[...] = jnp.sum(bc_ref[...], axis=0)
    mine = pl.ds(lax.axis_index("gz") * own, own)
    a_ref[...] = sum_a_ref[mine, :][:, :rank]
    b_ref[...] = sum_b_ref[mine, :][:, :rank]
    c_ref[...] = sum_b_ref[:1, :][:, rank:]


def last_sums(ac, other, bc, own, rank):
    return pl.pallas_call(
        last_kernel,
        out_shape=tuple(jax.ShapeDtypeStruct((n, rank), F32) for n in (own, own, 1)),
        scratch_shapes=[pltpu.VMEM(ac.shape, F32)] * 2,
        compiler_params=pltpu.CompilerParams(vmem_limit_bytes=4 << 20),
        name="last_sums",
    )(ac, other, bc)


def shift(x, axis, stride, count, by):
    pairs = []
    for n in range(lax.axis_size(axis)):
        place = n // stride % count
        pairs.append((n, n + ((place + by) % count - place) * stride))
    return lax.ppermute(x, axis, pairs)


def ring8(x):
    below, above = shift(x, "gx", 1, 8, 1), shift(x, "gx", 1, 8, -1)
    two = x + above
    three = two + below
    return three + (shift(three, "gx", 1, 8, -3) + shift(two, "gx", 1, 8, 3))


def ring4(x, stride):
    ones = shift(x, "gy", stride, 4, 1) + shift(x, "gy", stride, 4, -1)
    return (x + ones) + shift(x, "gy", stride, 4, 2)


def swap(x):
    return lax.ppermute(x, "gz", [(0, 1), (1, 0)])


def shards(tensor, factor_a, factor_b, factor_c):
    count_x, count_y, count_z = (lax.axis_size(n) for n in ("gx", "gy", "gz"))
    core = lax.axis_index("gz")
    count_i, count_j, count_k = tensor.shape
    whole = (
        float(count_j * count_y * count_k * count_z),
        float(count_i * count_x * count_k * count_z),
        float(count_i * count_x * count_j * count_y),
    )
    copies = (count_y * count_z, count_x * count_z, count_x * count_y)
    own, rank = factor_a.shape
    wide = 2 * rank

    slots, mine = first_slots(factor_a, factor_b, factor_c, count_x)
    along_x = lax.all_to_all(slots, "gx", 0, 0, tiled=True)
    others = swap(jnp.concatenate([along_x, mine[None]], axis=0))
    other = others[-1]
    rows_a = jnp.concatenate(
        [jnp.where(core == 0, mine, other), jnp.where(core == 0, other, mine)], axis=0
    )
    slot = jnp.where(lower_half(rows_a.shape), rows_a, along_x[:, 0])
    along_y = lax.all_to_all(jnp.broadcast_to(slot[None], (count_y, *slot.shape)), "gy", 0, 0, tiled=True)

    keep = tuple(1.0 / n for n in copies)
    scale = tuple(-STEP_SIZE / n for n in whole)
    sizes = tensor.shape
    tensor = tensor.reshape(count_i * count_j, count_k)
    shapes = ((count_i, wide), (count_k, wide))
    a, cb, tensor = partials(True, keep, scale, (along_y, along_x, others), tensor, sizes, shapes)
    a = a + swap(a)
    cb = ring8(cb)
    ca = ring4(ring4(jnp.where(lower_half(cb.shape), cb, a), 1), 4)
    b = cb[:count_j]
    b = b + swap(b)

    scale = tuple(1.0 / n for n in whole)
    shapes = ((count_y, 2 * own, wide), (count_j, wide))
    slots_ac, b = partials(False, (0.0,) * 3, scale, (ca, b), tensor, sizes, shapes)
    ac = jnp.sum(lax.all_to_all(slots_ac, "gy", 0, 0, tiled=True), axis=0)
    others = swap(jnp.concatenate([b, ac], axis=0))
    b = b + others[:count_j]
    slots_b = b.reshape(count_x, 2 * own, wide)
    slots_bc = jnp.where(lower_half(slots_b.shape), slots_b, ac[:, None])
    bc = lax.all_to_all(slots_bc, "gx", 0, 0, tiled=True)
    return last_sums(ac, others, bc, own, rank)


def solution(mesh):
    factors = (
        P(("gx", "gy", "gz"), None),
        P(("gy", "gx", "gz"), None),
        P(("gz", "gx", "gy"), None),
    )
    return jax.shard_map(
        shards,
        mesh=mesh,
        in_specs=(P("gx", "gy", "gz"), *factors),
        out_specs=factors,
        check_vma=False,
    )
```

```python
import functools

import jax
import jax.numpy as jnp
from jax import lax
from jax.experimental import pallas as pl
from jax.experimental.pallas import tpu as pltpu
from jax.sharding import PartitionSpec as P

STEPS = 2
STEP_SIZE = 0.1
F32 = jnp.float32
BF16 = jnp.bfloat16
HIGHEST = lax.Precision.HIGHEST
VMEM = pl.BlockSpec(memory_space=pltpu.VMEM)
HBM = pl.BlockSpec(memory_space=pltpu.HBM)
CHUNK = 512
OWN = 4


def split(x):
    high = x.astype(BF16)
    return high, (x - high.astype(F32)).astype(BF16)


def lower_half(shape):
    return lax.broadcasted_iota(jnp.int32, shape, len(shape) - 1) < shape[-1] // 2


def turn(x):
    return pltpu.roll(x, x.shape[1] // 2, 1)


def from_lower(x):
    return jnp.where(lower_half(x.shape), x, turn(x))


def from_upper(x):
    return jnp.where(lower_half(x.shape), turn(x), x)


def gram(x):
    return lax.dot_general(
        x, x, (((0,), (0,)), ((), ())), precision=HIGHEST, preferred_element_type=F32
    )


def unpack_first(all_ref, own_ref, other_ref, a2_ref, b2_ref, c2_ref):
    core = lax.axis_index("gz")
    slots, tall, width = all_ref.shape
    each = tall // 2
    for ref in (a2_ref, b2_ref):
        for n in range(ref.shape[0] // tall):
            own, other = (x[n * each : (n + 1) * each, :] for x in (own_ref, other_ref))
            ref[n * tall : n * tall + each, :] = jnp.where(core == 0, own, other)
            ref[n * tall + each : (n + 1) * tall, :] = jnp.where(core == 0, other, own)
    a2_ref[...] = from_lower(a2_ref[...])
    b2_ref[...] = from_upper(b2_ref[...])
    c2_ref[...] = all_ref.reshape(slots * tall, width)[pl.ds(each, slots, stride=tall), :]


def unpack_second(ca_ref, b_ref, a2_ref, b2_ref, c2_ref):
    a2_ref[...] = from_upper(ca_ref[...])
    b2_ref[...] = from_upper(b_ref[...])
    c2_ref[...] = from_lower(ca_ref[...])


def pack_first(a, b, c_ref, a_ref, cb_ref):
    count_b = b.shape[0]
    c = c_ref[...]
    a_ref[...] = a
    cb_ref[:count_b, :] = jnp.where(lower_half(b.shape), c[:count_b], b)
    cb_ref[count_b:, :] = jnp.where(lower_half(c[count_b:].shape), c[count_b:], 0.0)


def pack_second(a, b, c_ref, keep_ref, give_ref, out_c_ref):
    core = lax.axis_index("gz")
    out_c_ref[...] = c_ref[...]
    each = OWN
    for n in range(a.shape[0] // (2 * each)):
        rows = slice(2 * each * n, 2 * each * (n + 1))
        both = a[rows]
        if n < b.shape[0] // (2 * each):
            both = jnp.where(lower_half(both.shape), both, b[rows])
        low, high = both[:each], both[each:]
        keep_ref[n * each : (n + 1) * each, :] = jnp.where(core == 0, low, high)
        give_ref[n * each : (n + 1) * each, :] = jnp.where(core == 0, high, low)


def round_kernel(first, keep, scale, *refs):
    n_small, n_out = (3, 2) if first else (2, 3)
    small, t_ref, refs = refs[:n_small], refs[n_small], refs[n_small + 1 :]
    outs, refs = refs[:n_out], refs[n_out:]
    if first:
        t_hbm, t_ref, sems, refs = t_ref, refs[0], refs[-1], refs[1:-1]
    a2_ref, b2_ref, c2_ref, wc_ref, ma_ref = refs
    count_i, count_j, count_k = a2_ref.shape[0], b2_ref.shape[0], c2_ref.shape[0]
    width = a2_ref.shape[1]
    rank = width // 2
    chunks = t_ref.shape[0] // CHUNK
    per = CHUNK // count_j

    def fetch(c):
        at = pl.ds(c * CHUNK, CHUNK)
        return pltpu.make_async_copy(t_hbm.at[at, :], t_ref.at[at, :], sems.at[c])

    for c in range(chunks if first else 0):
        fetch(c).start()

    (unpack_first if first else unpack_second)(*small, a2_ref, b2_ref, c2_ref)
    a2, b2, c2 = a2_ref[...], b2_ref[...], c2_ref[...]
    high = c2.astype(BF16).astype(F32)
    both = jnp.where(lower_half(c2.shape), high, c2 - high).astype(BF16)
    wc_ref[:count_k, :] = both
    wc_ref[count_k:, :] = both
    turned_a = a2.T[:rank]
    turned_b = b2.T[:rank]
    turned_b = jnp.concatenate([turned_b] * (128 // count_j), axis=1)
    gram_a, gram_b, gram_c = gram(a2), gram(b2), gram(c2)

    def model(factor, one, two):
        return 0.5 * jnp.dot(factor, one * two, precision=HIGHEST, preferred_element_type=F32)

    model_a = model(a2, gram_b, gram_c)
    model_b = model(b2, gram_a, gram_c)
    model_c = model(c2, gram_a, gram_b)
    group = 128 // count_j
    lane = lax.broadcasted_iota(jnp.int32, (rank, 128), 1) // count_j

    moment_b = jnp.zeros((count_j, width), F32)
    moment_c = jnp.zeros((width, 2 * count_k), F32)
    for c in range(chunks):
        if first and c % (chunks // 2) == 0:
            for n in range(c, c + chunks // 2):
                fetch(n).wait()
        high, low = split(t_ref[c * CHUNK : (c + 1) * CHUNK, :])
        terms = jnp.concatenate([high, low], axis=1)
        y = jnp.dot(terms, wc_ref[...], preferred_element_type=F32)
        y = y.reshape(per, count_j, width)
        at_i = c * per
        ma_ref[at_i : at_i + per, :] = jnp.sum(y * b2_ref[...][None], axis=1)
        for m in range(per):
            moment_b = moment_b + y[m] * a2_ref[at_i + m : at_i + m + 1, :]
        pieces = []
        for m in range(at_i, at_i + per, group):
            columns = jnp.broadcast_to(turned_a[:, m : m + 1], (rank, 128))
            for g in range(1, group):
                other = jnp.broadcast_to(turned_a[:, m + g : m + g + 1], (rank, 128))
                columns = jnp.where(lane == g, other, columns)
            pieces.append(columns * turned_b)
        rows_high, rows_low = split(jnp.concatenate(pieces, axis=1))
        rows = jnp.concatenate([rows_high, rows_low], axis=0)
        moment_c = moment_c + jnp.dot(rows, terms, preferred_element_type=F32)
    moment_c = moment_c[:, :count_k] + moment_c[:, count_k:]
    moment_c = moment_c[:rank] + moment_c[rank:]
    moment_c = jnp.concatenate([moment_c, moment_c], axis=0).T
    moment_a = ma_ref[...]

    def result(factor, whole, moment, weight, factor_scale):
        out = (whole - moment) * factor_scale
        return out + factor * weight if weight else out

    a = result(a2_ref[...], model_a, moment_a + turn(moment_a), keep[0], scale[0])
    b = result(b2_ref[...], model_b, moment_b + turn(moment_b), keep[1], scale[1])
    c2_ref[...] = result(c2_ref[...], model_c, moment_c, keep[2], scale[2])
    (pack_first if first else pack_second)(a, b, c2_ref, *outs)


def partials(first, keep, scale, small, tensor, sizes, out_shapes):
    count_i, count_j, count_k = sizes
    width = small[0].shape[-1]
    tall = count_i * count_j
    if first:
        tensor = pltpu.with_memory_space_constraint(tensor, pltpu.HBM)
        out_shapes += ((tall, count_k),)
    return pl.pallas_call(
        functools.partial(round_kernel, first, keep, scale),
        out_shape=tuple(jax.ShapeDtypeStruct(s, F32) for s in out_shapes),
        in_specs=[VMEM] * len(small) + [HBM if first else VMEM],
        out_specs=(VMEM,) * len(out_shapes),
        scratch_shapes=[
            pltpu.VMEM((count_i, width), F32),
            pltpu.VMEM((count_j, width), F32),
            pltpu.VMEM((count_k, width), F32),
            pltpu.VMEM((2 * count_k, width), BF16),
            pltpu.VMEM((count_i, width), F32),
        ]
        + [pltpu.SemaphoreType.DMA((tall // CHUNK,))] * first,
        compiler_params=pltpu.CompilerParams(vmem_limit_bytes=24 << 20),
        cost_estimate=pl.CostEstimate(flops=1 << 30, bytes_accessed=4 << 20, transcendentals=0),
        name="partials",
    )(*small, tensor)


def first_kernel(a_hbm, b_hbm, c_hbm, slots_ref, a_ref, b_ref, c_ref, sems):
    own, rank = a_ref.shape
    pairs = ((a_hbm, a_ref), (b_hbm, b_ref), (c_hbm, c_ref))
    copies = [pltpu.make_async_copy(x, y, sems.at[n]) for n, (x, y) in enumerate(pairs)]
    for copy in copies:
        copy.start()
    for copy in copies:
        copy.wait()
    rows = jnp.concatenate([a_ref[...], b_ref[...]], axis=1)
    c = jnp.broadcast_to(c_ref[...], (own, rank))
    slot = jnp.concatenate([rows, jnp.concatenate([c, c], axis=1)], axis=0)
    for n in range(slots_ref.shape[0]):
        slots_ref[n, :, :] = slot


def first_slots(a, b, c, count):
    own, rank = a.shape
    factors = [pltpu.with_memory_space_constraint(x, pltpu.HBM) for x in (a, b, c)]
    return pl.pallas_call(
        first_kernel,
        out_shape=jax.ShapeDtypeStruct((count, 2 * own, 2 * rank), F32),
        in_specs=[HBM] * 3,
        out_specs=VMEM,
        scratch_shapes=[pltpu.VMEM(x.shape, F32) for x in (a, b, c)]
        + [pltpu.SemaphoreType.DMA((3,))],
        compiler_params=pltpu.CompilerParams(vmem_limit_bytes=4 << 20),
        name="first_slots",
    )(*factors)


def pick_kernel(count_x, count_y, all_ref, out_ref):
    me_x, me_y = lax.axis_index("gx"), lax.axis_index("gy")
    own = out_ref.shape[0] // count_y
    for n in range(count_y):
        rows = all_ref[me_x * count_y + n, :own, :]
        if n < count_x:
            rows = jnp.where(lower_half(rows.shape), rows, all_ref[n * count_y + me_y, :own, :])
        out_ref[n * own : (n + 1) * own, :] = rows


def pick(received, count_x, count_y):
    _, tall, width = received.shape
    return pl.pallas_call(
        functools.partial(pick_kernel, count_x, count_y),
        out_shape=jax.ShapeDtypeStruct((count_y * tall // 2, width), F32),
        in_specs=[VMEM],
        out_specs=VMEM,
        compiler_params=pltpu.CompilerParams(vmem_limit_bytes=4 << 20),
        name="pick",
    )(received)


def build_kernel(count_x, count_y, keep_ref, other_ref, c_ref, slots_ref):
    own = keep_ref.shape[0] // count_y
    rows = keep_ref[...] + other_ref[...]
    rows = [rows[n * own : (n + 1) * own] for n in range(count_y)]
    lower = lower_half(rows[0].shape)
    for x in range(count_x):
        for y in range(count_y):
            n = x * count_y + y
            slots_ref[n, :own, :] = jnp.where(lower, rows[y], rows[x])
            slots_ref[n, own:, :] = jnp.broadcast_to(c_ref[n : n + 1, :], rows[0].shape)


def build(keep, other, c, count_x, count_y):
    own = keep.shape[0] // count_y
    return pl.pallas_call(
        functools.partial(build_kernel, count_x, count_y),
        out_shape=jax.ShapeDtypeStruct((count_x * count_y, 2 * own, keep.shape[1]), F32),
        in_specs=[VMEM] * 3,
        out_specs=VMEM,
        compiler_params=pltpu.CompilerParams(vmem_limit_bytes=4 << 20),
        name="build",
    )(keep, other, c)


def last_kernel(count_x, count_y, all_ref, a_ref, b_ref, c_ref):
    me_x, me_y = lax.axis_index("gx"), lax.axis_index("gy")
    own, rank = a_ref.shape
    slots, tall, width = all_ref.shape
    a = sum(all_ref[me_x * count_y + n, :own, :] for n in range(count_y))
    b = sum(all_ref[n * count_y + me_y, :own, :] for n in range(count_x))
    c = all_ref.reshape(slots * tall, width)[pl.ds(own, slots, stride=tall), :]
    a_ref[...] = a[:, :rank]
    b_ref[...] = b[:, rank:]
    c_ref[...] = jnp.sum(c, axis=0, keepdims=True)[:, :rank]


def last_sums(received, count_x, count_y, own, rank):
    return pl.pallas_call(
        functools.partial(last_kernel, count_x, count_y),
        out_shape=tuple(jax.ShapeDtypeStruct((n, rank), F32) for n in (own, own, 1)),
        compiler_params=pltpu.CompilerParams(vmem_limit_bytes=4 << 20),
        name="last_sums",
    )(received)


def shift(x, axis, stride, count, by):
    pairs = []
    for n in range(lax.axis_size(axis)):
        place = n // stride % count
        pairs.append((n, n + ((place + by) % count - place) * stride))
    return lax.ppermute(x, axis, pairs)


def ring8(x):
    below, above = shift(x, "gx", 1, 8, 1), shift(x, "gx", 1, 8, -1)
    two = x + above
    three = two + below
    return three + (shift(three, "gx", 1, 8, -3) + shift(two, "gx", 1, 8, 3))


def ring4(x, stride):
    ones = shift(x, "gy", stride, 4, 1) + shift(x, "gy", stride, 4, -1)
    return (x + ones) + shift(x, "gy", stride, 4, 2)


def swap(x):
    return lax.ppermute(x, "gz", [(0, 1), (1, 0)])


def shards(tensor, factor_a, factor_b, factor_c):
    count_x, count_y, count_z = (lax.axis_size(n) for n in ("gx", "gy", "gz"))
    count_i, count_j, count_k = tensor.shape
    whole = (
        float(count_j * count_y * count_k * count_z),
        float(count_i * count_x * count_k * count_z),
        float(count_i * count_x * count_j * count_y),
    )
    copies = (count_y * count_z, count_x * count_z, count_x * count_y)
    own, rank = factor_a.shape
    wide = 2 * rank

    slots = first_slots(factor_a, factor_b, factor_c, count_x * count_y)
    received = lax.all_to_all(slots, ("gx", "gy"), 0, 0, tiled=True)
    rows = pick(received, count_x, count_y)
    small = (received, rows, swap(rows))

    keep = tuple(1.0 / n for n in copies)
    scale = tuple(-STEP_SIZE / n for n in whole)
    sizes = tensor.shape
    tensor = tensor.reshape(count_i * count_j, count_k)
    shapes = ((count_i, wide), (count_k, wide))
    a, cb, tensor = partials(True, keep, scale, small, tensor, sizes, shapes)
    a = a + swap(a)
    cb = ring8(cb)
    ca = ring4(ring4(jnp.where(lower_half(cb.shape), cb, a), 1), 4)
    b = cb[:count_j]
    b = b + swap(b)

    scale = tuple(1.0 / n for n in whole)
    shapes = ((count_y * own, wide), (count_y * own, wide), (count_k, wide))
    rows, other, c = partials(False, (0.0,) * 3, scale, (ca, b), tensor, sizes, shapes)
    slots = build(rows, swap(other), c, count_x, count_y)
    received = lax.all_to_all(slots, ("gx", "gy"), 0, 0, tiled=True)
    return last_sums(received, count_x, count_y, own, rank)


def solution(mesh):
    factors = (
        P(("gx", "gy", "gz"), None),
        P(("gy", "gx", "gz"), None),
        P(("gz", "gx", "gy"), None),
    )
    return jax.shard_map(
        shards,
        mesh=mesh,
        in_specs=(P("gx", "gy", "gz"), *factors),
        out_specs=factors,
        check_vma=False,
    )
```

```python
import functools

import jax
import jax.numpy as jnp
from jax import lax
from jax.experimental import pallas as pl
from jax.experimental.pallas import tpu as pltpu
from jax.sharding import PartitionSpec as P

STEPS = 2
STEP_SIZE = 0.1
F32 = jnp.float32
BF16 = jnp.bfloat16
HIGHEST = lax.Precision.HIGHEST
VMEM = pl.BlockSpec(memory_space=pltpu.VMEM)
HBM = pl.BlockSpec(memory_space=pltpu.HBM)
CHUNK = 512


def split(x):
    high = x.astype(BF16)
    return high, (x - high.astype(F32)).astype(BF16)


def lower_half(shape):
    return lax.broadcasted_iota(jnp.int32, shape, len(shape) - 1) < shape[-1] // 2


def turn(x):
    return pltpu.roll(x, x.shape[1] // 2, 1)


def from_lower(x):
    return jnp.where(lower_half(x.shape), x, turn(x))


def from_upper(x):
    return jnp.where(lower_half(x.shape), turn(x), x)


def gram(x):
    return lax.dot_general(
        x, x, (((0,), (0,)), ((), ())), precision=HIGHEST, preferred_element_type=F32
    )


def unpack_first(ac_ref, own_ref, other_ref, a2_ref, b2_ref, c2_ref):
    slots, each, width = ac_ref.shape
    core = lax.axis_index("gz")
    a2_ref[...] = from_lower(ac_ref[...].reshape(slots * each, width))
    for g in range(each):
        c2_ref[g * slots : (g + 1) * slots, :] = ac_ref[:, g, :]
    c2_ref[...] = from_upper(c2_ref[...])
    slots, each, width = own_ref.shape
    for n in range(slots):
        own, other = own_ref[n], other_ref[n]
        at = 2 * each * n
        b2_ref[at : at + each, :] = jnp.where(core == 0, own, other)
        b2_ref[at + each : at + 2 * each, :] = jnp.where(core == 0, other, own)
    b2_ref[...] = from_lower(b2_ref[...])


def unpack_second(ca_ref, b_ref, a2_ref, b2_ref, c2_ref):
    a2_ref[...] = from_upper(ca_ref[...])
    b2_ref[...] = from_upper(b_ref[...])
    c2_ref[...] = from_lower(ca_ref[...])


def pack_first(a, b, c_ref, a_ref, cb_ref):
    count_b = b.shape[0]
    c = c_ref[...]
    a_ref[...] = a
    cb_ref[:count_b, :] = jnp.where(lower_half(b.shape), c[:count_b], b)
    cb_ref[count_b:, :] = jnp.where(lower_half(c[count_b:].shape), c[count_b:], 0.0)


def pack_second(a, b, c_ref, ac_ref, b_ref):
    core = lax.axis_index("gz")
    slots, each, width = ac_ref.shape
    own, apart = a.shape[0] // slots, c_ref.shape[0] // each
    lower = lower_half((own, width))
    for n in range(slots):
        block = c_ref[pl.ds(n // 2, each, stride=apart), :]
        block = jnp.where(core == n % 2, block, 0.0)
        ac_ref[n, :own, :] = jnp.where(lower, a[n * own : (n + 1) * own], block[:own])
        ac_ref[n, own:, :] = block[own:]
    b_ref[...] = b


def round_kernel(first, keep, scale, *refs):
    n_small = 3 if first else 2
    small, t_ref, outs, refs = refs[:n_small], refs[n_small], refs[n_small + 1 :][:2], refs[n_small + 3 :]
    if first:
        t_hbm, t_ref, sems, refs = t_ref, refs[0], refs[-1], refs[1:-1]
    a2_ref, b2_ref, c2_ref, wc_ref, ma_ref = refs
    count_i, count_j, count_k = a2_ref.shape[0], b2_ref.shape[0], c2_ref.shape[0]
    width = a2_ref.shape[1]
    rank = width // 2
    chunks = t_ref.shape[0] // CHUNK
    per = CHUNK // count_j

    def fetch(c):
        at = pl.ds(c * CHUNK, CHUNK)
        return pltpu.make_async_copy(t_hbm.at[at, :], t_ref.at[at, :], sems.at[c])

    for c in range(chunks if first else 0):
        fetch(c).start()

    (unpack_first if first else unpack_second)(*small, a2_ref, b2_ref, c2_ref)
    a2, b2, c2 = a2_ref[...], b2_ref[...], c2_ref[...]
    high = c2.astype(BF16).astype(F32)
    both = jnp.where(lower_half(c2.shape), high, c2 - high).astype(BF16)
    wc_ref[:count_k, :] = both
    wc_ref[count_k:, :] = both
    turned_a = a2.T[:rank]
    turned_b = b2.T[:rank]
    turned_b = jnp.concatenate([turned_b] * (128 // count_j), axis=1)
    gram_a, gram_b, gram_c = gram(a2), gram(b2), gram(c2)

    def model(factor, one, two):
        return 0.5 * jnp.dot(factor, one * two, precision=HIGHEST, preferred_element_type=F32)

    model_a = model(a2, gram_b, gram_c)
    model_b = model(b2, gram_a, gram_c)
    model_c = model(c2, gram_a, gram_b)
    group = 128 // count_j
    lane = lax.broadcasted_iota(jnp.int32, (rank, 128), 1) // count_j

    moment_b = jnp.zeros((count_j, width), F32)
    moment_c = jnp.zeros((width, 2 * count_k), F32)
    for c in range(chunks):
        if first and c % (chunks // 2) == 0:
            for n in range(c, c + chunks // 2):
                fetch(n).wait()
        high, low = split(t_ref[c * CHUNK : (c + 1) * CHUNK, :])
        terms = jnp.concatenate([high, low], axis=1)
        y = jnp.dot(terms, wc_ref[...], preferred_element_type=F32)
        y = y.reshape(per, count_j, width)
        at_i = c * per
        ma_ref[at_i : at_i + per, :] = jnp.sum(y * b2_ref[...][None], axis=1)
        for m in range(per):
            moment_b = moment_b + y[m] * a2_ref[at_i + m : at_i + m + 1, :]
        pieces = []
        for m in range(at_i, at_i + per, group):
            columns = jnp.broadcast_to(turned_a[:, m : m + 1], (rank, 128))
            for g in range(1, group):
                other = jnp.broadcast_to(turned_a[:, m + g : m + g + 1], (rank, 128))
                columns = jnp.where(lane == g, other, columns)
            pieces.append(columns * turned_b)
        rows_high, rows_low = split(jnp.concatenate(pieces, axis=1))
        rows = jnp.concatenate([rows_high, rows_low], axis=0)
        moment_c = moment_c + jnp.dot(rows, terms, preferred_element_type=F32)
    moment_c = moment_c[:, :count_k] + moment_c[:, count_k:]
    moment_c = moment_c[:rank] + moment_c[rank:]
    moment_c = jnp.concatenate([moment_c, moment_c], axis=0).T
    moment_a = ma_ref[...]

    def result(factor, whole, moment, weight, factor_scale):
        out = (whole - moment) * factor_scale
        return out + factor * weight if weight else out

    a = result(a2_ref[...], model_a, moment_a + turn(moment_a), keep[0], scale[0])
    b = result(b2_ref[...], model_b, moment_b + turn(moment_b), keep[1], scale[1])
    c2_ref[...] = result(c2_ref[...], model_c, moment_c, keep[2], scale[2])
    (pack_first if first else pack_second)(a, b, c2_ref, *outs)


def partials(first, keep, scale, small, tensor, sizes, out_shapes):
    count_i, count_j, count_k = sizes
    width = small[0].shape[-1]
    tall = count_i * count_j
    if first:
        tensor = pltpu.with_memory_space_constraint(tensor, pltpu.HBM)
        out_shapes += ((tall, count_k),)
    return pl.pallas_call(
        functools.partial(round_kernel, first, keep, scale),
        out_shape=tuple(jax.ShapeDtypeStruct(s, F32) for s in out_shapes),
        in_specs=[VMEM] * len(small) + [HBM if first else VMEM],
        out_specs=(VMEM,) * len(out_shapes),
        scratch_shapes=[
            pltpu.VMEM((count_i, width), F32),
            pltpu.VMEM((count_j, width), F32),
            pltpu.VMEM((count_k, width), F32),
            pltpu.VMEM((2 * count_k, width), BF16),
            pltpu.VMEM((count_i, width), F32),
        ]
        + [pltpu.SemaphoreType.DMA((tall // CHUNK,))] * first,
        compiler_params=pltpu.CompilerParams(vmem_limit_bytes=24 << 20),
        cost_estimate=pl.CostEstimate(flops=1 << 30, bytes_accessed=4 << 20, transcendentals=0),
        name="partials",
    )(*small, tensor)


def first_kernel(a_hbm, b_hbm, c_hbm, slots_ref, a_out_ref, a_ref, b_ref, c_ref, sems):
    own, rank = a_ref.shape
    pairs = ((a_hbm, a_ref), (b_hbm, b_ref), (c_hbm, c_ref))
    copies = [pltpu.make_async_copy(x, y, sems.at[n]) for n, (x, y) in enumerate(pairs)]
    for copy in copies:
        copy.start()
    for copy in copies:
        copy.wait()
    a = a_ref[...]
    a_out_ref[...] = jnp.concatenate([a, a], axis=1)
    slot = jnp.concatenate([b_ref[...], jnp.broadcast_to(c_ref[...], (own, rank))], axis=1)
    for n in range(slots_ref.shape[0]):
        slots_ref[n, :, :] = slot


def first_slots(a, b, c, count):
    own, rank = a.shape
    factors = [pltpu.with_memory_space_constraint(x, pltpu.HBM) for x in (a, b, c)]
    return pl.pallas_call(
        first_kernel,
        out_shape=(
            jax.ShapeDtypeStruct((count, own, 2 * rank), F32),
            jax.ShapeDtypeStruct((own, 2 * rank), F32),
        ),
        in_specs=[HBM] * 3,
        out_specs=(VMEM, VMEM),
        scratch_shapes=[pltpu.VMEM(x.shape, F32) for x in (a, b, c)]
        + [pltpu.SemaphoreType.DMA((3,))],
        compiler_params=pltpu.CompilerParams(vmem_limit_bytes=4 << 20),
        name="first_slots",
    )(*factors)


def middle_kernel(received_ref, b_ref, ac_ref, slots_ref):
    core = lax.axis_index("gz")
    slots, own, width = slots_ref.shape
    ac_ref[...] = jnp.sum(received_ref[...], axis=0)
    lower = lower_half((own, width))
    for n in range(slots):
        c = jnp.broadcast_to(ac_ref[n // 2 : n // 2 + 1, :], (own, width))
        c = jnp.where(core == n % 2, c, 0.0)
        slots_ref[n, :, :] = jnp.where(lower, b_ref[n * own : (n + 1) * own, :], c)


def middle(received, b, own):
    _, each, width = received.shape
    return pl.pallas_call(
        middle_kernel,
        out_shape=(
            jax.ShapeDtypeStruct((each, width), F32),
            jax.ShapeDtypeStruct((b.shape[0] // own, own, width), F32),
        ),
        in_specs=[VMEM] * 2,
        out_specs=(VMEM,) * 2,
        compiler_params=pltpu.CompilerParams(vmem_limit_bytes=4 << 20),
        name="middle",
    )(received, b)


def last_kernel(ac_ref, bc_ref, a_ref, b_ref, c_ref):
    own, rank = a_ref.shape
    bc = jnp.sum(bc_ref[...], axis=0)
    a_ref[...] = ac_ref[:own, :][:, :rank]
    b_ref[...] = bc[:, :rank]
    c_ref[...] = bc[:1, rank:]


def last_sums(ac, bc, own, rank):
    return pl.pallas_call(
        last_kernel,
        out_shape=tuple(jax.ShapeDtypeStruct((n, rank), F32) for n in (own, own, 1)),
        compiler_params=pltpu.CompilerParams(vmem_limit_bytes=4 << 20),
        name="last_sums",
    )(ac, bc)


def shift(x, axis, stride, count, by):
    pairs = []
    for n in range(lax.axis_size(axis)):
        place = n // stride % count
        pairs.append((n, n + ((place + by) % count - place) * stride))
    return lax.ppermute(x, axis, pairs)


def ring8(x):
    below, above = shift(x, "gx", 1, 8, 1), shift(x, "gx", 1, 8, -1)
    two = x + above
    three = two + below
    return three + (shift(three, "gx", 1, 8, -3) + shift(two, "gx", 1, 8, 3))


def ring4(x, stride):
    ones = shift(x, "gy", stride, 4, 1) + shift(x, "gy", stride, 4, -1)
    return (x + ones) + shift(x, "gy", stride, 4, 2)


def swap(x):
    return lax.ppermute(x, "gz", [(0, 1), (1, 0)])


def shards(tensor, factor_a, factor_b, factor_c):
    count_x, count_y, count_z = (lax.axis_size(n) for n in ("gx", "gy", "gz"))
    core = lax.axis_index("gz")
    count_i, count_j, count_k = tensor.shape
    whole = (
        float(count_j * count_y * count_k * count_z),
        float(count_i * count_x * count_k * count_z),
        float(count_i * count_x * count_j * count_y),
    )
    copies = (count_y * count_z, count_x * count_z, count_x * count_y)
    own, rank = factor_a.shape
    wide = 2 * rank

    slots, mine = first_slots(factor_a, factor_b, factor_c, count_x)
    along_x = lax.all_to_all(slots, "gx", 0, 0, tiled=True)
    others = swap(jnp.concatenate([along_x, mine[None]], axis=0))
    other = others[-1]
    rows_a = jnp.concatenate(
        [jnp.where(core == 0, mine, other), jnp.where(core == 0, other, mine)], axis=0
    )
    slot = jnp.where(lower_half(rows_a.shape), rows_a, along_x[:, 0])
    along_y = lax.all_to_all(jnp.broadcast_to(slot[None], (count_y, *slot.shape)), "gy", 0, 0, tiled=True)

    keep = tuple(1.0 / n for n in copies)
    scale = tuple(-STEP_SIZE / n for n in whole)
    sizes = tensor.shape
    tensor = tensor.reshape(count_i * count_j, count_k)
    shapes = ((count_i, wide), (count_k, wide))
    a, cb, tensor = partials(True, keep, scale, (along_y, along_x, others), tensor, sizes, shapes)
    a = a + swap(a)
    cb = ring8(cb)
    ca = ring4(ring4(jnp.where(lower_half(cb.shape), cb, a), 1), 4)
    b = cb[:count_j]
    b = b + swap(b)

    scale = tuple(1.0 / n for n in whole)
    shapes = ((count_y * count_z, count_x, wide), (count_j, wide))
    slots, b = partials(False, (0.0,) * 3, scale, (ca, b), tensor, sizes, shapes)
    received = lax.all_to_all(slots, ("gy", "gz"), 0, 0, tiled=True)
    ac, slots = middle(received, b, own)
    bc = lax.all_to_all(slots, ("gx", "gz"), 0, 0, tiled=True)
    return last_sums(ac, bc, own, rank)


def solution(mesh):
    factors = (
        P(("gx", "gy", "gz"), None),
        P(("gy", "gx", "gz"), None),
        P(("gz", "gx", "gy"), None),
    )
    return jax.shard_map(
        shards,
        mesh=mesh,
        in_specs=(P("gx", "gy", "gz"), *factors),
        out_specs=factors,
        check_vma=False,
    )
```

```python
import functools

import jax
import jax.numpy as jnp
from jax import lax
from jax.experimental import pallas as pl
from jax.experimental.pallas import tpu as pltpu
from jax.sharding import PartitionSpec as P

STEPS = 2
STEP_SIZE = 0.1
F32 = jnp.float32
BF16 = jnp.bfloat16
HIGHEST = lax.Precision.HIGHEST
VMEM = pl.BlockSpec(memory_space=pltpu.VMEM)
HBM = pl.BlockSpec(memory_space=pltpu.HBM)
CHUNK = 512


def split(x):
    high = x.astype(BF16)
    return high, (x - high.astype(F32)).astype(BF16)


def lower_half(shape):
    return lax.broadcasted_iota(jnp.int32, shape, len(shape) - 1) < shape[-1] // 2


def turn(x):
    return pltpu.roll(x, x.shape[1] // 2, 1)


def from_lower(x):
    return jnp.where(lower_half(x.shape), x, turn(x))


def from_upper(x):
    return jnp.where(lower_half(x.shape), turn(x), x)


def gram(x):
    return lax.dot_general(
        x, x, (((0,), (0,)), ((), ())), precision=HIGHEST, preferred_element_type=F32
    )


def unpack_first(ac_ref, b_ref, a2_ref, b2_ref, c2_ref):
    slots, each, width = ac_ref.shape
    a2_ref[...] = from_lower(ac_ref[...].reshape(slots * each, width))
    for g in range(each):
        c2_ref[g * slots : (g + 1) * slots, :] = ac_ref[:, g, :]
    c2_ref[...] = from_upper(c2_ref[...])
    slots = b_ref.shape[0]
    own = b2_ref.shape[0] // slots
    for n in range(slots):
        b2_ref[n * own : (n + 1) * own, :] = b_ref[n, :own, :]
    b2_ref[...] = from_lower(b2_ref[...])


def unpack_second(ca_ref, b_ref, a2_ref, b2_ref, c2_ref):
    a2_ref[...] = from_upper(ca_ref[...])
    b2_ref[...] = from_upper(b_ref[...])
    c2_ref[...] = from_lower(ca_ref[...])


def pack_first(a, b, c_ref, a_ref, cb_ref):
    count_b = b.shape[0]
    c = c_ref[...]
    a_ref[...] = a
    cb_ref[:count_b, :] = jnp.where(lower_half(b.shape), c[:count_b], b)
    cb_ref[count_b:, :] = jnp.where(lower_half(c[count_b:].shape), c[count_b:], 0.0)


def pack_second(a, b, c_ref, ac_ref, b_ref):
    slots, each, width = ac_ref.shape
    lower = lower_half((each, width))
    for n in range(slots):
        block = c_ref[pl.ds(n, each, stride=slots), :]
        ac_ref[n, :, :] = jnp.where(lower, a[n * each : (n + 1) * each], block)
    b_ref[...] = b


def round_kernel(first, keep, scale, *refs):
    small, t_ref, outs, refs = refs[:2], refs[2], refs[3:5], refs[5:]
    if first:
        t_hbm, t_ref, sems, refs = t_ref, refs[0], refs[-1], refs[1:-1]
    a2_ref, b2_ref, c2_ref, wc_ref, ma_ref = refs
    count_i, count_j, count_k = a2_ref.shape[0], b2_ref.shape[0], c2_ref.shape[0]
    width = a2_ref.shape[1]
    rank = width // 2
    chunks = t_ref.shape[0] // CHUNK
    per = CHUNK // count_j

    def fetch(c):
        at = pl.ds(c * CHUNK, CHUNK)
        return pltpu.make_async_copy(t_hbm.at[at, :], t_ref.at[at, :], sems.at[c])

    for c in range(chunks if first else 0):
        fetch(c).start()

    (unpack_first if first else unpack_second)(*small, a2_ref, b2_ref, c2_ref)
    a2, b2, c2 = a2_ref[...], b2_ref[...], c2_ref[...]
    high = c2.astype(BF16).astype(F32)
    both = jnp.where(lower_half(c2.shape), high, c2 - high).astype(BF16)
    wc_ref[:count_k, :] = both
    wc_ref[count_k:, :] = both
    turned_a = a2.T[:rank]
    turned_b = b2.T[:rank]
    turned_b = jnp.concatenate([turned_b] * (128 // count_j), axis=1)
    gram_a, gram_b, gram_c = gram(a2), gram(b2), gram(c2)

    def model(factor, one, two):
        return 0.5 * jnp.dot(factor, one * two, precision=HIGHEST, preferred_element_type=F32)

    model_a = model(a2, gram_b, gram_c)
    model_b = model(b2, gram_a, gram_c)
    model_c = model(c2, gram_a, gram_b)
    group = 128 // count_j
    lane = lax.broadcasted_iota(jnp.int32, (rank, 128), 1) // count_j

    moment_b = jnp.zeros((count_j, width), F32)
    moment_c = jnp.zeros((width, 2 * count_k), F32)
    for c in range(chunks):
        if first and c % (chunks // 2) == 0:
            for n in range(c, c + chunks // 2):
                fetch(n).wait()
        high, low = split(t_ref[c * CHUNK : (c + 1) * CHUNK, :])
        terms = jnp.concatenate([high, low], axis=1)
        y = jnp.dot(terms, wc_ref[...], preferred_element_type=F32)
        y = y.reshape(per, count_j, width)
        at_i = c * per
        ma_ref[at_i : at_i + per, :] = jnp.sum(y * b2_ref[...][None], axis=1)
        for m in range(per):
            moment_b = moment_b + y[m] * a2_ref[at_i + m : at_i + m + 1, :]
        pieces = []
        for m in range(at_i, at_i + per, group):
            columns = jnp.broadcast_to(turned_a[:, m : m + 1], (rank, 128))
            for g in range(1, group):
                other = jnp.broadcast_to(turned_a[:, m + g : m + g + 1], (rank, 128))
                columns = jnp.where(lane == g, other, columns)
            pieces.append(columns * turned_b)
        rows_high, rows_low = split(jnp.concatenate(pieces, axis=1))
        rows = jnp.concatenate([rows_high, rows_low], axis=0)
        moment_c = moment_c + jnp.dot(rows, terms, preferred_element_type=F32)
    moment_c = moment_c[:, :count_k] + moment_c[:, count_k:]
    moment_c = moment_c[:rank] + moment_c[rank:]
    moment_c = jnp.concatenate([moment_c, moment_c], axis=0).T
    moment_a = ma_ref[...]

    def result(factor, whole, moment, weight, factor_scale):
        out = (whole - moment) * factor_scale
        return out + factor * weight if weight else out

    a = result(a2_ref[...], model_a, moment_a + turn(moment_a), keep[0], scale[0])
    b = result(b2_ref[...], model_b, moment_b + turn(moment_b), keep[1], scale[1])
    c2_ref[...] = result(c2_ref[...], model_c, moment_c, keep[2], scale[2])
    (pack_first if first else pack_second)(a, b, c2_ref, *outs)


def partials(first, keep, scale, small, tensor, sizes, out_shapes):
    count_i, count_j, count_k = sizes
    width = small[0].shape[-1]
    tall = count_i * count_j
    if first:
        tensor = pltpu.with_memory_space_constraint(tensor, pltpu.HBM)
        out_shapes += ((tall, count_k),)
    return pl.pallas_call(
        functools.partial(round_kernel, first, keep, scale),
        out_shape=tuple(jax.ShapeDtypeStruct(s, F32) for s in out_shapes),
        in_specs=[VMEM] * len(small) + [HBM if first else VMEM],
        out_specs=(VMEM,) * len(out_shapes),
        scratch_shapes=[
            pltpu.VMEM((count_i, width), F32),
            pltpu.VMEM((count_j, width), F32),
            pltpu.VMEM((count_k, width), F32),
            pltpu.VMEM((2 * count_k, width), BF16),
            pltpu.VMEM((count_i, width), F32),
        ]
        + [pltpu.SemaphoreType.DMA((tall // CHUNK,))] * first,
        compiler_params=pltpu.CompilerParams(vmem_limit_bytes=24 << 20),
        cost_estimate=pl.CostEstimate(flops=1 << 30, bytes_accessed=4 << 20, transcendentals=0),
        name="partials",
    )(*small, tensor)


def first_kernel(a_hbm, b_hbm, c_hbm, slots_ref, a_ref, b_ref, c_ref, sems):
    own, rank = a_ref.shape
    pairs = ((a_hbm, a_ref), (b_hbm, b_ref), (c_hbm, c_ref))
    copies = [pltpu.make_async_copy(x, y, sems.at[n]) for n, (x, y) in enumerate(pairs)]
    for copy in copies:
        copy.start()
    for copy in copies:
        copy.wait()
    a = a_ref[...]
    rows = jnp.concatenate([b_ref[...], jnp.broadcast_to(c_ref[...], (own, rank))], axis=1)
    slot = jnp.concatenate([rows, jnp.concatenate([a, a], axis=1)], axis=0)
    for n in range(slots_ref.shape[0]):
        slots_ref[n, :, :] = slot


def first_slots(a, b, c, count):
    own, rank = a.shape
    factors = [pltpu.with_memory_space_constraint(x, pltpu.HBM) for x in (a, b, c)]
    return pl.pallas_call(
        first_kernel,
        out_shape=jax.ShapeDtypeStruct((count, 2 * own, 2 * rank), F32),
        in_specs=[HBM] * 3,
        out_specs=VMEM,
        scratch_shapes=[pltpu.VMEM(x.shape, F32) for x in (a, b, c)]
        + [pltpu.SemaphoreType.DMA((3,))],
        compiler_params=pltpu.CompilerParams(vmem_limit_bytes=4 << 20),
        name="first_slots",
    )(*factors)


def second_kernel(all_ref, slots_ref):
    core = lax.axis_index("gz")
    chip = lax.axis_index("gx") * 2
    slots, tall, width = all_ref.shape
    own = tall // 2
    a = jnp.concatenate([all_ref[chip, own:, :], all_ref[chip + 1, own:, :]], axis=0)
    flat = all_ref.reshape(slots * tall, width)
    c = flat[pl.ds(core * tall, slots // 2, stride=2 * tall), :]
    slot = jnp.where(lower_half(a.shape), a, c)
    for n in range(slots_ref.shape[0]):
        slots_ref[n, :, :] = slot


def second_slots(received, count):
    _, tall, width = received.shape
    return pl.pallas_call(
        second_kernel,
        out_shape=jax.ShapeDtypeStruct((count, tall, width), F32),
        in_specs=[VMEM],
        out_specs=VMEM,
        compiler_params=pltpu.CompilerParams(vmem_limit_bytes=4 << 20),
        name="second_slots",
    )(received)


def last_kernel(ac_ref, other_ref, bc_ref, a_ref, b_ref, c_ref, sum_a_ref, sum_b_ref):
    own, rank = a_ref.shape
    sum_a_ref[...] = ac_ref[...] + other_ref[other_ref.shape[0] - ac_ref.shape[0] :, :]
    sum_b_ref[...] = jnp.sum(bc_ref[...], axis=0)
    mine = pl.ds(lax.axis_index("gz") * own, own)
    a_ref[...] = sum_a_ref[mine, :][:, :rank]
    b_ref[...] = sum_b_ref[mine, :][:, :rank]
    c_ref[...] = sum_b_ref[:1, :][:, rank:]


def last_sums(ac, other, bc, own, rank):
    return pl.pallas_call(
        last_kernel,
        out_shape=tuple(jax.ShapeDtypeStruct((n, rank), F32) for n in (own, own, 1)),
        scratch_shapes=[pltpu.VMEM(ac.shape, F32)] * 2,
        compiler_params=pltpu.CompilerParams(vmem_limit_bytes=4 << 20),
        name="last_sums",
    )(ac, other, bc)


def shift(x, axis, stride, count, by):
    pairs = []
    for n in range(lax.axis_size(axis)):
        place = n // stride % count
        pairs.append((n, n + ((place + by) % count - place) * stride))
    return lax.ppermute(x, axis, pairs)


def ring8(x):
    three = x + shift(x, "gx", 1, 8, 1) + shift(x, "gx", 1, 8, -1)
    return three + shift(three, "gx", 1, 8, 4) + shift(x, "gx", 1, 8, 2) + shift(x, "gx", 1, 8, -2)


def ring4(x, stride):
    ones = shift(x, "gy", stride, 4, 1) + shift(x, "gy", stride, 4, -1)
    return (x + ones) + shift(x, "gy", stride, 4, 2)


def swap(x):
    return lax.ppermute(x, "gz", [(0, 1), (1, 0)])


def shards(tensor, factor_a, factor_b, factor_c):
    count_x, count_y, count_z = (lax.axis_size(n) for n in ("gx", "gy", "gz"))
    count_i, count_j, count_k = tensor.shape
    whole = (
        float(count_j * count_y * count_k * count_z),
        float(count_i * count_x * count_k * count_z),
        float(count_i * count_x * count_j * count_y),
    )
    copies = (count_y * count_z, count_x * count_z, count_x * count_y)
    own, rank = factor_a.shape
    wide = 2 * rank

    slots = first_slots(factor_a, factor_b, factor_c, count_x * count_z)
    along_x = lax.all_to_all(slots, ("gx", "gz"), 0, 0, tiled=True)
    along_y = lax.all_to_all(second_slots(along_x, count_y), "gy", 0, 0, tiled=True)

    keep = tuple(1.0 / n for n in copies)
    scale = tuple(-STEP_SIZE / n for n in whole)
    sizes = tensor.shape
    tensor = tensor.reshape(count_i * count_j, count_k)
    shapes = ((count_i, wide), (count_k, wide))
    a, cb, tensor = partials(True, keep, scale, (along_y, along_x), tensor, sizes, shapes)
    a = a + swap(a)
    cb = ring8(cb)
    ca = ring4(ring4(jnp.where(lower_half(cb.shape), cb, a), 1), 4)
    b = cb[:count_j]
    b = b + swap(b)

    scale = tuple(1.0 / n for n in whole)
    shapes = ((count_y, 2 * own, wide), (count_j, wide))
    slots_ac, b = partials(False, (0.0,) * 3, scale, (ca, b), tensor, sizes, shapes)
    ac = jnp.sum(lax.all_to_all(slots_ac, "gy", 0, 0, tiled=True), axis=0)
    others = swap(jnp.concatenate([b, ac], axis=0))
    b = b + others[:count_j]
    slots_b = b.reshape(count_x, 2 * own, wide)
    slots_bc = jnp.where(lower_half(slots_b.shape), slots_b, ac[:, None])
    bc = lax.all_to_all(slots_bc, "gx", 0, 0, tiled=True)
    return last_sums(ac, others, bc, own, rank)


def solution(mesh):
    factors = (
        P(("gx", "gy", "gz"), None),
        P(("gy", "gx", "gz"), None),
        P(("gz", "gx", "gy"), None),
    )
    return jax.shard_map(
        shards,
        mesh=mesh,
        in_specs=(P("gx", "gy", "gz"), *factors),
        out_specs=factors,
        check_vma=False,
    )
```

```python
import functools

import jax
import jax.numpy as jnp
from jax import lax
from jax.experimental import pallas as pl
from jax.experimental.pallas import tpu as pltpu
from jax.sharding import PartitionSpec as P

STEPS = 2
STEP_SIZE = 0.1
F32 = jnp.float32
BF16 = jnp.bfloat16
HIGHEST = lax.Precision.HIGHEST
VMEM = pl.BlockSpec(memory_space=pltpu.VMEM)
HBM = pl.BlockSpec(memory_space=pltpu.HBM)
CHUNK = 512


def split(x):
    high = x.astype(BF16)
    return high, (x - high.astype(F32)).astype(BF16)


def lower_half(shape):
    return lax.broadcasted_iota(jnp.int32, shape, len(shape) - 1) < shape[-1] // 2


def turn(x):
    return pltpu.roll(x, x.shape[1] // 2, 1)


def from_lower(x):
    return jnp.where(lower_half(x.shape), x, turn(x))


def from_upper(x):
    return jnp.where(lower_half(x.shape), turn(x), x)


def gram(x):
    return lax.dot_general(
        x, x, (((0,), (0,)), ((), ())), precision=HIGHEST, preferred_element_type=F32
    )


def unpack_first(ac_ref, b_ref, a2_ref, b2_ref, c2_ref):
    slots, each, width = ac_ref.shape
    a2_ref[...] = from_lower(ac_ref[...].reshape(slots * each, width))
    for g in range(each):
        c2_ref[g * slots : (g + 1) * slots, :] = ac_ref[:, g, :]
    c2_ref[...] = from_upper(c2_ref[...])
    slots = b_ref.shape[0]
    own = b2_ref.shape[0] // slots
    for n in range(slots):
        b2_ref[n * own : (n + 1) * own, :] = b_ref[n, :own, :]
    b2_ref[...] = from_lower(b2_ref[...])


def unpack_second(ca_ref, b_ref, a2_ref, b2_ref, c2_ref):
    a2_ref[...] = from_upper(ca_ref[...])
    b2_ref[...] = from_upper(b_ref[...])
    c2_ref[...] = from_lower(ca_ref[...])


def pack_first(a, b, c_ref, a_ref, cb_ref):
    count_b = b.shape[0]
    c = c_ref[...]
    a_ref[...] = a
    cb_ref[:count_b, :] = jnp.where(lower_half(b.shape), c[:count_b], b)
    cb_ref[count_b:, :] = jnp.where(lower_half(c[count_b:].shape), c[count_b:], 0.0)


def pack_second(a, b, c_ref, ac_ref, b_ref):
    slots, each, width = ac_ref.shape
    lower = lower_half((each, width))
    for n in range(slots):
        block = c_ref[pl.ds(n, each, stride=slots), :]
        ac_ref[n, :, :] = jnp.where(lower, a[n * each : (n + 1) * each], block)
    b_ref[...] = b


def round_kernel(first, keep, scale, *refs):
    small, t_ref, outs, refs = refs[:2], refs[2], refs[3:5], refs[5:]
    if first:
        t_hbm, t_ref, sems, refs = t_ref, refs[0], refs[-1], refs[1:-1]
    a2_ref, b2_ref, c2_ref, wc_ref, ma_ref = refs
    count_i, count_j, count_k = a2_ref.shape[0], b2_ref.shape[0], c2_ref.shape[0]
    width = a2_ref.shape[1]
    rank = width // 2
    chunks = t_ref.shape[0] // CHUNK
    per = CHUNK // count_j

    def fetch(c):
        at = pl.ds(c * CHUNK, CHUNK)
        return pltpu.make_async_copy(t_hbm.at[at, :], t_ref.at[at, :], sems.at[c])

    for c in range(chunks if first else 0):
        fetch(c).start()

    (unpack_first if first else unpack_second)(*small, a2_ref, b2_ref, c2_ref)
    a2, b2, c2 = a2_ref[...], b2_ref[...], c2_ref[...]
    high = c2.astype(BF16).astype(F32)
    both = jnp.where(lower_half(c2.shape), high, c2 - high).astype(BF16)
    wc_ref[:count_k, :] = both
    wc_ref[count_k:, :] = both
    turned_a = a2.T[:rank]
    turned_b = b2.T[:rank]
    turned_b = jnp.concatenate([turned_b] * (128 // count_j), axis=1)
    gram_a, gram_b, gram_c = gram(a2), gram(b2), gram(c2)

    def model(factor, one, two):
        return 0.5 * jnp.dot(factor, one * two, precision=HIGHEST, preferred_element_type=F32)

    model_a = model(a2, gram_b, gram_c)
    model_b = model(b2, gram_a, gram_c)
    model_c = model(c2, gram_a, gram_b)
    group = 128 // count_j
    lane = lax.broadcasted_iota(jnp.int32, (rank, 128), 1) // count_j

    half, quarter = chunks // 2, chunks // 4
    waits = {0: half, half: half + quarter, half + quarter: chunks}
    moment_b = jnp.zeros((count_j, width), F32)
    moment_c = jnp.zeros((width, 2 * count_k), F32)
    for c in range(chunks):
        if first and c in waits:
            for n in range(c, waits[c]):
                fetch(n).wait()
        high, low = split(t_ref[c * CHUNK : (c + 1) * CHUNK, :])
        terms = jnp.concatenate([high, low], axis=1)
        y = jnp.dot(terms, wc_ref[...], preferred_element_type=F32)
        y = y.reshape(per, count_j, width)
        at_i = c * per
        ma_ref[at_i : at_i + per, :] = jnp.sum(y * b2_ref[...][None], axis=1)
        for m in range(per):
            moment_b = moment_b + y[m] * a2_ref[at_i + m : at_i + m + 1, :]
        pieces = []
        for m in range(at_i, at_i + per, group):
            columns = jnp.broadcast_to(turned_a[:, m : m + 1], (rank, 128))
            for g in range(1, group):
                other = jnp.broadcast_to(turned_a[:, m + g : m + g + 1], (rank, 128))
                columns = jnp.where(lane == g, other, columns)
            pieces.append(columns * turned_b)
        rows_high, rows_low = split(jnp.concatenate(pieces, axis=1))
        rows = jnp.concatenate([rows_high, rows_low], axis=0)
        moment_c = moment_c + jnp.dot(rows, terms, preferred_element_type=F32)
    moment_c = moment_c[:, :count_k] + moment_c[:, count_k:]
    moment_c = moment_c[:rank] + moment_c[rank:]
    moment_c = jnp.concatenate([moment_c, moment_c], axis=0).T
    moment_a = ma_ref[...]

    def result(factor, whole, moment, weight, factor_scale):
        out = (whole - moment) * factor_scale
        return out + factor * weight if weight else out

    a = result(a2_ref[...], model_a, moment_a + turn(moment_a), keep[0], scale[0])
    b = result(b2_ref[...], model_b, moment_b + turn(moment_b), keep[1], scale[1])
    c2_ref[...] = result(c2_ref[...], model_c, moment_c, keep[2], scale[2])
    (pack_first if first else pack_second)(a, b, c2_ref, *outs)


def partials(first, keep, scale, small, tensor, sizes, out_shapes):
    count_i, count_j, count_k = sizes
    width = small[0].shape[-1]
    tall = count_i * count_j
    if first:
        tensor = pltpu.with_memory_space_constraint(tensor, pltpu.HBM)
        out_shapes += ((tall, count_k),)
    return pl.pallas_call(
        functools.partial(round_kernel, first, keep, scale),
        out_shape=tuple(jax.ShapeDtypeStruct(s, F32) for s in out_shapes),
        in_specs=[VMEM] * len(small) + [HBM if first else VMEM],
        out_specs=(VMEM,) * len(out_shapes),
        scratch_shapes=[
            pltpu.VMEM((count_i, width), F32),
            pltpu.VMEM((count_j, width), F32),
            pltpu.VMEM((count_k, width), F32),
            pltpu.VMEM((2 * count_k, width), BF16),
            pltpu.VMEM((count_i, width), F32),
        ]
        + [pltpu.SemaphoreType.DMA((tall // CHUNK,))] * first,
        compiler_params=pltpu.CompilerParams(vmem_limit_bytes=24 << 20),
        cost_estimate=pl.CostEstimate(flops=1 << 30, bytes_accessed=4 << 20, transcendentals=0),
        name="partials",
    )(*small, tensor)


def first_kernel(a_hbm, b_hbm, c_hbm, slots_ref, a_ref, b_ref, c_ref, sems):
    own, rank = a_ref.shape
    pairs = ((a_hbm, a_ref), (b_hbm, b_ref), (c_hbm, c_ref))
    copies = [pltpu.make_async_copy(x, y, sems.at[n]) for n, (x, y) in enumerate(pairs)]
    for copy in copies:
        copy.start()
    for copy in copies:
        copy.wait()
    a = a_ref[...]
    rows = jnp.concatenate([b_ref[...], jnp.broadcast_to(c_ref[...], (own, rank))], axis=1)
    slot = jnp.concatenate([rows, jnp.concatenate([a, a], axis=1)], axis=0)
    for n in range(slots_ref.shape[0]):
        slots_ref[n, :, :] = slot


def first_slots(a, b, c, count):
    own, rank = a.shape
    factors = [pltpu.with_memory_space_constraint(x, pltpu.HBM) for x in (a, b, c)]
    return pl.pallas_call(
        first_kernel,
        out_shape=jax.ShapeDtypeStruct((count, 2 * own, 2 * rank), F32),
        in_specs=[HBM] * 3,
        out_specs=VMEM,
        scratch_shapes=[pltpu.VMEM(x.shape, F32) for x in (a, b, c)]
        + [pltpu.SemaphoreType.DMA((3,))],
        compiler_params=pltpu.CompilerParams(vmem_limit_bytes=4 << 20),
        name="first_slots",
    )(*factors)


def second_kernel(all_ref, slots_ref):
    core = lax.axis_index("gz")
    chip = lax.axis_index("gx") * 2
    slots, tall, width = all_ref.shape
    own = tall // 2
    a = jnp.concatenate([all_ref[chip, own:, :], all_ref[chip + 1, own:, :]], axis=0)
    flat = all_ref.reshape(slots * tall, width)
    c = flat[pl.ds(core * tall, slots // 2, stride=2 * tall), :]
    slot = jnp.where(lower_half(a.shape), a, c)
    for n in range(slots_ref.shape[0]):
        slots_ref[n, :, :] = slot


def second_slots(received, count):
    _, tall, width = received.shape
    return pl.pallas_call(
        second_kernel,
        out_shape=jax.ShapeDtypeStruct((count, tall, width), F32),
        in_specs=[VMEM],
        out_specs=VMEM,
        compiler_params=pltpu.CompilerParams(vmem_limit_bytes=4 << 20),
        name="second_slots",
    )(received)


def middle_kernel(received_ref, b_ref, slots_ref, ac_ref):
    core, me_x = lax.axis_index("gz"), lax.axis_index("gx")
    slots, tall, width = slots_ref.shape
    own = tall // 2
    ac_ref[...] = jnp.sum(received_ref[...], axis=0)
    lower = lower_half((own, width))
    for n in range(slots):
        x, z = n // 2, n % 2
        c = jnp.broadcast_to(ac_ref[x : x + 1, :], (own, width))
        c = jnp.where(core == z, c, 0.0)
        slots_ref[n, :own, :] = jnp.where(lower, b_ref[n * own : (n + 1) * own, :], c)
        slots_ref[n, own:, :] = jnp.where(me_x == x, ac_ref[z * own : (z + 1) * own, :], 0.0)


def middle_slots(received, b, count):
    _, tall, width = received.shape
    return pl.pallas_call(
        middle_kernel,
        out_shape=jax.ShapeDtypeStruct((count, tall, width), F32),
        in_specs=[VMEM] * 2,
        out_specs=VMEM,
        scratch_shapes=[pltpu.VMEM((tall, width), F32)],
        compiler_params=pltpu.CompilerParams(vmem_limit_bytes=4 << 20),
        name="middle_slots",
    )(received, b)


def last_kernel(all_ref, a_ref, b_ref, c_ref):
    own, rank = a_ref.shape
    sums = jnp.sum(all_ref[...], axis=0)
    a_ref[...] = sums[own:, :rank]
    b_ref[...] = sums[:own, :rank]
    c_ref[...] = sums[:1, rank:]


def last_sums(received, own, rank):
    return pl.pallas_call(
        last_kernel,
        out_shape=tuple(jax.ShapeDtypeStruct((n, rank), F32) for n in (own, own, 1)),
        compiler_params=pltpu.CompilerParams(vmem_limit_bytes=4 << 20),
        name="last_sums",
    )(received)


def shift(x, axis, stride, count, by):
    pairs = []
    for n in range(lax.axis_size(axis)):
        place = n // stride % count
        pairs.append((n, n + ((place + by) % count - place) * stride))
    return lax.ppermute(x, axis, pairs)


def ring8(x):
    three = x + shift(x, "gx", 1, 8, 1) + shift(x, "gx", 1, 8, -1)
    return three + shift(three, "gx", 1, 8, 4) + shift(x, "gx", 1, 8, 2) + shift(x, "gx", 1, 8, -2)


def ring4(x, stride):
    ones = shift(x, "gy", stride, 4, 1) + shift(x, "gy", stride, 4, -1)
    return (x + ones) + shift(x, "gy", stride, 4, 2)


def swap(x):
    return lax.ppermute(x, "gz", [(0, 1), (1, 0)])


def shards(tensor, factor_a, factor_b, factor_c):
    count_x, count_y, count_z = (lax.axis_size(n) for n in ("gx", "gy", "gz"))
    count_i, count_j, count_k = tensor.shape
    whole = (
        float(count_j * count_y * count_k * count_z),
        float(count_i * count_x * count_k * count_z),
        float(count_i * count_x * count_j * count_y),
    )
    copies = (count_y * count_z, count_x * count_z, count_x * count_y)
    own, rank = factor_a.shape
    wide = 2 * rank

    slots = first_slots(factor_a, factor_b, factor_c, count_x * count_z)
    along_x = lax.all_to_all(slots, ("gx", "gz"), 0, 0, tiled=True)
    along_y = lax.all_to_all(second_slots(along_x, count_y), "gy", 0, 0, tiled=True)

    keep = tuple(1.0 / n for n in copies)
    scale = tuple(-STEP_SIZE / n for n in whole)
    sizes = tensor.shape
    tensor = tensor.reshape(count_i * count_j, count_k)
    shapes = ((count_i, wide), (count_k, wide))
    a, cb, tensor = partials(True, keep, scale, (along_y, along_x), tensor, sizes, shapes)
    a = a + swap(a)
    cb = ring8(cb)
    ca = ring4(ring4(jnp.where(lower_half(cb.shape), cb, a), 1), 4)
    b = cb[:count_j]
    b = b + swap(b)

    scale = tuple(1.0 / n for n in whole)
    shapes = ((count_y, 2 * own, wide), (count_j, wide))
    slots_ac, b = partials(False, (0.0,) * 3, scale, (ca, b), tensor, sizes, shapes)
    received = lax.all_to_all(slots_ac, "gy", 0, 0, tiled=True)
    slots = middle_slots(received, b, count_x * count_z)
    return last_sums(lax.all_to_all(slots, ("gx", "gz"), 0, 0, tiled=True), own, rank)


def solution(mesh):
    factors = (
        P(("gx", "gy", "gz"), None),
        P(("gy", "gx", "gz"), None),
        P(("gz", "gx", "gy"), None),
    )
    return jax.shard_map(
        shards,
        mesh=mesh,
        in_specs=(P("gx", "gy", "gz"), *factors),
        out_specs=factors,
        check_vma=False,
    )
```

```python
import functools

import jax
import jax.numpy as jnp
from jax import lax
from jax.experimental import pallas as pl
from jax.experimental.pallas import tpu as pltpu
from jax.sharding import PartitionSpec as P

STEPS = 2
STEP_SIZE = 0.1
F32 = jnp.float32
BF16 = jnp.bfloat16
HIGHEST = lax.Precision.HIGHEST
VMEM = pl.BlockSpec(memory_space=pltpu.VMEM)
HBM = pl.BlockSpec(memory_space=pltpu.HBM)
CHUNK = 512


def split(x):
    high = x.astype(BF16)
    return high, (x - high.astype(F32)).astype(BF16)


def lower_half(shape):
    return lax.broadcasted_iota(jnp.int32, shape, len(shape) - 1) < shape[-1] // 2


def turn(x):
    return pltpu.roll(x, x.shape[1] // 2, 1)


def from_lower(x):
    return jnp.where(lower_half(x.shape), x, turn(x))


def from_upper(x):
    return jnp.where(lower_half(x.shape), turn(x), x)


def gram(x):
    return lax.dot_general(
        x, x, (((0,), (0,)), ((), ())), precision=HIGHEST, preferred_element_type=F32
    )


def unpack_first(ac_ref, b_ref, a2_ref, b2_ref, c2_ref):
    slots, each, width = ac_ref.shape
    a2_ref[...] = from_lower(ac_ref[...].reshape(slots * each, width))
    for g in range(each):
        c2_ref[g * slots : (g + 1) * slots, :] = ac_ref[:, g, :]
    c2_ref[...] = from_upper(c2_ref[...])
    slots = b_ref.shape[0]
    own = b2_ref.shape[0] // slots
    for n in range(slots):
        b2_ref[n * own : (n + 1) * own, :] = b_ref[n, :own, :]
    b2_ref[...] = from_lower(b2_ref[...])


def unpack_second(ca_ref, b_ref, a2_ref, b2_ref, c2_ref):
    a2_ref[...] = from_upper(ca_ref[...])
    b2_ref[...] = from_upper(b_ref[...])
    c2_ref[...] = from_lower(ca_ref[...])


def pack_first(a, b, c_ref, a_ref, cb_ref):
    count_b = b.shape[0]
    c = c_ref[...]
    a_ref[...] = a
    cb_ref[:count_b, :] = jnp.where(lower_half(b.shape), c[:count_b], b)
    cb_ref[count_b:, :] = jnp.where(lower_half(c[count_b:].shape), c[count_b:], 0.0)


def pack_second(a, b, c_ref, ac_ref, b_ref):
    slots, each, width = ac_ref.shape
    lower = lower_half((each, width))
    for n in range(slots):
        block = c_ref[pl.ds(n, each, stride=slots), :]
        ac_ref[n, :, :] = jnp.where(lower, a[n * each : (n + 1) * each], block)
    b_ref[...] = b


def round_kernel(first, keep, scale, *refs):
    small, t_ref, outs, refs = refs[:2], refs[2], refs[3:5], refs[5:]
    if first:
        t_hbm, t_ref, sems, refs = t_ref, refs[0], refs[-1], refs[1:-1]
    a2_ref, b2_ref, c2_ref, wc_ref, ma_ref = refs
    count_i, count_j, count_k = a2_ref.shape[0], b2_ref.shape[0], c2_ref.shape[0]
    width = a2_ref.shape[1]
    rank = width // 2
    chunks = t_ref.shape[0] // CHUNK
    per = CHUNK // count_j

    def fetch(c):
        at = pl.ds(c * CHUNK, CHUNK)
        return pltpu.make_async_copy(t_hbm.at[at, :], t_ref.at[at, :], sems.at[c])

    for c in range(chunks if first else 0):
        fetch(c).start()

    (unpack_first if first else unpack_second)(*small, a2_ref, b2_ref, c2_ref)
    a2, b2, c2 = a2_ref[...], b2_ref[...], c2_ref[...]
    high = c2.astype(BF16).astype(F32)
    both = jnp.where(lower_half(c2.shape), high, c2 - high).astype(BF16)
    wc_ref[:count_k, :] = both
    wc_ref[count_k:, :] = both
    turned_a = a2.T[:rank]
    turned_b = b2.T[:rank]
    turned_b = jnp.concatenate([turned_b] * (128 // count_j), axis=1)
    gram_a, gram_b, gram_c = gram(a2), gram(b2), gram(c2)

    def model(factor, one, two):
        return 0.5 * jnp.dot(factor, one * two, precision=HIGHEST, preferred_element_type=F32)

    model_a = model(a2, gram_b, gram_c)
    model_b = model(b2, gram_a, gram_c)
    model_c = model(c2, gram_a, gram_b)
    group = 128 // count_j
    lane = lax.broadcasted_iota(jnp.int32, (rank, 128), 1) // count_j

    waits = {0: chunks // 2, chunks // 2: chunks}
    moment_b = jnp.zeros((count_j, width), F32)
    moment_c = jnp.zeros((width, 2 * count_k), F32)
    for c in range(chunks):
        if first and c in waits:
            for n in range(c, waits[c]):
                fetch(n).wait()
        high, low = split(t_ref[c * CHUNK : (c + 1) * CHUNK, :])
        terms = jnp.concatenate([high, low], axis=1)
        y = jnp.dot(terms, wc_ref[...], preferred_element_type=F32)
        y = y.reshape(per, count_j, width)
        at_i = c * per
        ma_ref[at_i : at_i + per, :] = jnp.sum(y * b2_ref[...][None], axis=1)
        for m in range(per):
            moment_b = moment_b + y[m] * a2_ref[at_i + m : at_i + m + 1, :]
        pieces = []
        for m in range(at_i, at_i + per, group):
            columns = jnp.broadcast_to(turned_a[:, m : m + 1], (rank, 128))
            for g in range(1, group):
                other = jnp.broadcast_to(turned_a[:, m + g : m + g + 1], (rank, 128))
                columns = jnp.where(lane == g, other, columns)
            pieces.append(columns * turned_b)
        rows_high, rows_low = split(jnp.concatenate(pieces, axis=1))
        rows = jnp.concatenate([rows_high, rows_low], axis=0)
        moment_c = moment_c + jnp.dot(rows, terms, preferred_element_type=F32)
    moment_c = moment_c[:, :count_k] + moment_c[:, count_k:]
    moment_c = moment_c[:rank] + moment_c[rank:]
    moment_c = jnp.concatenate([moment_c, moment_c], axis=0).T
    moment_a = ma_ref[...]

    def result(factor, whole, moment, weight, factor_scale):
        out = (whole - moment) * factor_scale
        return out + factor * weight if weight else out

    a = result(a2_ref[...], model_a, moment_a + turn(moment_a), keep[0], scale[0])
    b = result(b2_ref[...], model_b, moment_b + turn(moment_b), keep[1], scale[1])
    c2_ref[...] = result(c2_ref[...], model_c, moment_c, keep[2], scale[2])
    (pack_first if first else pack_second)(a, b, c2_ref, *outs)


def partials(first, keep, scale, small, tensor, sizes, out_shapes):
    count_i, count_j, count_k = sizes
    width = small[0].shape[-1]
    tall = count_i * count_j
    if first:
        tensor = pltpu.with_memory_space_constraint(tensor, pltpu.HBM)
        out_shapes += ((tall, count_k),)
    return pl.pallas_call(
        functools.partial(round_kernel, first, keep, scale),
        out_shape=tuple(jax.ShapeDtypeStruct(s, F32) for s in out_shapes),
        in_specs=[VMEM] * len(small) + [HBM if first else VMEM],
        out_specs=(VMEM,) * len(out_shapes),
        scratch_shapes=[
            pltpu.VMEM((count_i, width), F32),
            pltpu.VMEM((count_j, width), F32),
            pltpu.VMEM((count_k, width), F32),
            pltpu.VMEM((2 * count_k, width), BF16),
            pltpu.VMEM((count_i, width), F32),
        ]
        + [pltpu.SemaphoreType.DMA((tall // CHUNK,))] * first,
        compiler_params=pltpu.CompilerParams(vmem_limit_bytes=24 << 20),
        cost_estimate=pl.CostEstimate(flops=1 << 30, bytes_accessed=4 << 20, transcendentals=0),
        name="partials",
    )(*small, tensor)


def first_kernel(a_hbm, b_hbm, c_hbm, slots_ref, a_ref, b_ref, c_ref, sems):
    own, rank = a_ref.shape
    pairs = ((a_hbm, a_ref), (b_hbm, b_ref), (c_hbm, c_ref))
    copies = [pltpu.make_async_copy(x, y, sems.at[n]) for n, (x, y) in enumerate(pairs)]
    for copy in copies:
        copy.start()
    for copy in copies:
        copy.wait()
    a = a_ref[...]
    rows = jnp.concatenate([b_ref[...], jnp.broadcast_to(c_ref[...], (own, rank))], axis=1)
    slot = jnp.concatenate([rows, jnp.concatenate([a, a], axis=1)], axis=0)
    for n in range(slots_ref.shape[0]):
        slots_ref[n, :, :] = slot


def first_slots(a, b, c, count):
    own, rank = a.shape
    factors = [pltpu.with_memory_space_constraint(x, pltpu.HBM) for x in (a, b, c)]
    return pl.pallas_call(
        first_kernel,
        out_shape=jax.ShapeDtypeStruct((count, 2 * own, 2 * rank), F32),
        in_specs=[HBM] * 3,
        out_specs=VMEM,
        scratch_shapes=[pltpu.VMEM(x.shape, F32) for x in (a, b, c)]
        + [pltpu.SemaphoreType.DMA((3,))],
        compiler_params=pltpu.CompilerParams(vmem_limit_bytes=4 << 20),
        name="first_slots",
    )(*factors)


def second_kernel(all_ref, slots_ref):
    core = lax.axis_index("gz")
    chip = lax.axis_index("gx") * 2
    slots, tall, width = all_ref.shape
    own = tall // 2
    a = jnp.concatenate([all_ref[chip, own:, :], all_ref[chip + 1, own:, :]], axis=0)
    flat = all_ref.reshape(slots * tall, width)
    c = flat[pl.ds(core * tall, slots // 2, stride=2 * tall), :]
    slot = jnp.where(lower_half(a.shape), a, c)
    for n in range(slots_ref.shape[0]):
        slots_ref[n, :, :] = slot


def second_slots(received, count):
    _, tall, width = received.shape
    return pl.pallas_call(
        second_kernel,
        out_shape=jax.ShapeDtypeStruct((count, tall, width), F32),
        in_specs=[VMEM],
        out_specs=VMEM,
        compiler_params=pltpu.CompilerParams(vmem_limit_bytes=4 << 20),
        name="second_slots",
    )(received)


def middle_kernel(received_ref, b_ref, slots_ref, ac_ref):
    core, me_x = lax.axis_index("gz"), lax.axis_index("gx")
    slots, tall, width = slots_ref.shape
    own = tall // 2
    ac_ref[...] = jnp.sum(received_ref[...], axis=0)
    lower = lower_half((own, width))
    for n in range(slots):
        x, z = n // 2, n % 2
        c = jnp.broadcast_to(ac_ref[x : x + 1, :], (own, width))
        c = jnp.where(core == z, c, 0.0)
        slots_ref[n, :own, :] = jnp.where(lower, b_ref[n * own : (n + 1) * own, :], c)
        slots_ref[n, own:, :] = jnp.where(me_x == x, ac_ref[z * own : (z + 1) * own, :], 0.0)


def middle_slots(received, b, count):
    _, tall, width = received.shape
    return pl.pallas_call(
        middle_kernel,
        out_shape=jax.ShapeDtypeStruct((count, tall, width), F32),
        in_specs=[VMEM] * 2,
        out_specs=VMEM,
        scratch_shapes=[pltpu.VMEM((tall, width), F32)],
        compiler_params=pltpu.CompilerParams(vmem_limit_bytes=4 << 20),
        name="middle_slots",
    )(received, b)


def last_kernel(all_ref, a_ref, b_ref, c_ref):
    own, rank = a_ref.shape
    sums = jnp.sum(all_ref[...], axis=0)
    a_ref[...] = sums[own:, :rank]
    b_ref[...] = sums[:own, :rank]
    c_ref[...] = sums[:1, rank:]


def last_sums(received, own, rank):
    return pl.pallas_call(
        last_kernel,
        out_shape=tuple(jax.ShapeDtypeStruct((n, rank), F32) for n in (own, own, 1)),
        compiler_params=pltpu.CompilerParams(vmem_limit_bytes=4 << 20),
        name="last_sums",
    )(received)


def shift(x, axis, stride, count, by):
    pairs = []
    for n in range(lax.axis_size(axis)):
        place = n // stride % count
        pairs.append((n, n + ((place + by) % count - place) * stride))
    return lax.ppermute(x, axis, pairs)


def ring8(x):
    three = x + shift(x, "gx", 1, 8, 1) + shift(x, "gx", 1, 8, -1)
    return three + shift(three, "gx", 1, 8, 4) + shift(x, "gx", 1, 8, 2) + shift(x, "gx", 1, 8, -2)


def cross(x, stride, by):
    pairs = []
    for n in range(lax.axis_size("gy")):
        place = n // stride % 4
        to = n + ((place + by) % 4 - place) * stride
        pairs += [(2 * n, 2 * to + 1), (2 * n + 1, 2 * to)]
    return lax.ppermute(x, ("gy", "gz"), pairs)


def ring4(x, stride):
    ones = cross(x, stride, 1) + cross(x, stride, -1)
    return (swap(x) + ones) + cross(x, stride, 2)


def swap(x):
    return lax.ppermute(x, "gz", [(0, 1), (1, 0)])


def shards(tensor, factor_a, factor_b, factor_c):
    count_x, count_y, count_z = (lax.axis_size(n) for n in ("gx", "gy", "gz"))
    count_i, count_j, count_k = tensor.shape
    whole = (
        float(count_j * count_y * count_k * count_z),
        float(count_i * count_x * count_k * count_z),
        float(count_i * count_x * count_j * count_y),
    )
    copies = (count_y * count_z, count_x * count_z, count_x * count_y)
    own, rank = factor_a.shape
    wide = 2 * rank

    slots = first_slots(factor_a, factor_b, factor_c, count_x * count_z)
    along_x = lax.all_to_all(slots, ("gx", "gz"), 0, 0, tiled=True)
    along_y = lax.all_to_all(second_slots(along_x, count_y), "gy", 0, 0, tiled=True)

    keep = tuple(1.0 / n for n in copies)
    scale = tuple(-STEP_SIZE / n for n in whole)
    sizes = tensor.shape
    tensor = tensor.reshape(count_i * count_j, count_k)
    shapes = ((count_i, wide), (count_k, wide))
    a, cb, tensor = partials(True, keep, scale, (along_y, along_x), tensor, sizes, shapes)
    a = a + swap(a)
    cb = ring8(cb)
    ca = ring4(ring4(jnp.where(lower_half(cb.shape), cb, a), 1), 4)
    b = cb[:count_j]
    b = b + swap(b)

    scale = tuple(1.0 / n for n in whole)
    shapes = ((count_y, 2 * own, wide), (count_j, wide))
    slots_ac, b = partials(False, (0.0,) * 3, scale, (ca, b), tensor, sizes, shapes)
    received = lax.all_to_all(slots_ac, "gy", 0, 0, tiled=True)
    slots = middle_slots(received, b, count_x * count_z)
    return last_sums(lax.all_to_all(slots, ("gx", "gz"), 0, 0, tiled=True), own, rank)


def solution(mesh):
    factors = (
        P(("gx", "gy", "gz"), None),
        P(("gy", "gx", "gz"), None),
        P(("gz", "gx", "gy"), None),
    )
    return jax.shard_map(
        shards,
        mesh=mesh,
        in_specs=(P("gx", "gy", "gz"), *factors),
        out_specs=factors,
        check_vma=False,
    )
```

```python
import functools

import jax
import jax.numpy as jnp
from jax import lax
from jax.experimental import pallas as pl
from jax.experimental.pallas import tpu as pltpu
from jax.sharding import PartitionSpec as P

STEPS = 2
STEP_SIZE = 0.1
F32 = jnp.float32
BF16 = jnp.bfloat16
HIGHEST = lax.Precision.HIGHEST
VMEM = pl.BlockSpec(memory_space=pltpu.VMEM)
HBM = pl.BlockSpec(memory_space=pltpu.HBM)
CHUNK = 512


def split(x):
    high = x.astype(BF16)
    return high, (x - high.astype(F32)).astype(BF16)


def lower_half(shape):
    return lax.broadcasted_iota(jnp.int32, shape, len(shape) - 1) < shape[-1] // 2


def turn(x):
    return pltpu.roll(x, x.shape[1] // 2, 1)


def from_lower(x):
    return jnp.where(lower_half(x.shape), x, turn(x))


def from_upper(x):
    return jnp.where(lower_half(x.shape), turn(x), x)


def gram(x):
    return lax.dot_general(
        x, x, (((0,), (0,)), ((), ())), precision=HIGHEST, preferred_element_type=F32
    )


def unpack_first(ac_ref, b_ref, a2_ref, b2_ref, c2_ref):
    slots, each, width = ac_ref.shape
    a2_ref[...] = from_lower(ac_ref[...].reshape(slots * each, width))
    for g in range(each):
        c2_ref[g * slots : (g + 1) * slots, :] = ac_ref[:, g, :]
    c2_ref[...] = from_upper(c2_ref[...])
    slots = b_ref.shape[0]
    own = b2_ref.shape[0] // slots
    for n in range(slots):
        b2_ref[n * own : (n + 1) * own, :] = b_ref[n, :own, :]
    b2_ref[...] = from_lower(b2_ref[...])


def unpack_second(ca_ref, b_ref, a2_ref, b2_ref, c2_ref):
    a2_ref[...] = from_upper(ca_ref[...])
    b2_ref[...] = from_upper(b_ref[...])
    c2_ref[...] = from_lower(ca_ref[...])


def pack_first(a, b, c_ref, a_ref, cb_ref):
    count_b = b.shape[0]
    c = c_ref[...]
    a_ref[...] = a
    cb_ref[:count_b, :] = jnp.where(lower_half(b.shape), c[:count_b], b)
    cb_ref[count_b:, :] = jnp.where(lower_half(c[count_b:].shape), c[count_b:], 0.0)


def pack_second(a, b, c_ref, ac_ref, b_ref):
    slots, each, width = ac_ref.shape
    lower = lower_half((each, width))
    for n in range(slots):
        block = c_ref[pl.ds(n, each, stride=slots), :]
        ac_ref[n, :, :] = jnp.where(lower, a[n * each : (n + 1) * each], block)
    b_ref[...] = b


def round_kernel(first, keep, scale, *refs):
    small, t_ref, outs, refs = refs[:2], refs[2], refs[3:5], refs[5:]
    if first:
        t_hbm, t_ref, sems, refs = t_ref, refs[0], refs[-1], refs[1:-1]
    a2_ref, b2_ref, c2_ref, wc_ref, ma_ref = refs
    count_i, count_j, count_k = a2_ref.shape[0], b2_ref.shape[0], c2_ref.shape[0]
    width = a2_ref.shape[1]
    rank = width // 2
    chunks = t_ref.shape[0] // CHUNK
    per = CHUNK // count_j

    def fetch(c):
        at = pl.ds(c * CHUNK, CHUNK)
        return pltpu.make_async_copy(t_hbm.at[at, :], t_ref.at[at, :], sems.at[c])

    for c in range(chunks if first else 0):
        fetch(c).start()

    (unpack_first if first else unpack_second)(*small, a2_ref, b2_ref, c2_ref)
    a2, b2, c2 = a2_ref[...], b2_ref[...], c2_ref[...]
    high = c2.astype(BF16).astype(F32)
    both = jnp.where(lower_half(c2.shape), high, c2 - high).astype(BF16)
    wc_ref[:count_k, :] = both
    wc_ref[count_k:, :] = both
    turned_a = a2.T[:rank]
    turned_b = b2.T[:rank]
    turned_b = jnp.concatenate([turned_b] * (128 // count_j), axis=1)
    gram_a, gram_b, gram_c = gram(a2), gram(b2), gram(c2)

    def model(factor, one, two):
        return 0.5 * jnp.dot(factor, one * two, precision=HIGHEST, preferred_element_type=F32)

    model_a = model(a2, gram_b, gram_c)
    model_b = model(b2, gram_a, gram_c)
    model_c = model(c2, gram_a, gram_b)
    group = 128 // count_j
    lane = lax.broadcasted_iota(jnp.int32, (rank, 128), 1) // count_j

    waits = {0: chunks // 2, chunks // 2: chunks}
    moment_b = jnp.zeros((count_j, width), F32)
    moment_c = jnp.zeros((width, 2 * count_k), F32)
    for c in range(chunks):
        if first and c in waits:
            for n in range(c, waits[c]):
                fetch(n).wait()
        high, low = split(t_ref[c * CHUNK : (c + 1) * CHUNK, :])
        terms = jnp.concatenate([high, low], axis=1)
        y = jnp.dot(terms, wc_ref[...], preferred_element_type=F32)
        y = y.reshape(per, count_j, width)
        at_i = c * per
        ma_ref[at_i : at_i + per, :] = jnp.sum(y * b2_ref[...][None], axis=1)
        for m in range(per):
            moment_b = moment_b + y[m] * a2_ref[at_i + m : at_i + m + 1, :]
        pieces = []
        for m in range(at_i, at_i + per, group):
            columns = jnp.broadcast_to(turned_a[:, m : m + 1], (rank, 128))
            for g in range(1, group):
                other = jnp.broadcast_to(turned_a[:, m + g : m + g + 1], (rank, 128))
                columns = jnp.where(lane == g, other, columns)
            pieces.append(columns * turned_b)
        rows_high, rows_low = split(jnp.concatenate(pieces, axis=1))
        rows = jnp.concatenate([rows_high, rows_low], axis=0)
        moment_c = moment_c + jnp.dot(rows, terms, preferred_element_type=F32)
    moment_c = moment_c[:, :count_k] + moment_c[:, count_k:]
    moment_c = moment_c[:rank] + moment_c[rank:]
    moment_c = jnp.concatenate([moment_c, moment_c], axis=0).T
    moment_a = ma_ref[...]

    def result(factor, whole, moment, weight, factor_scale):
        out = (whole - moment) * factor_scale
        return out + factor * weight if weight else out

    a = result(a2_ref[...], model_a, moment_a + turn(moment_a), keep[0], scale[0])
    b = result(b2_ref[...], model_b, moment_b + turn(moment_b), keep[1], scale[1])
    c2_ref[...] = result(c2_ref[...], model_c, moment_c, keep[2], scale[2])
    (pack_first if first else pack_second)(a, b, c2_ref, *outs)


def partials(first, keep, scale, small, tensor, sizes, out_shapes):
    count_i, count_j, count_k = sizes
    width = small[0].shape[-1]
    tall = count_i * count_j
    if first:
        tensor = pltpu.with_memory_space_constraint(tensor, pltpu.HBM)
        out_shapes += ((tall, count_k),)
    return pl.pallas_call(
        functools.partial(round_kernel, first, keep, scale),
        out_shape=tuple(jax.ShapeDtypeStruct(s, F32) for s in out_shapes),
        in_specs=[VMEM] * len(small) + [HBM if first else VMEM],
        out_specs=(VMEM,) * len(out_shapes),
        scratch_shapes=[
            pltpu.VMEM((count_i, width), F32),
            pltpu.VMEM((count_j, width), F32),
            pltpu.VMEM((count_k, width), F32),
            pltpu.VMEM((2 * count_k, width), BF16),
            pltpu.VMEM((count_i, width), F32),
        ]
        + [pltpu.SemaphoreType.DMA((tall // CHUNK,))] * first,
        compiler_params=pltpu.CompilerParams(vmem_limit_bytes=24 << 20),
        cost_estimate=pl.CostEstimate(flops=1 << 30, bytes_accessed=4 << 20, transcendentals=0),
        name="partials",
    )(*small, tensor)


def first_kernel(a_hbm, b_hbm, c_hbm, slots_ref, a_ref, b_ref, c_ref, sems):
    own, rank = a_ref.shape
    pairs = ((a_hbm, a_ref), (b_hbm, b_ref), (c_hbm, c_ref))
    copies = [pltpu.make_async_copy(x, y, sems.at[n]) for n, (x, y) in enumerate(pairs)]
    for copy in copies:
        copy.start()
    for copy in copies:
        copy.wait()
    a = a_ref[...]
    rows = jnp.concatenate([b_ref[...], jnp.broadcast_to(c_ref[...], (own, rank))], axis=1)
    slot = jnp.concatenate([rows, jnp.concatenate([a, a], axis=1)], axis=0)
    for n in range(slots_ref.shape[0]):
        slots_ref[n, :, :] = slot


def first_slots(a, b, c, count):
    own, rank = a.shape
    factors = [pltpu.with_memory_space_constraint(x, pltpu.HBM) for x in (a, b, c)]
    return pl.pallas_call(
        first_kernel,
        out_shape=jax.ShapeDtypeStruct((count, 2 * own, 2 * rank), F32),
        in_specs=[HBM] * 3,
        out_specs=VMEM,
        scratch_shapes=[pltpu.VMEM(x.shape, F32) for x in (a, b, c)]
        + [pltpu.SemaphoreType.DMA((3,))],
        compiler_params=pltpu.CompilerParams(vmem_limit_bytes=4 << 20),
        name="first_slots",
    )(*factors)


def second_kernel(all_ref, slots_ref):
    core = lax.axis_index("gz")
    chip = lax.axis_index("gx") * 2
    slots, tall, width = all_ref.shape
    own = tall // 2
    a = jnp.concatenate([all_ref[chip, own:, :], all_ref[chip + 1, own:, :]], axis=0)
    flat = all_ref.reshape(slots * tall, width)
    c = flat[pl.ds(core * tall, slots // 2, stride=2 * tall), :]
    slot = jnp.where(lower_half(a.shape), a, c)
    for n in range(slots_ref.shape[0]):
        slots_ref[n, :, :] = slot


def second_slots(received, count):
    _, tall, width = received.shape
    return pl.pallas_call(
        second_kernel,
        out_shape=jax.ShapeDtypeStruct((count, tall, width), F32),
        in_specs=[VMEM],
        out_specs=VMEM,
        compiler_params=pltpu.CompilerParams(vmem_limit_bytes=4 << 20),
        name="second_slots",
    )(received)


def middle_kernel(received_ref, b_ref, slots_ref, ac_ref):
    core, me_x = lax.axis_index("gz"), lax.axis_index("gx")
    slots, tall, width = slots_ref.shape
    own = tall // 2
    ac_ref[...] = jnp.sum(received_ref[...], axis=0)
    lower = lower_half((own, width))
    for n in range(slots):
        x, z = n // 2, n % 2
        c = jnp.broadcast_to(ac_ref[x : x + 1, :], (own, width))
        c = jnp.where(core == z, c, 0.0)
        slots_ref[n, :own, :] = jnp.where(lower, b_ref[n * own : (n + 1) * own, :], c)
        slots_ref[n, own:, :] = jnp.where(me_x == x, ac_ref[z * own : (z + 1) * own, :], 0.0)


def middle_slots(received, b, count):
    _, tall, width = received.shape
    return pl.pallas_call(
        middle_kernel,
        out_shape=jax.ShapeDtypeStruct((count, tall, width), F32),
        in_specs=[VMEM] * 2,
        out_specs=VMEM,
        scratch_shapes=[pltpu.VMEM((tall, width), F32)],
        compiler_params=pltpu.CompilerParams(vmem_limit_bytes=4 << 20),
        name="middle_slots",
    )(received, b)


def last_kernel(all_ref, a_ref, b_ref, c_ref):
    own, rank = a_ref.shape
    sums = jnp.sum(all_ref[...], axis=0)
    a_ref[...] = sums[own:, :rank]
    b_ref[...] = sums[:own, :rank]
    c_ref[...] = sums[:1, rank:]


def last_sums(received, own, rank):
    return pl.pallas_call(
        last_kernel,
        out_shape=tuple(jax.ShapeDtypeStruct((n, rank), F32) for n in (own, own, 1)),
        compiler_params=pltpu.CompilerParams(vmem_limit_bytes=4 << 20),
        name="last_sums",
    )(received)


def shift(x, axis, stride, count, by):
    pairs = []
    for n in range(lax.axis_size(axis)):
        place = n // stride % count
        pairs.append((n, n + ((place + by) % count - place) * stride))
    return lax.ppermute(x, axis, pairs)


def ring8(x):
    below, above = shift(x, "gx", 1, 8, 1), shift(x, "gx", 1, 8, -1)
    two = x + above
    three = two + below
    return three + (shift(three, "gx", 1, 8, -3) + shift(two, "gx", 1, 8, 3))


def ring4(x, stride):
    ones = shift(x, "gy", stride, 4, 1) + shift(x, "gy", stride, 4, -1)
    return (x + ones) + shift(x, "gy", stride, 4, 2)


def swap(x):
    return lax.ppermute(x, "gz", [(0, 1), (1, 0)])


def shards(tensor, factor_a, factor_b, factor_c):
    count_x, count_y, count_z = (lax.axis_size(n) for n in ("gx", "gy", "gz"))
    count_i, count_j, count_k = tensor.shape
    whole = (
        float(count_j * count_y * count_k * count_z),
        float(count_i * count_x * count_k * count_z),
        float(count_i * count_x * count_j * count_y),
    )
    copies = (count_y * count_z, count_x * count_z, count_x * count_y)
    own, rank = factor_a.shape
    wide = 2 * rank

    slots = first_slots(factor_a, factor_b, factor_c, count_x * count_z)
    along_x = lax.all_to_all(slots, ("gx", "gz"), 0, 0, tiled=True)
    along_y = lax.all_to_all(second_slots(along_x, count_y), "gy", 0, 0, tiled=True)

    keep = tuple(1.0 / n for n in copies)
    scale = tuple(-STEP_SIZE / n for n in whole)
    sizes = tensor.shape
    tensor = tensor.reshape(count_i * count_j, count_k)
    shapes = ((count_i, wide), (count_k, wide))
    a, cb, tensor = partials(True, keep, scale, (along_y, along_x), tensor, sizes, shapes)
    a = a + swap(a)
    cb = ring8(cb)
    ca = ring4(ring4(jnp.where(lower_half(cb.shape), cb, a), 1), 4)
    b = cb[:count_j]
    b = b + swap(b)

    scale = tuple(1.0 / n for n in whole)
    shapes = ((count_y, 2 * own, wide), (count_j, wide))
    slots_ac, b = partials(False, (0.0,) * 3, scale, (ca, b), tensor, sizes, shapes)
    received = lax.all_to_all(slots_ac, "gy", 0, 0, tiled=True)
    slots = middle_slots(received, b, count_x * count_z)
    return last_sums(lax.all_to_all(slots, ("gx", "gz"), 0, 0, tiled=True), own, rank)


def solution(mesh):
    factors = (
        P(("gx", "gy", "gz"), None),
        P(("gy", "gx", "gz"), None),
        P(("gz", "gx", "gy"), None),
    )
    return jax.shard_map(
        shards,
        mesh=mesh,
        in_specs=(P("gx", "gy", "gz"), *factors),
        out_specs=factors,
        check_vma=False,
    )
```

```python
import functools

import jax
import jax.numpy as jnp
from jax import lax
from jax.experimental import pallas as pl
from jax.experimental.pallas import tpu as pltpu
from jax.sharding import PartitionSpec as P

STEPS = 2
STEP_SIZE = 0.1
F32 = jnp.float32
BF16 = jnp.bfloat16
HIGHEST = lax.Precision.HIGHEST
VMEM = pl.BlockSpec(memory_space=pltpu.VMEM)
HBM = pl.BlockSpec(memory_space=pltpu.HBM)
CHUNK = 512


def split(x):
    high = x.astype(BF16)
    return high, (x - high.astype(F32)).astype(BF16)


def lower_half(shape):
    return lax.broadcasted_iota(jnp.int32, shape, len(shape) - 1) < shape[-1] // 2


def turn(x):
    return pltpu.roll(x, x.shape[1] // 2, 1)


def from_lower(x):
    return jnp.where(lower_half(x.shape), x, turn(x))


def from_upper(x):
    return jnp.where(lower_half(x.shape), turn(x), x)


def gram(x):
    return lax.dot_general(
        x, x, (((0,), (0,)), ((), ())), precision=HIGHEST, preferred_element_type=F32
    )


def unpack_first(ac_ref, b_ref, a2_ref, b2_ref, c2_ref):
    slots, each, width = ac_ref.shape
    a2_ref[...] = from_lower(ac_ref[...].reshape(slots * each, width))
    for g in range(each):
        c2_ref[g * slots : (g + 1) * slots, :] = ac_ref[:, g, :]
    c2_ref[...] = from_upper(c2_ref[...])
    slots = b_ref.shape[0]
    own = b2_ref.shape[0] // slots
    for n in range(slots):
        b2_ref[n * own : (n + 1) * own, :] = b_ref[n, :own, :]
    b2_ref[...] = from_lower(b2_ref[...])


def unpack_second(ca_ref, b_ref, a2_ref, b2_ref, c2_ref):
    a2_ref[...] = from_upper(ca_ref[...])
    b2_ref[...] = from_upper(b_ref[...])
    c2_ref[...] = from_lower(ca_ref[...])


def pack_first(a, b, c_ref, a_ref, cb_ref):
    count_b = b.shape[0]
    c = c_ref[...]
    a_ref[...] = a
    cb_ref[:count_b, :] = jnp.where(lower_half(b.shape), c[:count_b], b)
    cb_ref[count_b:, :] = jnp.where(lower_half(c[count_b:].shape), c[count_b:], 0.0)


def pack_second(a, b, c_ref, ac_ref, b_ref):
    slots, each, width = ac_ref.shape
    lower = lower_half((each, width))
    for n in range(slots):
        block = c_ref[pl.ds(n, each, stride=slots), :]
        ac_ref[n, :, :] = jnp.where(lower, a[n * each : (n + 1) * each], block)
    b_ref[...] = b


def round_kernel(first, keep, scale, *refs):
    small, t_ref, outs, refs = refs[:2], refs[2], refs[3:5], refs[5:]
    if first:
        t_hbm, t_ref, sems, refs = t_ref, refs[0], refs[-1], refs[1:-1]
    a2_ref, b2_ref, c2_ref, wc_ref, ma_ref = refs
    count_i, count_j, count_k = a2_ref.shape[0], b2_ref.shape[0], c2_ref.shape[0]
    width = a2_ref.shape[1]
    rank = width // 2
    chunks = t_ref.shape[0] // CHUNK
    per = CHUNK // count_j

    def fetch(c):
        at = pl.ds(c * CHUNK, CHUNK)
        return pltpu.make_async_copy(t_hbm.at[at, :], t_ref.at[at, :], sems.at[c])

    for c in range(chunks if first else 0):
        fetch(c).start()

    (unpack_first if first else unpack_second)(*small, a2_ref, b2_ref, c2_ref)
    a2, b2, c2 = a2_ref[...], b2_ref[...], c2_ref[...]
    high = c2.astype(BF16).astype(F32)
    both = jnp.where(lower_half(c2.shape), high, c2 - high).astype(BF16)
    wc_ref[:count_k, :] = both
    wc_ref[count_k:, :] = both
    turned_a = a2.T[:rank]
    turned_b = b2.T[:rank]
    turned_b = jnp.concatenate([turned_b] * (128 // count_j), axis=1)
    gram_a, gram_b, gram_c = gram(a2), gram(b2), gram(c2)

    def model(factor, one, two):
        return 0.5 * jnp.dot(factor, one * two, precision=HIGHEST, preferred_element_type=F32)

    model_a = model(a2, gram_b, gram_c)
    model_b = model(b2, gram_a, gram_c)
    model_c = model(c2, gram_a, gram_b)
    group = 128 // count_j
    lane = lax.broadcasted_iota(jnp.int32, (rank, 128), 1) // count_j

    waits = {0: chunks // 2, chunks // 2: chunks}
    moment_b = jnp.zeros((count_j, width), F32)
    moment_c = jnp.zeros((width, 2 * count_k), F32)
    for c in range(chunks):
        if first and c in waits:
            for n in range(c, waits[c]):
                fetch(n).wait()
        high, low = split(t_ref[c * CHUNK : (c + 1) * CHUNK, :])
        terms = jnp.concatenate([high, low], axis=1)
        y = jnp.dot(terms, wc_ref[...], preferred_element_type=F32)
        y = y.reshape(per, count_j, width)
        at_i = c * per
        ma_ref[at_i : at_i + per, :] = jnp.sum(y * b2_ref[...][None], axis=1)
        for m in range(per):
            moment_b = moment_b + y[m] * a2_ref[at_i + m : at_i + m + 1, :]
        pieces = []
        for m in range(at_i, at_i + per, group):
            columns = jnp.broadcast_to(turned_a[:, m : m + 1], (rank, 128))
            for g in range(1, group):
                other = jnp.broadcast_to(turned_a[:, m + g : m + g + 1], (rank, 128))
                columns = jnp.where(lane == g, other, columns)
            pieces.append(columns * turned_b)
        rows_high, rows_low = split(jnp.concatenate(pieces, axis=1))
        rows = jnp.concatenate([rows_high, rows_low], axis=0)
        moment_c = moment_c + jnp.dot(rows, terms, preferred_element_type=F32)
    moment_c = moment_c[:, :count_k] + moment_c[:, count_k:]
    moment_c = moment_c[:rank] + moment_c[rank:]
    moment_c = jnp.concatenate([moment_c, moment_c], axis=0).T
    moment_a = ma_ref[...]

    def result(factor, whole, moment, weight, factor_scale):
        out = (whole - moment) * factor_scale
        return out + factor * weight if weight else out

    a = result(a2_ref[...], model_a, moment_a + turn(moment_a), keep[0], scale[0])
    b = result(b2_ref[...], model_b, moment_b + turn(moment_b), keep[1], scale[1])
    c2_ref[...] = result(c2_ref[...], model_c, moment_c, keep[2], scale[2])
    (pack_first if first else pack_second)(a, b, c2_ref, *outs)


def partials(first, keep, scale, small, tensor, sizes, out_shapes):
    count_i, count_j, count_k = sizes
    width = small[0].shape[-1]
    tall = count_i * count_j
    if first:
        tensor = pltpu.with_memory_space_constraint(tensor, pltpu.HBM)
        out_shapes += ((tall, count_k),)
    return pl.pallas_call(
        functools.partial(round_kernel, first, keep, scale),
        out_shape=tuple(jax.ShapeDtypeStruct(s, F32) for s in out_shapes),
        in_specs=[VMEM] * len(small) + [HBM if first else VMEM],
        out_specs=(VMEM,) * len(out_shapes),
        scratch_shapes=[
            pltpu.VMEM((count_i, width), F32),
            pltpu.VMEM((count_j, width), F32),
            pltpu.VMEM((count_k, width), F32),
            pltpu.VMEM((2 * count_k, width), BF16),
            pltpu.VMEM((count_i, width), F32),
        ]
        + [pltpu.SemaphoreType.DMA((tall // CHUNK,))] * first,
        compiler_params=pltpu.CompilerParams(vmem_limit_bytes=24 << 20),
        cost_estimate=pl.CostEstimate(flops=1 << 30, bytes_accessed=4 << 20, transcendentals=0),
        name="partials",
    )(*small, tensor)


def first_kernel(a_hbm, b_hbm, c_hbm, slots_ref, a_ref, b_ref, c_ref, sems):
    own, rank = a_ref.shape
    pairs = ((a_hbm, a_ref), (b_hbm, b_ref), (c_hbm, c_ref))
    copies = [pltpu.make_async_copy(x, y, sems.at[n]) for n, (x, y) in enumerate(pairs)]
    for copy in copies:
        copy.start()
    for copy in copies:
        copy.wait()
    a = a_ref[...]
    rows = jnp.concatenate([b_ref[...], jnp.broadcast_to(c_ref[...], (own, rank))], axis=1)
    slot = jnp.concatenate([rows, jnp.concatenate([a, a], axis=1)], axis=0)
    for n in range(slots_ref.shape[0]):
        slots_ref[n, :, :] = slot


def first_slots(a, b, c, count):
    own, rank = a.shape
    factors = [pltpu.with_memory_space_constraint(x, pltpu.HBM) for x in (a, b, c)]
    return pl.pallas_call(
        first_kernel,
        out_shape=jax.ShapeDtypeStruct((count, 2 * own, 2 * rank), F32),
        in_specs=[HBM] * 3,
        out_specs=VMEM,
        scratch_shapes=[pltpu.VMEM(x.shape, F32) for x in (a, b, c)]
        + [pltpu.SemaphoreType.DMA((3,))],
        compiler_params=pltpu.CompilerParams(vmem_limit_bytes=4 << 20),
        name="first_slots",
    )(*factors)


def second_kernel(all_ref, slots_ref):
    core = lax.axis_index("gz")
    chip = lax.axis_index("gx") * 2
    slots, tall, width = all_ref.shape
    own = tall // 2
    a = jnp.concatenate([all_ref[chip, own:, :], all_ref[chip + 1, own:, :]], axis=0)
    flat = all_ref.reshape(slots * tall, width)
    c = flat[pl.ds(core * tall, slots // 2, stride=2 * tall), :]
    slot = jnp.where(lower_half(a.shape), a, c)
    for n in range(slots_ref.shape[0]):
        slots_ref[n, :, :] = slot


def second_slots(received, count):
    _, tall, width = received.shape
    return pl.pallas_call(
        second_kernel,
        out_shape=jax.ShapeDtypeStruct((count, tall, width), F32),
        in_specs=[VMEM],
        out_specs=VMEM,
        compiler_params=pltpu.CompilerParams(vmem_limit_bytes=4 << 20),
        name="second_slots",
    )(received)


def middle_kernel(received_ref, b_ref, slots_ref, ac_ref):
    core, me_x = lax.axis_index("gz"), lax.axis_index("gx")
    slots, tall, width = slots_ref.shape
    own = tall // 2
    ac_ref[...] = jnp.sum(received_ref[...], axis=0)
    lower = lower_half((own, width))
    for n in range(slots):
        x, z = n // 2, n % 2
        c = jnp.broadcast_to(ac_ref[x : x + 1, :], (own, width))
        c = jnp.where(core == z, c, 0.0)
        slots_ref[n, :own, :] = jnp.where(lower, b_ref[n * own : (n + 1) * own, :], c)
        slots_ref[n, own:, :] = jnp.where(me_x == x, ac_ref[z * own : (z + 1) * own, :], 0.0)


def middle_slots(received, b, count):
    _, tall, width = received.shape
    return pl.pallas_call(
        middle_kernel,
        out_shape=jax.ShapeDtypeStruct((count, tall, width), F32),
        in_specs=[VMEM] * 2,
        out_specs=VMEM,
        scratch_shapes=[pltpu.VMEM((tall, width), F32)],
        compiler_params=pltpu.CompilerParams(vmem_limit_bytes=4 << 20),
        name="middle_slots",
    )(received, b)


def last_kernel(all_ref, a_ref, b_ref, c_ref):
    own, rank = a_ref.shape
    sums = jnp.sum(all_ref[...], axis=0)
    a_ref[...] = sums[own:, :rank]
    b_ref[...] = sums[:own, :rank]
    c_ref[...] = sums[:1, rank:]


def last_sums(received, own, rank):
    return pl.pallas_call(
        last_kernel,
        out_shape=tuple(jax.ShapeDtypeStruct((n, rank), F32) for n in (own, own, 1)),
        compiler_params=pltpu.CompilerParams(vmem_limit_bytes=4 << 20),
        name="last_sums",
    )(received)


def shift(x, axis, stride, count, by):
    pairs = []
    for n in range(lax.axis_size(axis)):
        place = n // stride % count
        pairs.append((n, n + ((place + by) % count - place) * stride))
    return lax.ppermute(x, axis, pairs)


def ring8(x):
    three = x + shift(x, "gx", 1, 8, 1) + shift(x, "gx", 1, 8, -1)
    return three + shift(three, "gx", 1, 8, 4) + shift(x, "gx", 1, 8, 2) + shift(x, "gx", 1, 8, -2)


def ring4(x, stride):
    ones = shift(x, "gy", stride, 4, 1) + shift(x, "gy", stride, 4, -1)
    return (x + ones) + shift(x, "gy", stride, 4, 2)


def swap(x):
    return lax.ppermute(x, "gz", [(0, 1), (1, 0)])


def shards(tensor, factor_a, factor_b, factor_c):
    count_x, count_y, count_z = (lax.axis_size(n) for n in ("gx", "gy", "gz"))
    count_i, count_j, count_k = tensor.shape
    whole = (
        float(count_j * count_y * count_k * count_z),
        float(count_i * count_x * count_k * count_z),
        float(count_i * count_x * count_j * count_y),
    )
    copies = (count_y * count_z, count_x * count_z, count_x * count_y)
    own, rank = factor_a.shape
    wide = 2 * rank

    slots = first_slots(factor_a, factor_b, factor_c, count_x * count_z)
    along_x = lax.all_to_all(slots, ("gx", "gz"), 0, 0, tiled=True)
    along_y = lax.all_to_all(second_slots(along_x, count_y), "gy", 0, 0, tiled=True)

    keep = tuple(1.0 / n for n in copies)
    scale = tuple(-STEP_SIZE / n for n in whole)
    sizes = tensor.shape
    tensor = tensor.reshape(count_i * count_j, count_k)
    shapes = ((count_i, wide), (count_k, wide))
    a, cb, tensor = partials(True, keep, scale, (along_y, along_x), tensor, sizes, shapes)
    a = a + swap(a)
    cb = ring8(cb)
    ca = ring4(ring4(jnp.where(lower_half(cb.shape), cb, a), 1), 4)
    b = cb[:count_j]
    b = b + swap(b)

    scale = tuple(1.0 / n for n in whole)
    shapes = ((count_y, 2 * own, wide), (count_j, wide))
    slots_ac, b = partials(False, (0.0,) * 3, scale, (ca, b), tensor, sizes, shapes)
    received = lax.all_to_all(slots_ac, "gy", 0, 0, tiled=True)
    slots = middle_slots(received, b, count_x * count_z)
    return last_sums(lax.all_to_all(slots, ("gx", "gz"), 0, 0, tiled=True), own, rank)


def solution(mesh):
    factors = (
        P(("gx", "gy", "gz"), None),
        P(("gy", "gx", "gz"), None),
        P(("gz", "gx", "gy"), None),
    )
    return jax.shard_map(
        shards,
        mesh=mesh,
        in_specs=(P("gx", "gy", "gz"), *factors),
        out_specs=factors,
        check_vma=False,
    )
```

```python
import functools

import jax
import jax.numpy as jnp
from jax import lax
from jax.experimental import pallas as pl
from jax.experimental.pallas import tpu as pltpu
from jax.sharding import PartitionSpec as P

STEPS = 2
STEP_SIZE = 0.1
F32 = jnp.float32
BF16 = jnp.bfloat16
HIGHEST = lax.Precision.HIGHEST
VMEM = pl.BlockSpec(memory_space=pltpu.VMEM)
HBM = pl.BlockSpec(memory_space=pltpu.HBM)
CHUNK = 512


def split(x):
    high = x.astype(BF16)
    return high, (x - high.astype(F32)).astype(BF16)


def lower_half(shape):
    return lax.broadcasted_iota(jnp.int32, shape, len(shape) - 1) < shape[-1] // 2


def turn(x):
    return pltpu.roll(x, x.shape[1] // 2, 1)


def from_lower(x):
    return jnp.where(lower_half(x.shape), x, turn(x))


def from_upper(x):
    return jnp.where(lower_half(x.shape), turn(x), x)


def gram(x):
    return lax.dot_general(
        x, x, (((0,), (0,)), ((), ())), precision=HIGHEST, preferred_element_type=F32
    )


def unpack_first(ac_ref, b_ref, a2_ref, b2_ref, c2_ref):
    slots, each, width = ac_ref.shape
    a2_ref[...] = from_lower(ac_ref[...].reshape(slots * each, width))
    for g in range(each):
        c2_ref[g * slots : (g + 1) * slots, :] = ac_ref[:, g, :]
    c2_ref[...] = from_upper(c2_ref[...])
    slots = b_ref.shape[0]
    own = b2_ref.shape[0] // slots
    for n in range(slots):
        b2_ref[n * own : (n + 1) * own, :] = b_ref[n, :own, :]
    b2_ref[...] = from_lower(b2_ref[...])


def unpack_second(ca_ref, b_ref, a2_ref, b2_ref, c2_ref):
    a2_ref[...] = from_upper(ca_ref[...])
    b2_ref[...] = from_upper(b_ref[...])
    c2_ref[...] = from_lower(ca_ref[...])


def pack_first(a, b, c_ref, a_ref, cb_ref):
    count_b = b.shape[0]
    c = c_ref[...]
    a_ref[...] = a
    cb_ref[:count_b, :] = jnp.where(lower_half(b.shape), c[:count_b], b)
    cb_ref[count_b:, :] = jnp.where(lower_half(c[count_b:].shape), c[count_b:], 0.0)


def pack_second(a, b, c_ref, ac_ref, b_ref):
    slots, each, width = ac_ref.shape
    lower = lower_half((each, width))
    for n in range(slots):
        block = c_ref[pl.ds(n, each, stride=slots), :]
        ac_ref[n, :, :] = jnp.where(lower, a[n * each : (n + 1) * each], block)
    b_ref[...] = b


def round_kernel(first, keep, scale, *refs):
    small, t_ref, outs, refs = refs[:2], refs[2], refs[3:5], refs[5:]
    if first:
        t_hbm, t_ref, sems, refs = t_ref, refs[0], refs[-1], refs[1:-1]
    a2_ref, b2_ref, c2_ref, wc_ref, ma_ref = refs
    count_i, count_j, count_k = a2_ref.shape[0], b2_ref.shape[0], c2_ref.shape[0]
    width = a2_ref.shape[1]
    rank = width // 2
    chunks = t_ref.shape[0] // CHUNK
    per = CHUNK // count_j

    def fetch(c):
        at = pl.ds(c * (chunks // 4) * CHUNK, chunks // 4 * CHUNK)
        return pltpu.make_async_copy(t_hbm.at[at, :], t_ref.at[at, :], sems.at[c])

    for c in range(4 if first else 0):
        fetch(c).start()

    (unpack_first if first else unpack_second)(*small, a2_ref, b2_ref, c2_ref)
    a2, b2, c2 = a2_ref[...], b2_ref[...], c2_ref[...]
    high = c2.astype(BF16).astype(F32)
    both = jnp.where(lower_half(c2.shape), high, c2 - high).astype(BF16)
    wc_ref[:count_k, :] = both
    wc_ref[count_k:, :] = both
    turned_a = a2.T[:rank]
    turned_b = b2.T[:rank]
    turned_b = jnp.concatenate([turned_b] * (128 // count_j), axis=1)
    gram_a, gram_b, gram_c = gram(a2), gram(b2), gram(c2)

    def model(factor, one, two):
        return 0.5 * jnp.dot(factor, one * two, precision=HIGHEST, preferred_element_type=F32)

    model_a = model(a2, gram_b, gram_c)
    model_b = model(b2, gram_a, gram_c)
    model_c = model(c2, gram_a, gram_b)
    group = 128 // count_j
    lane = lax.broadcasted_iota(jnp.int32, (rank, 128), 1) // count_j

    moment_b = jnp.zeros((count_j, width), F32)
    moment_c = jnp.zeros((width, 2 * count_k), F32)
    for c in range(chunks):
        if first and c % (chunks // 2) == 0:
            for n in range(2):
                fetch(4 * c // chunks + n).wait()
        high, low = split(t_ref[c * CHUNK : (c + 1) * CHUNK, :])
        terms = jnp.concatenate([high, low], axis=1)
        y = jnp.dot(terms, wc_ref[...], preferred_element_type=F32)
        y = y.reshape(per, count_j, width)
        at_i = c * per
        ma_ref[at_i : at_i + per, :] = jnp.sum(y * b2_ref[...][None], axis=1)
        for m in range(per):
            moment_b = moment_b + y[m] * a2_ref[at_i + m : at_i + m + 1, :]
        pieces = []
        for m in range(at_i, at_i + per, group):
            columns = jnp.broadcast_to(turned_a[:, m : m + 1], (rank, 128))
            for g in range(1, group):
                other = jnp.broadcast_to(turned_a[:, m + g : m + g + 1], (rank, 128))
                columns = jnp.where(lane == g, other, columns)
            pieces.append(columns * turned_b)
        rows_high, rows_low = split(jnp.concatenate(pieces, axis=1))
        rows = jnp.concatenate([rows_high, rows_low], axis=0)
        moment_c = moment_c + jnp.dot(rows, terms, preferred_element_type=F32)
    moment_c = moment_c[:, :count_k] + moment_c[:, count_k:]
    moment_c = moment_c[:rank] + moment_c[rank:]
    moment_c = jnp.concatenate([moment_c, moment_c], axis=0).T
    moment_a = ma_ref[...]

    def result(factor, whole, moment, weight, factor_scale):
        out = (whole - moment) * factor_scale
        return out + factor * weight if weight else out

    a = result(a2_ref[...], model_a, moment_a + turn(moment_a), keep[0], scale[0])
    b = result(b2_ref[...], model_b, moment_b + turn(moment_b), keep[1], scale[1])
    c2_ref[...] = result(c2_ref[...], model_c, moment_c, keep[2], scale[2])
    (pack_first if first else pack_second)(a, b, c2_ref, *outs)


def partials(first, keep, scale, small, tensor, sizes, out_shapes):
    count_i, count_j, count_k = sizes
    width = small[0].shape[-1]
    tall = count_i * count_j
    if first:
        tensor = pltpu.with_memory_space_constraint(tensor, pltpu.HBM)
        out_shapes += ((tall, count_k),)
    return pl.pallas_call(
        functools.partial(round_kernel, first, keep, scale),
        out_shape=tuple(jax.ShapeDtypeStruct(s, F32) for s in out_shapes),
        in_specs=[VMEM] * len(small) + [HBM if first else VMEM],
        out_specs=(VMEM,) * len(out_shapes),
        scratch_shapes=[
            pltpu.VMEM((count_i, width), F32),
            pltpu.VMEM((count_j, width), F32),
            pltpu.VMEM((count_k, width), F32),
            pltpu.VMEM((2 * count_k, width), BF16),
            pltpu.VMEM((count_i, width), F32),
        ]
        + [pltpu.SemaphoreType.DMA((4,))] * first,
        compiler_params=pltpu.CompilerParams(vmem_limit_bytes=24 << 20),
        cost_estimate=pl.CostEstimate(flops=1 << 30, bytes_accessed=4 << 20, transcendentals=0),
        name="partials",
    )(*small, tensor)


def first_kernel(a_hbm, b_hbm, c_hbm, slots_ref, a_ref, b_ref, c_ref, sems):
    own, rank = a_ref.shape
    pairs = ((a_hbm, a_ref), (b_hbm, b_ref), (c_hbm, c_ref))
    copies = [pltpu.make_async_copy(x, y, sems.at[n]) for n, (x, y) in enumerate(pairs)]
    for copy in copies:
        copy.start()
    for copy in copies:
        copy.wait()
    a = a_ref[...]
    rows = jnp.concatenate([b_ref[...], jnp.broadcast_to(c_ref[...], (own, rank))], axis=1)
    slot = jnp.concatenate([rows, jnp.concatenate([a, a], axis=1)], axis=0)
    for n in range(slots_ref.shape[0]):
        slots_ref[n, :, :] = slot


def first_slots(a, b, c, count):
    own, rank = a.shape
    factors = [pltpu.with_memory_space_constraint(x, pltpu.HBM) for x in (a, b, c)]
    return pl.pallas_call(
        first_kernel,
        out_shape=jax.ShapeDtypeStruct((count, 2 * own, 2 * rank), F32),
        in_specs=[HBM] * 3,
        out_specs=VMEM,
        scratch_shapes=[pltpu.VMEM(x.shape, F32) for x in (a, b, c)]
        + [pltpu.SemaphoreType.DMA((3,))],
        compiler_params=pltpu.CompilerParams(vmem_limit_bytes=4 << 20),
        name="first_slots",
    )(*factors)


def second_kernel(all_ref, slots_ref):
    core = lax.axis_index("gz")
    chip = lax.axis_index("gx") * 2
    slots, tall, width = all_ref.shape
    own = tall // 2
    a = jnp.concatenate([all_ref[chip, own:, :], all_ref[chip + 1, own:, :]], axis=0)
    flat = all_ref.reshape(slots * tall, width)
    c = flat[pl.ds(core * tall, slots // 2, stride=2 * tall), :]
    slot = jnp.where(lower_half(a.shape), a, c)
    for n in range(slots_ref.shape[0]):
        slots_ref[n, :, :] = slot


def second_slots(received, count):
    _, tall, width = received.shape
    return pl.pallas_call(
        second_kernel,
        out_shape=jax.ShapeDtypeStruct((count, tall, width), F32),
        in_specs=[VMEM],
        out_specs=VMEM,
        compiler_params=pltpu.CompilerParams(vmem_limit_bytes=4 << 20),
        name="second_slots",
    )(received)


def last_kernel(ac_ref, other_ref, bc_ref, a_ref, b_ref, c_ref, sum_a_ref, sum_b_ref):
    own, rank = a_ref.shape
    sum_a_ref[...] = ac_ref[...] + other_ref[other_ref.shape[0] - ac_ref.shape[0] :, :]
    sum_b_ref[...] = jnp.sum(bc_ref[...], axis=0)
    mine = pl.ds(lax.axis_index("gz") * own, own)
    a_ref[...] = sum_a_ref[mine, :][:, :rank]
    b_ref[...] = sum_b_ref[mine, :][:, :rank]
    c_ref[...] = sum_b_ref[:1, :][:, rank:]


def last_sums(ac, other, bc, own, rank):
    return pl.pallas_call(
        last_kernel,
        out_shape=tuple(jax.ShapeDtypeStruct((n, rank), F32) for n in (own, own, 1)),
        scratch_shapes=[pltpu.VMEM(ac.shape, F32)] * 2,
        compiler_params=pltpu.CompilerParams(vmem_limit_bytes=4 << 20),
        name="last_sums",
    )(ac, other, bc)


def shift(x, axis, stride, count, by):
    pairs = []
    for n in range(lax.axis_size(axis)):
        place = n // stride % count
        pairs.append((n, n + ((place + by) % count - place) * stride))
    return lax.ppermute(x, axis, pairs)


def ring8(x):
    three = x + shift(x, "gx", 1, 8, 1) + shift(x, "gx", 1, 8, -1)
    return three + shift(three, "gx", 1, 8, 4) + shift(x, "gx", 1, 8, 2) + shift(x, "gx", 1, 8, -2)


def ring4(x, stride):
    ones = shift(x, "gy", stride, 4, 1) + shift(x, "gy", stride, 4, -1)
    return (x + ones) + shift(x, "gy", stride, 4, 2)


def swap(x):
    return lax.ppermute(x, "gz", [(0, 1), (1, 0)])


def shards(tensor, factor_a, factor_b, factor_c):
    count_x, count_y, count_z = (lax.axis_size(n) for n in ("gx", "gy", "gz"))
    count_i, count_j, count_k = tensor.shape
    whole = (
        float(count_j * count_y * count_k * count_z),
        float(count_i * count_x * count_k * count_z),
        float(count_i * count_x * count_j * count_y),
    )
    copies = (count_y * count_z, count_x * count_z, count_x * count_y)
    own, rank = factor_a.shape
    wide = 2 * rank

    slots = first_slots(factor_a, factor_b, factor_c, count_x * count_z)
    along_x = lax.all_to_all(slots, ("gx", "gz"), 0, 0, tiled=True)
    along_y = lax.all_to_all(second_slots(along_x, count_y), "gy", 0, 0, tiled=True)

    keep = tuple(1.0 / n for n in copies)
    scale = tuple(-STEP_SIZE / n for n in whole)
    sizes = tensor.shape
    tensor = tensor.reshape(count_i * count_j, count_k)
    shapes = ((count_i, wide), (count_k, wide))
    a, cb, tensor = partials(True, keep, scale, (along_y, along_x), tensor, sizes, shapes)
    a = a + swap(a)
    cb = ring8(cb)
    ca = ring4(ring4(jnp.where(lower_half(cb.shape), cb, a), 1), 4)
    b = cb[:count_j]
    b = b + swap(b)

    scale = tuple(1.0 / n for n in whole)
    shapes = ((count_y, 2 * own, wide), (count_j, wide))
    slots_ac, b = partials(False, (0.0,) * 3, scale, (ca, b), tensor, sizes, shapes)
    ac = jnp.sum(lax.all_to_all(slots_ac, "gy", 0, 0, tiled=True), axis=0)
    others = swap(jnp.concatenate([b, ac], axis=0))
    b = b + others[:count_j]
    slots_b = b.reshape(count_x, 2 * own, wide)
    slots_bc = jnp.where(lower_half(slots_b.shape), slots_b, ac[:, None])
    bc = lax.all_to_all(slots_bc, "gx", 0, 0, tiled=True)
    return last_sums(ac, others, bc, own, rank)


def solution(mesh):
    factors = (
        P(("gx", "gy", "gz"), None),
        P(("gy", "gx", "gz"), None),
        P(("gz", "gx", "gy"), None),
    )
    return jax.shard_map(
        shards,
        mesh=mesh,
        in_specs=(P("gx", "gy", "gz"), *factors),
        out_specs=factors,
        check_vma=False,
    )
```
